32 devices in a mesh: dp: 4 (over z), expert: 8 (over y, x, core).
Axes of the slice: x: 2, y: 2, z: 4, core: 2. Of those that a mesh axis runs over, the one named last changes fastest.
Arguments:
- tokens: bfloat16 [8, 512, 1024], P('expert', 'dp'), may hold values from -6 to 6
- qkv_weight: bfloat16 [1024, 3072], P(('dp', 'expert')), may hold values from -0.1875 to 0.1875
- proj_weight: bfloat16 [1024, 1024], P(('dp', 'expert')), may hold values from -0.75 to 0.75
- router_weight: bfloat16 [1024, 8], P(('dp', 'expert')), may hold values from -0.09375 to 0.09375
- norm_gains: bfloat16 [2, 1024], P(None, ('dp', 'expert')), may hold values from 0.5 to 1.5
- biases: bfloat16 [5, 1024], P(None, ('dp', 'expert')), may hold values from -1.1953125 to 1.1953125
- up_weight: bfloat16 [8, 1024, 4096], P('expert', None, 'dp'), may hold values from -0.1875 to 0.1875
- up_bias: bfloat16 [8, 4096], P('expert', 'dp'), may hold values from -1.1953125 to 1.1953125
- down_weight: bfloat16 [8, 4096, 1024], P('expert', 'dp'), may hold values from -0.75 to 0.75
- down_bias: bfloat16 [8, 1024], P('expert', 'dp'), may hold values from -6 to 6
- routes: int32 [8, 512, 1], P('expert', 'dp'), may hold values from 0 to 7
- slot_order: int32 [8, 4, 128], P('expert', 'dp'), may hold values from 0 to 127, each once within a row
- segments: int32 [8, 512], P('expert'), may hold values from 0 to 6, never falling along the last dimension, each value on 1 to 256 neighbouring positions
- parents: int32 [8, 7], P('expert'), may hold values from 0 to 5, as said below
- cotangent: bfloat16 [8, 512, 1024], P('expert', 'dp'), may hold values from -6 to 6
Outputs:
- outputs: bfloat16 [8, 512, 1024], P('expert', 'dp')
- grad_tokens: float32 [8, 512, 1024], P('expert', 'dp')
- grad_qkv: float32 [1024, 3072], P(('dp', 'expert'))
- grad_proj: float32 [1024, 1024], P(('dp', 'expert'))
- grad_router: float32 [1024, 8], P(('dp', 'expert'))
- grad_gains: float32 [2, 1024], P(None, ('dp', 'expert'))
- grad_biases: float32 [5, 1024], P(None, ('dp', 'expert'))
- grad_up: float32 [8, 1024, 4096], P('expert', None, 'dp')
- grad_up_bias: float32 [8, 4096], P('expert', 'dp')
- grad_down: float32 [8, 4096, 1024], P('expert', 'dp')
- grad_down_bias: float32 [8, 1024], P('expert', 'dp')
The draws below stay inside these ranges and needn't reach their ends.
Inputs may be any that keep to these rules, and one draw needn't show every extreme that they name: Along each tree the segment number never falls, every one of the 7 segments has a token, and the longest has 256. parents[t, 0] = 0, parents[t, s] < s for every other s, and the last segment's parent is segment 7 - 2. `routes`: every expert is the route of some token. `slot_order`: each device's 128 tokens hold every priority once.
All inputs are finite; a program needn't handle non-finite values.
Results may differ from the reference program's by a relative error of at most 0.014.
Values may be sent and summed in bfloat16 or wider, within the bound.
No kernel may reach another device: no remote copies, remote signals or barrier semaphores. Data moves between devices by JAX's collectives and lax.ppermute only.
A program may use at most 192 MiB of HBM per device.

```python
import math
import jax
import jax.numpy as jnp
import numpy as np
from jax import lax

D = 1024
H = 16
HD = 64
FF = 4096
TOK_DEV = 128
NSEG = 7
EXPERTS = 8
TREES = 8
TREE = 512
MOST = 256
CAP = 18
N_DP = 4


def draw_parents(key, part):
    labels = jnp.arange(NSEG, dtype=jnp.int32)
    limits = jnp.maximum(labels, 1)
    drawn = jax.random.randint(key, (TREES, NSEG), 0, limits, dtype=jnp.int32)
    last = (labels == NSEG - 1)[None, :]
    return jnp.where(last, jnp.int32(NSEG - 2), drawn).astype(jnp.int32)


def levels(own_key, extent, split, least, high):
    loudness = 1.0
    for dim, parts in split:
        draws = jax.random.uniform(jax.random.fold_in(jax.random.fold_in(own_key, 6), dim), (parts,), jnp.float32, least / len(split), high / len(split))
        loudness = loudness * jnp.repeat(jnp.exp(draws), extent[dim] // parts).reshape((-1,) + (1,) * (len(extent) - 1 - dim))
    return loudness


def distinct(key, rows, count, top, lift):
    order = jax.random.permutation(jax.random.fold_in(key, 1), count)
    pull = order
    for power in range(3):
        pull = pull * pull // count
    pull = pull * lift // count
    tickets = jax.random.randint(jax.random.fold_in(key, 2), (rows, count), 0, 4096) + pull
    fixed_rows = jax.random.permutation(jax.random.fold_in(key, 3), rows)[jnp.arange(count) % rows]
    tickets = jnp.where(jnp.arange(rows)[:, None] == fixed_rows[None, :], 1 << 14, tickets)
    priority = tickets * count + jnp.arange(count)
    return lax.top_k(priority.astype(jnp.int32), top)[1].astype(jnp.int32)


def length_profile(number_of, total, most, skew):
    loads = [(1 << 20) // math.isqrt(grade ** skew) + 1 for grade in range(2, number_of + 1)]
    surplus, given = total - most - (number_of - 1), [1] * (number_of - 1)
    while surplus > 0:
        movable = [i for i in range(number_of - 1) if given[i] < most]
        whole, budget = sum([loads[i] for i in movable]), surplus
        for i in movable:
            extra = min(most - given[i], max(1, budget * loads[i] // whole), surplus)
            given[i] = given[i] + extra
            surplus = surplus - extra
    return np.array([most] + given)


def uneven(own_key, amount, total, most, slope):
    if amount == 2:
        one = jax.random.randint(own_key, (), max(1, total - most), min(most, total - 1) + 1)
        return jnp.stack([one, total - one])
    tallies = jnp.asarray(length_profile(amount, total, most, slope), jnp.int32)
    pairs = (amount - 1) // 2
    donor, sink = tallies[1:1 + 2 * pairs:2], tallies[2:2 + 2 * pairs:2]
    room = jnp.minimum(donor - 1, most - sink)
    moved = jax.random.randint(jax.random.fold_in(own_key, 1), (pairs,), 0, 1 << 20) % (room + 1)
    tallies = tallies.at[1:1 + 2 * pairs:2].set(donor - moved).at[2:2 + 2 * pairs:2].set(sink + moved)
    return tallies[jax.random.permutation(jax.random.fold_in(own_key, 2), amount)]


def gaussian(own_key, dims, scale, most, shards=(), held_as=jnp.bfloat16):
    factor_of = levels(own_key, dims, shards, -0.22, 0.18) if shards else 1.0
    values = jax.random.normal(own_key, dims, jnp.float32) * scale * factor_of
    return jnp.minimum(jnp.maximum(values, -most), most).astype(held_as)


def setup_inputs(seed: int = 0) -> dict:
    seeds = jax.random.split(jax.random.key(seed), 16)
    return {
        "tokens": gaussian(seeds[0], (TREES, TREE, D), 1.0, 6.0, ((0, 8), (1, 4))),
        "qkv_weight": gaussian(seeds[1], (D, 3 * D), D ** -0.5, 0.1875, ((0, 32),)),
        "proj_weight": gaussian(seeds[2], (D, D), (D // 16) ** -0.5, 0.75, ((0, 32),)),
        "router_weight": gaussian(seeds[3], (D, EXPERTS), (4 * D) ** -0.5, 0.09375, ((0, 32),)),
        "norm_gains": jnp.clip(1.0 + 0.1 * jax.random.normal(seeds[4], (2, D), jnp.float32), 0.5, 1.5).astype(jnp.bfloat16),
        "biases": gaussian(seeds[5], (5, D), 0.2, 1.1953125, ((1, 32),)),
        "up_weight": gaussian(seeds[6], (EXPERTS, D, FF), D ** -0.5, 0.1875, ((0, 8), (2, 4))),
        "up_bias": gaussian(seeds[7], (EXPERTS, FF), 0.2, 1.1953125, ((0, 8), (1, 4))),
        "down_weight": gaussian(seeds[8], (EXPERTS, FF, D), (max(1, FF // (EXPERTS * EXPERTS))) ** -0.5, 0.75, ((0, 8), (1, 4))),
        "down_bias": gaussian(seeds[9], (EXPERTS, D), 1.0, 6.0, ((0, 8), (1, 4))),
        "routes": distinct(seeds[10], TREES * TREE, EXPERTS, 1, 1024).reshape((TREES, TREE, 1)),
        "slot_order": jax.vmap(lambda own: jax.random.permutation(own, TOK_DEV))(jax.random.split(seeds[11], TREES * N_DP)).reshape((TREES, N_DP, TOK_DEV)).astype(jnp.int32),
        "segments": jax.vmap(lambda own: jnp.searchsorted(jnp.cumsum(uneven(own, NSEG, TREE, MOST, 0)), jnp.arange(TREE), side="right"))(jax.random.split(seeds[12], TREES)).reshape((TREES, TREE)).astype(jnp.int32),
        "parents": draw_parents(jax.random.fold_in(seeds[15], 71), 0),
        "cotangent": gaussian(seeds[14], (TREES, TREE, D), 1.0, 6.0, ((0, 8), (1, 4))),
    }


@jax.custom_vjp
def low(v):
    return lax.optimization_barrier(v.astype(jnp.bfloat16)).astype(jnp.float32)

@jax.custom_vjp
def low_back(v):
    return v

def low_keep(v):
    return (low(v), None)

def low_pass(kept, grad):
    return (grad,)

def back_keep(v):
    return (v, None)

def back_low(kept, grad):
    return (low(grad),)
low.defvjp(low_keep, low_pass)
low_back.defvjp(back_keep, back_low)
EPS = 1e-05
NEG = -1e+30
HIGH = lax.Precision.HIGHEST

def layer_norm(values, gain, shift):
    mean = lax.optimization_barrier(jnp.mean(values, axis=-1, keepdims=True))
    centred = values - mean
    spread = lax.optimization_barrier(jnp.mean(centred * centred, axis=-1, keepdims=True))
    return centred * lax.rsqrt(spread + EPS) * gain + shift

def ancestry(parents):
    labels = jnp.arange(NSEG, dtype=jnp.int32)
    direct = (labels[None, :] == parents[:, None]).astype(jnp.float32)
    reach = jnp.minimum(direct + jnp.eye(NSEG, dtype=jnp.float32), 1.0)
    for step in range(3):
        reach = jnp.minimum(jnp.dot(reach, reach, precision=HIGH), 1.0)
    return reach

def tree_attention(packed, seg_ids, parents):
    reach = ancestry(parents)
    key_hot = (seg_ids[:, None] == jnp.arange(NSEG, dtype=jnp.int32)[None, :]).astype(jnp.float32)
    row_reach = jnp.dot(key_hot, reach, precision=HIGH)
    keys = packed[:, D:2 * D].reshape(TREE, H, HD)
    values = packed[:, 2 * D:].reshape(TREE, H, HD)
    positions = jnp.arange(TREE, dtype=jnp.int32)

    def one_block(first):
        queries = lax.dynamic_slice_in_dim(packed[:, :D], first, TOK_DEV, 0).reshape(TOK_DEV, H, HD)
        reach_rows = lax.dynamic_slice_in_dim(row_reach, first, TOK_DEV, 0)
        query_pos = first + jnp.arange(TOK_DEV, dtype=jnp.int32)
        allowed = (jnp.dot(reach_rows, key_hot.T, precision=HIGH) > 0.5) & (positions[None, :] <= query_pos[:, None])
        scores = low_back(jnp.einsum('qhd,khd->hqk', queries, keys, precision=HIGH) * HD ** (-0.5))
        scores = jnp.where(allowed[None], scores, NEG)
        probs = low(jax.nn.softmax(scores, axis=-1))
        return jnp.einsum('hqk,khd->qhd', probs, values, precision=HIGH).reshape(TOK_DEV, D)
    firsts = jnp.arange(N_DP, dtype=jnp.int32) * TOK_DEV
    return lax.map(jax.checkpoint(one_block), firsts).reshape(TREE, D)

def slot_tables(route_ids, order):
    labels = jnp.arange(EXPERTS, dtype=jnp.int32)
    expert_hot = route_ids[:, None] == labels[None, :]
    same = route_ids[:, None] == route_ids[None, :]
    before = order[None, :] < order[:, None]
    rank = lax.optimization_barrier(jnp.sum((same & before).astype(jnp.int32), axis=1))
    slot_hot = rank[:, None] == jnp.arange(CAP, dtype=jnp.int32)[None, :]
    table = expert_hot[:, :, None] & slot_hot[:, None, :]
    return (expert_hot.astype(jnp.float32), table.astype(jnp.float32))

def expert_ffn(item):
    rows, up_e, up_shift, down_e, down_shift = item
    pre = low_back(jnp.dot(rows, up_e, precision=HIGH))
    act = low(jax.nn.gelu(pre + up_shift, approximate=True))
    return low_back(low(jnp.dot(act, down_e, precision=HIGH) + down_shift))

def tree_item(item):
    return tree_attention(item[0], item[1], item[2])

def forward(tokens, qkv_weight, proj_weight, router_weight, norm_gains, biases, up_weight, up_bias, down_weight, down_bias, segments, parents, tables, expert_hot):
    blocks = TREES * N_DP
    normed = low(layer_norm(tokens, norm_gains[0], biases[0]))
    shift = jnp.concatenate([biases[1], jnp.zeros((D,), jnp.float32), biases[2]])
    packed = low_back(low(jnp.einsum('tsd,de->tse', normed, qkv_weight, precision=HIGH) + shift))
    attended = lax.map(jax.checkpoint(tree_item), (packed, segments, parents))
    attended = low_back(low(attended))
    mixed = tokens + low_back(jnp.einsum('tsc,cd->tsd', attended, proj_weight, precision=HIGH)) + biases[3]
    normed2 = low(layer_norm(mixed, norm_gains[1], biases[4]))
    flat = normed2.reshape(blocks, TOK_DEV, D)
    probs = jax.nn.softmax(jnp.einsum('btd,de->bte', flat, router_weight, precision=HIGH), axis=-1)
    gate = lax.optimization_barrier(jnp.sum(probs * expert_hot, axis=-1))
    sent = low_back(jnp.einsum('btec,btd->becd', tables, flat, precision=HIGH))
    by_expert = jnp.transpose(sent, (1, 0, 2, 3)).reshape(EXPERTS, blocks * CAP, D)
    results = lax.map(jax.checkpoint(expert_ffn), (by_expert, up_weight, up_bias, down_weight, down_bias))
    back = jnp.transpose(results.reshape(EXPERTS, blocks, CAP, D), (1, 0, 2, 3))
    combined = jnp.einsum('btec,becd->btd', tables, back, precision=HIGH)
    output = mixed.reshape(blocks, TOK_DEV, D) + gate[:, :, None] * combined
    return low(output).reshape(TREES, TREE, D)

def reference(tokens, qkv_weight, proj_weight, router_weight, norm_gains, biases, up_weight, up_bias, down_weight, down_bias, routes, slot_order, segments, parents, cotangent):
    blocks = TREES * N_DP
    route_ids = routes.reshape(blocks, TOK_DEV)
    orders = slot_order.reshape(blocks, TOK_DEV)
    expert_hot, tables = lax.map(lambda item: slot_tables(item[0], item[1]), (route_ids, orders))
    floats = (tokens, qkv_weight, proj_weight, router_weight, norm_gains, biases, up_weight, up_bias, down_weight, down_bias)
    floats = tuple((value.astype(jnp.float32) for value in floats))

    def run(*values):
        return forward(*values, segments, parents, tables, expert_hot)
    output, pullback = jax.vjp(run, *floats)
    grads = pullback(cotangent.astype(jnp.float32))
    return (output.astype(jnp.bfloat16), grads[0], grads[1], grads[2], grads[3], grads[4], grads[5], grads[6], grads[7], grads[8], grads[9])
```

```python
import jax
import jax.numpy as jnp
from jax import lax
from jax.sharding import PartitionSpec as P

H = 16
NSEG = 7
EPS = 1e-05
NEG = -1e30
BF = jnp.bfloat16
F32 = jnp.float32


def mm(a, b, ca=1, cb=0):
    return lax.dot_general(a, b, (((ca,), (cb,)), ((), ())), preferred_element_type=F32)


def ahead(x, step):
    n = lax.axis_size("dp")
    return lax.ppermute(x, "dp", [(i, (i + step) % n) for i in range(n)])


def flip(x, bits):
    n = lax.axis_size("expert")
    return lax.ppermute(x, "expert", [(i, i ^ bits) for i in range(n)])


def gather_experts(x):
    n = lax.axis_size("expert")
    mine = [x] + [flip(x, 2 * k) for k in range(1, n // 2)]
    out = []
    for block in mine:
        out += [block, flip(block, 1)]
    return out


def in_order(blocks, me):
    n = len(blocks)
    stacked = jnp.stack(blocks)
    return jnp.take(stacked, me ^ jnp.arange(n), axis=0)


def rotated(blocks, me):
    n = len(blocks)
    back = jnp.stack([blocks[0]] + blocks[:0:-1])
    twice = jnp.concatenate([back, back])
    return lax.dynamic_slice_in_dim(twice, (n - me) % n, n, 0)


def pick(x, index):
    return lax.dynamic_index_in_dim(x, index, 0, keepdims=False)


def normalise(values):
    mean = jnp.mean(values, axis=-1, keepdims=True)
    centred = values - mean
    scale = lax.rsqrt(jnp.mean(centred * centred, axis=-1, keepdims=True) + EPS)
    return centred * scale, scale


def norm_back(upstream, gain, unit, scale):
    e = upstream * gain
    return scale * (
        e
        - jnp.mean(e, axis=-1, keepdims=True)
        - unit * jnp.mean(e * unit, axis=-1, keepdims=True)
    )


def ancestry(parents):
    labels = jnp.arange(NSEG, dtype=jnp.int32)
    direct = (labels[None, :] == parents[:, None]).astype(F32)
    reach = jnp.minimum(direct + jnp.eye(NSEG, dtype=F32), 1.0)
    for _ in range(3):
        reach = jnp.minimum(mm(reach, reach), 1.0)
    return reach


def slot_table(route_ids, order, experts, capacity):
    labels = jnp.arange(experts, dtype=jnp.int32)
    expert_hot = route_ids[:, None] == labels[None, :]
    same = route_ids[:, None] == route_ids[None, :]
    before = order[None, :] < order[:, None]
    rank = jnp.sum((same & before).astype(jnp.int32), axis=1)
    slot_hot = rank[:, None] == jnp.arange(capacity, dtype=jnp.int32)[None, :]
    table = expert_hot[:, :, None] & slot_hot[:, None, :]
    return expert_hot.astype(F32), table.reshape(table.shape[0], -1).astype(BF)


def to_experts(x, n_ex):
    blocks = x.reshape(n_ex, -1, x.shape[-1])
    return lax.all_to_all(blocks, "expert", split_axis=0, concat_axis=0, tiled=True).reshape(x.shape)


def owned_sum(payload, me_d, me_e):
    n_ex = payload.shape[1]
    low = payload.astype(BF)
    near = jnp.stack([pick_axis1(low, me_e ^ (2 * q + 1)) for q in range(n_ex // 2)])
    came = flip(near, 1)
    own = [
        pick_axis1(payload, me_e ^ (2 * q)) + came[q].astype(F32) for q in range(n_ex // 2)
    ]
    total = own[0]
    for q in range(1, n_ex // 2):
        total = total + flip(own[q].astype(BF), 2 * q).astype(F32)
    return total


def pick_axis1(x, index):
    return lax.dynamic_index_in_dim(x, index, 1, keepdims=False)


def shards(
    tokens,
    qkv_weight,
    proj_weight,
    router_weight,
    norm_gains,
    biases,
    up_weight,
    up_bias,
    down_weight,
    down_bias,
    routes,
    slot_order,
    segments,
    parents,
    cotangent,
):
    n_dp, n_ex = lax.axis_size("dp"), lax.axis_size("expert")
    me_d, me_e = lax.axis_index("dp"), lax.axis_index("expert")
    rows, width = tokens.shape[1], tokens.shape[2]
    part = width // n_dp
    head_dim = width // H
    heads = part // head_dim
    scale = head_dim ** (-0.5)
    own = qkv_weight.shape[0]
    experts = router_weight.shape[1]
    capacity = (9 * rows + 8 * experts - 1) // (8 * experts)

    by_part = jnp.transpose(qkv_weight.reshape(own, 3, n_dp, part), (2, 0, 1, 3)).reshape(
        n_dp, own, 3 * part
    )
    sliced = [pick(by_part, me_d)]
    for j in range(1, n_dp):
        sliced.append(ahead(pick(by_part, (me_d + j) % n_dp), j))
    line_qkv = rotated(sliced, me_d)
    token_blocks = [tokens[0]] + [ahead(tokens[0], j) for j in range(1, n_dp)]
    small = jnp.concatenate(
        [
            router_weight,
            norm_gains.T,
            biases.T,
            jnp.zeros((own, 128 - experts - 7), BF),
        ],
        axis=1,
    )
    mine = jnp.concatenate([proj_weight, small], axis=1)
    line_proj = rotated([mine] + [ahead(mine, j) for j in range(1, n_dp)], me_d)
    qkv_blocks = gather_experts(line_qkv)
    proj_blocks = gather_experts(line_proj)
    qkv_own = jnp.swapaxes(in_order(qkv_blocks, me_e), 0, 1).reshape(width, 3 * part)
    proj_all = jnp.swapaxes(in_order(proj_blocks, me_e), 0, 1).reshape(width, width + 128)
    proj_full = proj_all[:, :width]
    router_full = proj_all[:, width : width + experts]
    vectors = proj_all[:, width + experts : width + experts + 7].T.astype(F32)
    gain1, gain2 = vectors[0], vectors[1]
    shift1, shift_q, shift_v, shift_proj, shift2 = (vectors[2 + i] for i in range(5))

    expert_hot, table = slot_table(routes[0, :, 0], slot_order[0, 0], experts, capacity)
    upstream = cotangent[0].astype(F32)
    grads_out = mm(table, cotangent[0], 0, 0).astype(BF)
    grads_in = to_experts(grads_out, n_ex)
    grads_all = jnp.concatenate([grads_in] + [ahead(grads_in, j) for j in range(1, n_dp)])

    x_tree = jnp.concatenate(token_blocks).astype(F32)
    unit1, rstd1 = normalise(x_tree)
    normed1 = (unit1 * gain1 + shift1).astype(BF)
    own_q = lax.dynamic_slice_in_dim(shift_q, me_d * part, part)
    own_v = lax.dynamic_slice_in_dim(shift_v, me_d * part, part)
    shift = jnp.concatenate([own_q, jnp.zeros((part,), F32), own_v])
    packed = (mm(normed1, qkv_own) + shift).astype(BF)
    length = n_dp * rows
    seg_blocks = segments[0].reshape(n_dp, rows)
    order_d = [(me_d - j) % n_dp for j in range(n_dp)]
    seg = jnp.concatenate([pick(seg_blocks, d) for d in order_d])
    pos = jnp.concatenate([d * rows + jnp.arange(rows, dtype=jnp.int32) for d in order_d])
    reach = ancestry(parents[0])
    hot = (seg[:, None] == jnp.arange(NSEG, dtype=jnp.int32)[None, :]).astype(F32)
    allowed = (mm(mm(hot, reach), hot, 1, 1) > 0.5) & (pos[None, :] <= pos[:, None])
    q = packed[:, :part].reshape(length, heads, head_dim)
    k = packed[:, part : 2 * part].reshape(length, heads, head_dim)
    v = packed[:, 2 * part :].reshape(length, heads, head_dim)
    scores = jnp.einsum("qhd,khd->hqk", q, k, preferred_element_type=F32) * scale
    scores = jnp.where(allowed[None], scores, NEG)
    top = jnp.max(scores, axis=-1, keepdims=True)
    total = jnp.sum(jnp.exp(scores - top), axis=-1, keepdims=True)
    log_total = top + jnp.log(total)
    probs = jnp.exp(scores - log_total)
    probs_low = probs.astype(BF)
    attended = jnp.einsum("hqk,khd->qhd", probs_low, v, preferred_element_type=F32)
    attended = attended.astype(BF).reshape(n_dp, rows, part)
    att = [attended[0]] + [ahead(attended[j], -j) for j in range(1, n_dp)]
    att_full = jnp.concatenate(att, axis=1)
    proj_rel = jnp.concatenate(
        [
            lax.dynamic_slice_in_dim(proj_full, ((me_d + j) % n_dp) * part, part, 0)
            for j in range(n_dp)
        ]
    )
    inputs = tokens[0].astype(F32)
    mixed = inputs + mm(att_full, proj_rel) + shift_proj
    unit2, rstd2 = normalise(mixed)
    normed2 = (unit2 * gain2 + shift2).astype(BF)
    logits = mm(normed2, router_full)
    p = jax.nn.softmax(logits, axis=-1)
    gate = jnp.sum(p * expert_hot, axis=-1)
    sent = mm(table, normed2, 0, 0).astype(BF)

    slots_in = to_experts(sent, n_ex)
    slots = jnp.concatenate([slots_in] + [ahead(slots_in, j) for j in range(1, n_dp)])
    slot_p = jax.nn.softmax(mm(slots, router_full), axis=-1)
    slot_gate = lax.dynamic_slice_in_dim(slot_p, me_e, 1, 1)
    d_rows = (slot_gate * grads_all.astype(F32)).astype(BF)
    up, down = up_weight[0], down_weight[0]
    pre = mm(slots, up) + up_bias[0].astype(F32)
    act, act_back = jax.vjp(lambda u: jax.nn.gelu(u, approximate=True), pre)
    act_low = act.astype(BF)
    result = mm(act_low, down)
    spread = lax.dynamic_update_slice_in_dim(
        jnp.zeros((width,), F32), down_bias[0].astype(F32), me_d * part, 0
    )
    result = (result + spread).astype(BF).reshape(n_dp, -1, width)
    d_pre = act_back(mm(d_rows, down, 1, 1))[0]
    d_pre_low = d_pre.astype(BF)
    d_slots = mm(d_pre_low, up, 1, 1).astype(BF).reshape(n_dp, -1, width)
    both = jnp.concatenate([result, d_slots], axis=1)
    line = both[0].astype(F32)
    for j in range(1, n_dp):
        line = line + ahead(both[j], -j).astype(F32)
    line = line.astype(BF)
    slot_rows = n_ex * capacity
    back = jnp.concatenate(
        [line[:slot_rows].reshape(n_ex, capacity, width), line[slot_rows:].reshape(n_ex, capacity, width)], axis=1
    )
    back = lax.all_to_all(back, "expert", split_axis=0, concat_axis=0, tiled=True)
    returned = back[:, :capacity].reshape(slot_rows, width)
    d_sent = back[:, capacity:].reshape(slot_rows, width)
    grad_up = mm(slots, d_pre_low, 0, 0)
    grad_down = mm(act_low, d_rows, 0, 0)
    grad_up_bias = jnp.sum(d_pre, axis=0)
    all_down_bias = jnp.sum(d_rows.astype(F32), axis=0)
    grad_down_bias = lax.dynamic_slice_in_dim(all_down_bias, me_d * part, part)

    combined = mm(table, returned)
    outputs = (mixed + gate[:, None] * combined).astype(BF)
    d_gate = jnp.sum(upstream * combined, axis=-1)
    d_logits = p * (d_gate[:, None] * expert_hot - (d_gate * gate)[:, None])
    grad_router = mm(normed2, d_logits.astype(BF), 0, 0)
    d_normed2 = mm(table, d_sent) + mm(d_logits.astype(BF), router_full, 1, 1)
    grad_gain2 = jnp.sum(d_normed2 * unit2, axis=0)
    grad_shift2 = jnp.sum(d_normed2, axis=0)
    d_mixed = upstream + norm_back(d_normed2, gain2, unit2, rstd2)
    grad_shift_proj = jnp.sum(d_mixed, axis=0)
    d_mixed_low = d_mixed.astype(BF)
    grad_proj = mm(att_full, d_mixed_low, 0, 0)
    d_att_own = mm(d_mixed_low, proj_rel, 1, 1).astype(BF)
    d_att = [d_att_own[:, :part]] + [
        ahead(d_att_own[:, j * part : (j + 1) * part], j) for j in range(1, n_dp)
    ]
    d_heads = jnp.concatenate(d_att).reshape(length, heads, head_dim)
    proj_pay = owned_sum(grad_proj.reshape(n_dp, n_ex, own, width), me_d, me_e)
    proj_low = proj_pay.astype(BF)
    owned_proj = proj_pay[0]
    for j in range(1, n_dp):
        owned_proj = owned_proj + ahead(proj_low[j], j).astype(F32)

    d_value = jnp.einsum("hqk,qhd->khd", probs_low, d_heads, preferred_element_type=F32)
    d_probs = jnp.einsum("qhd,khd->hqk", d_heads, v, preferred_element_type=F32)
    delta = jnp.sum(d_probs * probs, axis=-1, keepdims=True)
    d_scores = (probs * (d_probs - delta)).astype(BF)
    d_query = jnp.einsum("hqk,khd->qhd", d_scores, k, preferred_element_type=F32) * scale
    d_key = jnp.einsum("hqk,qhd->khd", d_scores, q, preferred_element_type=F32) * scale
    d_packed = jnp.concatenate(
        [t.reshape(length, part) for t in (d_query, d_key, d_value)], axis=1
    ).astype(BF)
    d_normed = mm(d_packed, qkv_own, 1, 1)
    d_blocks = d_normed.astype(BF).reshape(n_dp, rows, width)
    d_own = d_normed[:rows]
    for j in range(1, n_dp):
        d_own = d_own + ahead(d_blocks[j], -j).astype(F32)
    grad_qkv = mm(normed1, d_packed, 0, 0)
    grad_gain1 = jnp.sum(d_normed * unit1, axis=0)
    grad_shift1 = jnp.sum(d_normed, axis=0)
    sums = jnp.sum(d_packed.astype(F32), axis=0)
    place = lambda s: lax.dynamic_update_slice_in_dim(jnp.zeros((width,), F32), s, me_d * part, 0)
    extra = jnp.stack(
        [
            grad_gain1,
            grad_gain2,
            grad_shift1,
            place(sums[:part]),
            place(sums[2 * part :]),
            grad_shift_proj,
            grad_shift2,
        ],
        axis=1,
    )
    extra = jnp.concatenate([grad_router, extra, jnp.zeros((width, 128 - experts - 7), F32)], axis=1)
    pay = jnp.concatenate([grad_qkv, extra], axis=1).reshape(n_dp, n_ex, own, 3 * part + 128)
    pay = owned_sum(pay, me_d, me_e)
    low = pay.astype(BF)
    got = [pick(pay, me_d)]
    for j in range(1, n_dp):
        got.append(ahead(pick(low, (me_d + j) % n_dp), j).astype(F32))
    owned_small = got[0][:, 3 * part :]
    for j in range(1, n_dp):
        owned_small = owned_small + got[j][:, 3 * part :]
    cols = rotated([g[:, : 3 * part] for g in got], me_d)
    owned_qkv = jnp.transpose(cols.reshape(n_dp, own, 3, part), (1, 2, 0, 3)).reshape(own, 3 * width)
    owned_router = owned_small[:, :experts]
    owned_vec = owned_small[:, experts : experts + 7].T
    grad_tokens = d_mixed + norm_back(d_own, gain1, unit1[:rows], rstd1[:rows])
    return (
        outputs[None],
        grad_tokens[None],
        owned_qkv,
        owned_proj,
        owned_router,
        owned_vec[:2],
        owned_vec[2:],
        grad_up[None],
        grad_up_bias[None],
        grad_down[None],
        grad_down_bias[None],
    )


def solution(mesh):
    line = P(("dp", "expert"), None)
    across = P(None, ("dp", "expert"))
    act = P("expert", "dp", None)
    return jax.shard_map(
        shards,
        mesh=mesh,
        in_specs=(
            act,
            line,
            line,
            line,
            across,
            across,
            P("expert", None, "dp"),
            P("expert", "dp"),
            act,
            P("expert", "dp"),
            act,
            act,
            P("expert", None),
            P("expert", None),
            act,
        ),
        out_specs=(
            act,
            act,
            line,
            line,
            line,
            across,
            across,
            P("expert", None, "dp"),
            P("expert", "dp"),
            act,
            P("expert", "dp"),
        ),
        check_vma=False,
    )
```

```python
import functools

import jax
import jax.numpy as jnp
from jax import lax
from jax.experimental import pallas as pl
from jax.experimental.pallas import tpu as pltpu
from jax.sharding import PartitionSpec as P

H = 16
NSEG = 7
EPS = 1e-05
NEG = -1e30
BF = jnp.bfloat16
F32 = jnp.float32
I32 = jnp.int32


def mm(a, b, ca=1, cb=0):
    return lax.dot_general(a, b, (((ca,), (cb,)), ((), ())), preferred_element_type=F32)


def call(kernel, outs, me, *args, scratch=(), **static):
    smem = pl.BlockSpec(memory_space=pltpu.SMEM)
    vmem = pl.BlockSpec(memory_space=pltpu.VMEM)
    return pl.pallas_call(
        functools.partial(kernel, **static),
        out_shape=[jax.ShapeDtypeStruct(s, d) for s, d in outs],
        in_specs=[smem] + [vmem] * len(args),
        out_specs=[vmem] * len(outs),
        scratch_shapes=list(scratch),
        name=kernel.__name__,
    )(me, *args)


def ahead(x, step):
    n = lax.axis_size("dp")
    return lax.ppermute(x, "dp", [(i, (i + step) % n) for i in range(n)])


def flip(x, bits):
    n = lax.axis_size("expert")
    return lax.ppermute(x, "expert", [(i, i ^ bits) for i in range(n)])


def swap(x, axis):
    return lax.all_to_all(x, axis, split_axis=0, concat_axis=0, tiled=True)


def along(blocks, sign=1):
    return [blocks[0]] + [ahead(blocks[j], sign * j) for j in range(1, len(blocks))]


def gather_experts(x):
    n = lax.axis_size("expert")
    mine = [x] + [flip(x, 2 * k) for k in range(1, n // 2)]
    out = []
    for block in mine:
        out += [block, flip(block, 1)]
    return out


def normalise(values):
    mean = jnp.mean(values, axis=-1, keepdims=True)
    centred = values - mean
    scale = lax.rsqrt(jnp.mean(centred * centred, axis=-1, keepdims=True) + EPS)
    return centred * scale, scale


def norm_back(upstream, gain, unit, scale):
    e = upstream * gain
    return scale * (
        e - jnp.mean(e, axis=-1, keepdims=True) - unit * jnp.mean(e * unit, axis=-1, keepdims=True)
    )


def lanes(shape, dim):
    return lax.broadcasted_iota(I32, shape, dim)


def softmax_of(logits, experts):
    logits = jnp.where(lanes(logits.shape, 1) < experts, logits, NEG)
    top = jnp.max(logits, axis=-1, keepdims=True)
    weight = jnp.exp(logits - top)
    return weight / jnp.sum(weight, axis=-1, keepdims=True)


def weights_kernel(me, qkv, router, gains, biases, columns, turned, small, *, n_dp):
    own, width = qkv.shape[0], qkv.shape[1] // 3
    part = width // n_dp
    experts = router.shape[1]
    turned[...] = jnp.zeros_like(turned)
    turned[experts : experts + 2, :own] = gains[...].astype(F32)
    turned[experts + 2 : experts + 7, :own] = biases[...].astype(F32)
    small[...] = turned[...].T[:own]
    small[:, :experts] = router[...].astype(F32)
    few = small[...].astype(BF)
    for d in range(n_dp):
        for i in range(3):
            columns[d, :, i * part : (i + 1) * part] = qkv[
                :, i * width + d * part : i * width + (d + 1) * part
            ]
        columns[d, :, 3 * part :] = few


def slots_kernel(
    me, parents, route, order, cotangent, seg, grads, tableT, rank_out, bias, *, pad, capacity, experts
):
    tok = route.shape[0]
    r = jnp.broadcast_to(route[...].astype(F32), (tok, tok))
    rt = r.T
    o = jnp.broadcast_to(order[...].astype(F32), (tok, tok))
    ot = o.T
    same = r == rt
    rank = jnp.sum(jnp.where(same & (o < ot), 1.0, 0.0), axis=1, keepdims=True)
    rank_row = jnp.sum(jnp.where(same & (ot < o), 1.0, 0.0), axis=0, keepdims=True)
    rank_out[...] = rank.astype(I32)
    key = jnp.where(rank_row < capacity, rt[0:1] * pad + rank_row, -1.0).astype(I32)
    table = jnp.where(lanes((experts * pad, tok), 0) == key, 1.0, 0.0).astype(BF)
    tableT[...] = table
    grads[...] = mm(table, cotangent[...]).astype(BF)
    length = seg.shape[1]
    masks = [jnp.int32(1)]
    for s in range(1, NSEG):
        up = jnp.int32(0)
        for a in range(s):
            up = jnp.where(parents[0, s] == a, masks[a], up)
        masks.append(up | (1 << s))
    block = 128
    keys = seg[...]
    for i in range(length // block):
        col = jnp.broadcast_to(seg[:, i * block : (i + 1) * block].astype(F32), (block, block)).T
        col = jnp.broadcast_to(col[:, 0:1], (block, length)).astype(I32)
        mine = jnp.zeros((block, length), I32)
        for s in range(NSEG):
            mine = jnp.where(col == s, masks[s], mine)
        ok = jnp.zeros((block, length), I32)
        for s in range(NSEG):
            ok = jnp.where(keys == s, mine & (1 << s), ok)
        seen = lanes((block, length), 1) <= lanes((block, length), 0) + i * block
        bias[i * block : (i + 1) * block] = jnp.where(seen & (ok > 0), 0.0, NEG)


def pack_kernel(me, rows, out, *, pad, capacity):
    n_out, n_in = out.shape[0], rows.shape[0]
    r, c = lanes((n_out, n_in), 0), lanes((n_out, n_in), 1)
    pick = jnp.zeros((n_out, n_in), jnp.bool_)
    for e in range(n_in // pad):
        inside = (r >= e * capacity) & (r < (e + 1) * capacity)
        pick = pick | (inside & (c - e * pad == r - e * capacity))
    out[...] = mm(jnp.where(pick, 1.0, 0.0).astype(BF), rows[...]).astype(BF)


def assemble_kernel(me, *refs):
    out = refs[-1]
    for k, block in enumerate(refs[:-1]):
        e = me[1] ^ k
        for d in range(block.shape[0]):
            out[d, e] = block[d]


def attend_kernel(me, qkv, bias, *refs, n_dp, head_dim, experts):
    tokens, (normed, unit, packed, probs, attended, vectors) = refs[:n_dp], refs[n_dp:]
    rows, width = tokens[0].shape
    part = width // n_dp
    small = qkv[:, 3 * part :].astype(F32).T
    vectors[...] = small[experts : experts + 8]
    gain, shift = vectors[0:1], vectors[2:3]
    parts = [jnp.zeros((1, part), F32)] * 2
    for d in range(n_dp):
        for i in range(2):
            here = vectors[3 + i : 4 + i, d * part : (d + 1) * part]
            parts[i] = parts[i] + jnp.where(me[0] == d, here, 0.0)
    for j in range(n_dp):
        base = pl.multiple_of(((me[0] + n_dp - j) % n_dp) * rows, rows)
        centred, _ = normalise(tokens[j][...].astype(F32))
        unit[pl.ds(base, rows)] = centred
        normed[pl.ds(base, rows)] = (centred * gain + shift).astype(BF)
    raw = mm(normed[...], qkv[:, : 3 * part])
    packed[:, :part] = (raw[:, :part] + parts[0]).astype(BF)
    packed[:, part : 2 * part] = raw[:, part : 2 * part].astype(BF)
    packed[:, 2 * part :] = (raw[:, 2 * part :] + parts[1]).astype(BF)
    scale = head_dim ** (-0.5)
    length = rows * n_dp
    for h in range(part // head_dim):
        q = packed[:, h * head_dim : (h + 1) * head_dim]
        k = packed[:, part + h * head_dim : part + (h + 1) * head_dim]
        v = packed[:, 2 * part + h * head_dim : 2 * part + (h + 1) * head_dim]
        for i in range(n_dp):
            lo, hi = i * rows, (i + 1) * rows
            s = mm(q[lo:hi], k[:hi], 1, 1) * scale + bias[lo:hi, :hi]
            top = jnp.max(s, axis=-1, keepdims=True)
            p = jnp.exp(s - top)
            p = (p * (1.0 / jnp.sum(p, axis=-1, keepdims=True))).astype(BF)
            probs[h, lo:hi, :hi] = p
            if hi < length:
                probs[h, lo:hi, hi:] = jnp.zeros((rows, length - hi), BF)
            attended[i, :, h * head_dim : (h + 1) * head_dim] = mm(p, v[:hi]).astype(BF)


def mix_kernel(me, tokens, attended, proj, qkv, vectors, tableT, mixed, normed, p, sent, *, experts):
    n_dp, rows, part = attended.shape
    total = tokens[...].astype(F32) + vectors[5:6]
    for d in range(n_dp):
        total = total + mm(attended[d], proj[d * part : (d + 1) * part])
    mixed[...] = total
    unit, _ = normalise(total)
    low = (unit * vectors[1:2] + vectors[6:7]).astype(BF)
    normed[...] = low
    p[...] = softmax_of(mm(low, qkv[:, 3 * part :]), experts)
    sent[...] = mm(tableT[...], low).astype(BF)


def expert_kernel(me, qkv, up, down, up_bias, down_bias, *refs, n_dp, experts, part):
    ins, both = refs[: 2 * n_dp], refs[2 * n_dp : 3 * n_dp]
    act_out, d_pre_out, slots, d_rows, g_up_bias, g_down_bias, acc_r, acc_s = refs[3 * n_dp :]
    f = pl.program_id(0)
    last = pl.num_programs(0) - 1
    each, width = ins[0].shape

    @pl.when(f == 0)
    def _():
        sums = jnp.zeros((1, width), F32)
        for j in range(n_dp):
            rows = ins[j][...]
            slots[j * each : (j + 1) * each] = rows
            p = softmax_of(mm(rows, qkv[:, 3 * part :]), experts)
            gate = jnp.sum(jnp.where(lanes(p.shape, 1) == me[1], p, 0.0), axis=-1, keepdims=True)
            d = (gate * ins[n_dp + j][...].astype(F32)).astype(BF)
            d_rows[j * each : (j + 1) * each] = d
            sums = sums + jnp.sum(d.astype(F32), axis=0, keepdims=True)
        own = jnp.zeros((1, part), F32)
        for d in range(n_dp):
            own = own + jnp.where(me[0] == d, sums[:, d * part : (d + 1) * part], 0.0)
        g_down_bias[...] = own
        acc_r[...] = jnp.zeros_like(acc_r)
        acc_s[...] = jnp.zeros_like(acc_s)
        for d in range(n_dp):
            acc_r[:, d * part : (d + 1) * part] = jnp.broadcast_to(
                jnp.where(me[0] == d, down_bias[...].astype(F32), 0.0), (n_dp * each, part)
            )

    u = mm(slots[...], up[...]) + up_bias[...].astype(F32)
    c, a = 0.7978845608028654, 0.044715
    t = jnp.tanh(c * (u + a * (u * u * u)))
    act = (0.5 * u * (1.0 + t)).astype(BF)
    slope = 0.5 * (1.0 + t) + 0.5 * u * (1.0 - t * t) * (c * (1.0 + 3.0 * a * (u * u)))
    d_pre = mm(d_rows[...], down[...], 1, 1) * slope
    g_up_bias[...] = jnp.sum(d_pre, axis=0, keepdims=True)
    low = d_pre.astype(BF)
    act_out[...] = act
    d_pre_out[...] = low
    acc_r[...] += mm(act, down[...])
    acc_s[...] += mm(low, up[...], 1, 1)

    @pl.when(f == last)
    def _():
        for j in range(n_dp):
            both[j][:each] = acc_r[j * each : (j + 1) * each].astype(BF)
            both[j][each:] = acc_s[j * each : (j + 1) * each].astype(BF)


def experts_call(me, qkv, up, down, up_bias, down_bias, slots, grads, experts, part):
    n_dp = len(slots)
    each, width = slots[0].shape
    ff = up.shape[1]
    chunk = min(ff, 256)
    total = n_dp * each
    whole = pl.BlockSpec(memory_space=pltpu.VMEM)
    return pl.pallas_call(
        functools.partial(expert_kernel, n_dp=n_dp, experts=experts, part=part),
        grid=(ff // chunk,),
        out_shape=[jax.ShapeDtypeStruct((2 * each, width), BF)] * n_dp
        + [
            jax.ShapeDtypeStruct((total, ff), BF),
            jax.ShapeDtypeStruct((total, ff), BF),
            jax.ShapeDtypeStruct((total, width), BF),
            jax.ShapeDtypeStruct((total, width), BF),
            jax.ShapeDtypeStruct((1, ff), F32),
            jax.ShapeDtypeStruct((1, part), F32),
        ],
        in_specs=[
            pl.BlockSpec(memory_space=pltpu.SMEM),
            whole,
            pl.BlockSpec((width, chunk), lambda f: (0, f)),
            pl.BlockSpec((chunk, width), lambda f: (f, 0)),
            pl.BlockSpec((1, chunk), lambda f: (0, f)),
            whole,
        ]
        + [whole] * (2 * n_dp),
        out_specs=[whole] * n_dp
        + [
            pl.BlockSpec((total, chunk), lambda f: (0, f)),
            pl.BlockSpec((total, chunk), lambda f: (0, f)),
            whole,
            whole,
            pl.BlockSpec((1, chunk), lambda f: (0, f)),
            whole,
        ],
        scratch_shapes=[pltpu.VMEM((total, width), F32), pltpu.VMEM((total, width), F32)],
        name="expert_kernel",
    )(me, qkv, up, down, up_bias, down_bias, *slots, *grads)


def sum_of(refs):
    total = refs[0][...].astype(F32)
    for ref in refs[1:]:
        total = total + ref[...].astype(F32)
    return total


def line_sum_kernel(me, *refs, pad, capacity):
    out = refs[-1]
    two, width = refs[0].shape
    total = sum_of(refs[:-1])
    n_out = out.shape[0]
    r, c = lanes((n_out, two), 0), lanes((n_out, two), 1)
    pick = jnp.zeros((n_out, two), jnp.bool_)
    for e in range(n_out // (2 * pad)):
        for w in range(2):
            row, col = e * 2 * pad + w * pad, w * (two // 2) + e * capacity
            inside = (r >= row) & (r < row + capacity)
            pick = pick | (inside & (r - row == c - col))
    out[...] = mm(jnp.where(pick, 1.0, 0.0).astype(BF), total.astype(BF)).astype(BF)


def combine_kernel(
    me, back, route, rank, mixed, p, cotangent, qkv, vectors, proj,
    outputs, d_mixed, d_low_out, d_att, d_logits_out, sums, *, pad, capacity, experts, part,
):
    tok, width = mixed.shape
    n_back = back.shape[0]
    r, k = route[...], rank[...]
    key = jnp.where(k < capacity, r * (2 * pad) + k, -4 * pad * experts)
    slot = lanes((tok, n_back), 1)
    combined = mm(jnp.where(slot == key, 1.0, 0.0).astype(BF), back[...])
    d_slot = mm(jnp.where(slot == key + pad, 1.0, 0.0).astype(BF), back[...])
    hot = jnp.where(lanes(p.shape, 1) == r, 1.0, 0.0)
    gate = jnp.sum(p[...] * hot, axis=-1, keepdims=True)
    g = cotangent[...].astype(F32)
    outputs[...] = (mixed[...] + gate * combined).astype(BF)
    d_gate = jnp.sum(g * combined, axis=-1, keepdims=True)
    d_logits = (p[...] * (d_gate * hot - d_gate * gate)).astype(BF)
    d_logits_out[...] = d_logits
    d_normed = d_slot + mm(d_logits, qkv[:, 3 * part :], 1, 1)
    unit, scale = normalise(mixed[...])
    sums[0:1] = jnp.sum(d_normed * unit, axis=0, keepdims=True)
    sums[1:2] = jnp.sum(d_normed, axis=0, keepdims=True)
    d = g + norm_back(d_normed, vectors[1:2], unit, scale)
    sums[2:3] = jnp.sum(d, axis=0, keepdims=True)
    d_mixed[...] = d
    low = d.astype(BF)
    d_low_out[...] = low
    for i in range(d_att.shape[0]):
        d_att[i] = mm(low, proj[i * part : (i + 1) * part], 1, 1).astype(BF)


def share(me, whole, near, keep):
    half, n_dp, own, _ = near.shape
    for q in range(half):
        for d in range(n_dp):
            row = d * 2 * half * own
            other = pl.multiple_of(row + (me[1] ^ (2 * q + 1)) * own, own)
            same = pl.multiple_of(row + (me[1] ^ (2 * q)) * own, own)
            near[q, d] = whole[pl.ds(other, own)].astype(BF)
            keep[q, d] = whole[pl.ds(same, own)]


def proj_grad_kernel(me, attended, d_low, near, keep, whole):
    n_dp, rows, part = attended.shape
    for d in range(n_dp):
        whole[d * part : (d + 1) * part] = mm(attended[d], d_low[...], 0, 0)
    share(me, whole, near, keep)


def core_sum_kernel(me, keep, came, first, *rest):
    first[...] = keep[0] + came[0].astype(F32)
    for q, out in enumerate(rest):
        out[...] = (keep[q + 1] + came[q + 1].astype(F32)).astype(BF)


def chip_sum_kernel(me, *refs):
    out, half = refs[-1], (len(refs) - 1) // 2
    wide = refs[0].shape[2]
    out[:, :, :wide] = sum_of(refs[:half]).astype(BF)
    out[:, :, wide:] = sum_of(refs[half:-1]).astype(BF)


def core_sum(me, near, keep):
    half = near.shape[0]
    shape = near.shape[1:]
    return call(core_sum_kernel, [(shape, F32)] + [(shape, BF)] * (half - 1), me, keep, flip(near, 1))


def to_chips(parts):
    return [parts[0]] + [flip(part, 2 * (q + 1)) for q, part in enumerate(parts[1:])]


def attend_back_kernel(me, d_att, probs, packed, qkv, d_packed, d_normed, d_scores, *, head_dim):
    n_dp, rows, part = d_att.shape
    length = n_dp * rows
    scale = head_dim ** (-0.5)
    for h in range(part // head_dim):
        a, b = h * head_dim, (h + 1) * head_dim
        q, k, v = packed[:, a:b], packed[:, part + a : part + b], packed[:, 2 * part + a : 2 * part + b]
        g = jnp.concatenate([d_att[i, :, a:b] for i in range(n_dp)], axis=0)
        for i in range(n_dp):
            lo, hi = i * rows, (i + 1) * rows
            dp = mm(g[lo:hi], v[:hi], 1, 1)
            p = probs[h, lo:hi, :hi].astype(F32)
            delta = jnp.sum(p * dp, axis=-1, keepdims=True)
            ds = (p * (dp - delta)).astype(BF)
            d_scores[lo:hi, :hi] = ds
            if hi < length:
                d_scores[lo:hi, hi:] = jnp.zeros((rows, length - hi), BF)
            d_packed[lo:hi, a:b] = (mm(ds, k[:hi]) * scale).astype(BF)
        d_packed[:, part + a : part + b] = (mm(d_scores[...], q, 0, 0) * scale).astype(BF)
        d_packed[:, 2 * part + a : 2 * part + b] = mm(probs[h], g, 0, 0).astype(BF)
    for i in range(n_dp):
        d_normed[i] = mm(d_packed[i * rows : (i + 1) * rows], qkv[:, : 3 * part], 1, 1).astype(BF)


def qkv_grad_kernel(
    me, normed, unit, d_packed, d_normed, token_normed, d_logits, sums, near, keep, whole, turned, *, experts
):
    n_dp, rows, width = d_normed.shape
    part = width // n_dp
    whole[:, : 3 * part] = mm(normed[...], d_packed[...], 0, 0)
    gain = jnp.zeros((1, width), F32)
    shift = jnp.zeros((1, width), F32)
    for i in range(n_dp):
        d = d_normed[i].astype(F32)
        gain = gain + jnp.sum(d * unit[i * rows : (i + 1) * rows], axis=0, keepdims=True)
        shift = shift + jnp.sum(d, axis=0, keepdims=True)
    columns = jnp.sum(d_packed[...].astype(F32), axis=0, keepdims=True)
    turned[...] = jnp.zeros_like(turned)
    e = experts
    turned[e : e + 1] = gain
    turned[e + 1 : e + 2] = sums[0:1]
    turned[e + 2 : e + 3] = shift
    for d in range(n_dp):
        here = me[0] == d
        turned[e + 3 : e + 4, d * part : (d + 1) * part] = jnp.where(here, columns[:, :part], 0.0)
        turned[e + 4 : e + 5, d * part : (d + 1) * part] = jnp.where(here, columns[:, 2 * part :], 0.0)
    turned[e + 5 : e + 6] = sums[2:3]
    turned[e + 6 : e + 7] = sums[1:2]
    whole[:, 3 * part :] = turned[...].T + mm(token_normed[...], d_logits[...], 0, 0)
    share(me, whole, near, keep)


def weights_end_kernel(me, came, qkv, proj, router, gains, biases, wide):
    n_dp, own, _ = came.shape
    width = proj.shape[1]
    part = width // n_dp
    experts = router.shape[1]
    edge = 3 * part
    total = jnp.zeros((own, 128), F32)
    rows = jnp.zeros((own, width), F32)
    for d in range(n_dp):
        for i in range(3):
            qkv[:, i * width + d * part : i * width + (d + 1) * part] = came[
                d, :, i * part : (i + 1) * part
            ].astype(F32)
        total = total + came[d, :, edge : edge + 128].astype(F32)
        rows = rows + came[d, :, edge + 128 :].astype(F32)
    proj[...] = rows
    router[...] = total[:, :experts]
    wide[...] = jnp.zeros_like(wide)
    wide[:own] = total
    flat = wide[...].T
    gains[...] = flat[experts : experts + 2, :own]
    biases[...] = flat[experts + 2 : experts + 7, :own]


def tokens_end_kernel(me, came, tokens, vectors, d_mixed, out):
    total = came[0].astype(F32)
    for d in range(1, came.shape[0]):
        total = total + came[d].astype(F32)
    unit, scale = normalise(tokens[...].astype(F32))
    out[...] = d_mixed[...] + norm_back(total, vectors[0:1], unit, scale)


def shards(
    tokens,
    qkv_weight,
    proj_weight,
    router_weight,
    norm_gains,
    biases,
    up_weight,
    up_bias,
    down_weight,
    down_bias,
    routes,
    slot_order,
    segments,
    parents,
    cotangent,
):
    n_dp, n_ex = lax.axis_size("dp"), lax.axis_size("expert")
    me = jnp.stack([lax.axis_index("dp"), lax.axis_index("expert")]).astype(I32)
    rows, width = tokens.shape[1], tokens.shape[2]
    part = width // n_dp
    head_dim = width // H
    own = qkv_weight.shape[0]
    experts = router_weight.shape[1]
    capacity = (9 * rows + 8 * experts - 1) // (8 * experts)
    pad = -(-capacity // 8) * 8
    length = n_dp * rows
    each = n_ex * capacity
    cols = 3 * part + 128
    x = tokens[0]

    token_blocks = along([x] * n_dp)
    columns = call(
        weights_kernel,
        [((n_dp, own, cols), BF)],
        me, qkv_weight, router_weight, norm_gains, biases,
        scratch=[pltpu.VMEM((128, 128), F32), pltpu.VMEM((own, 128), F32)],
        n_dp=n_dp,
    )[0]
    middle = n_dp // 2
    stacked, token_blocks[middle] = lax.optimization_barrier((swap(columns, "dp"), token_blocks[middle]))
    qkv_blocks = gather_experts(stacked)
    smem = pl.BlockSpec(memory_space=pltpu.SMEM)
    vmem = pl.BlockSpec(memory_space=pltpu.VMEM)
    grads_out, tableT, rank, bias = pl.pallas_call(
        functools.partial(slots_kernel, pad=pad, capacity=capacity, experts=experts),
        out_shape=[
            jax.ShapeDtypeStruct((n_ex * pad, width), BF),
            jax.ShapeDtypeStruct((n_ex * pad, rows), BF),
            jax.ShapeDtypeStruct((rows, 1), I32),
            jax.ShapeDtypeStruct((length, length), F32),
        ],
        in_specs=[smem, smem] + [vmem] * 4,
        out_specs=[vmem] * 4,
        name="slots_kernel",
    )(me, parents, routes[0], slot_order[0], cotangent[0], segments)

    def dispatch(rows_out):
        came = swap(rows_out.reshape(n_ex, pad, width), "expert").reshape(n_ex * pad, width)
        mine = call(pack_kernel, [((each, width), BF)], me, came, pad=pad, capacity=capacity)[0]
        return mine

    grads_in = dispatch(grads_out)
    proj_blocks = gather_experts(swap(jnp.broadcast_to(proj_weight, (n_dp, own, width)), "dp"))
    grads_in, bias = lax.optimization_barrier((grads_in, bias))
    grads = along([grads_in] * n_dp)
    qkv = call(assemble_kernel, [((n_dp, n_ex, own, cols), BF)], me, *qkv_blocks)[0].reshape(width, cols)
    normed1, unit1, packed, probs, att_out, vectors = call(
        attend_kernel,
        [
            ((length, width), BF),
            ((length, width), F32),
            ((length, 3 * part), BF),
            ((part // head_dim, length, length), BF),
            ((n_dp, rows, part), BF),
            ((8, width), F32),
        ],
        me, qkv, bias, *token_blocks,
        n_dp=n_dp, head_dim=head_dim, experts=experts,
    )
    early = [j for j in range(1, n_dp) if j != n_dp // 2]
    att_out, *came = lax.optimization_barrier((att_out, *[grads[j] for j in early]))
    for j, block in zip(early, came):
        grads[j] = block
    attended = swap(att_out, "dp")
    proj = call(assemble_kernel, [((n_dp, n_ex, own, width), BF)], me, *proj_blocks)[0].reshape(width, width)
    mixed, normed2, p, sent = call(
        mix_kernel,
        [((rows, width), F32), ((rows, width), BF), ((rows, 128), F32), ((n_ex * pad, width), BF)],
        me, x, attended, proj, qkv, vectors, tableT,
        experts=experts,
    )
    mine, grads = lax.optimization_barrier((dispatch(sent), grads))
    slots = along([mine] * n_dp)
    *both, act, d_pre, slot_rows, d_rows, grad_up_bias, grad_down_bias = experts_call(
        me, qkv, up_weight[0], down_weight[0], up_bias, down_bias, slots, grads, experts, part
    )
    came = along(both, -1)
    grad_up = mm(slot_rows, d_pre, 0, 0)
    grad_down = mm(act, d_rows, 0, 0)
    grad_up, grad_down, *came = lax.optimization_barrier((grad_up, grad_down, *came))
    summed = call(line_sum_kernel, [((n_ex * 2 * pad, width), BF)], me, *came, pad=pad, capacity=capacity)[0]
    back = swap(summed.reshape(n_ex, 2 * pad, width), "expert").reshape(n_ex * 2 * pad, width)
    outputs, d_mixed, d_low, d_att, d_logits, sums = call(
        combine_kernel,
        [
            ((rows, width), BF),
            ((rows, width), F32),
            ((rows, width), BF),
            ((n_dp, rows, part), BF),
            ((rows, 128), BF),
            ((8, width), F32),
        ],
        me, back, routes[0], rank, mixed, p, cotangent[0], qkv, vectors, proj,
        pad=pad, capacity=capacity, experts=experts, part=part,
    )
    d_heads = swap(d_att, "dp")
    half = n_ex // 2
    near, keep = call(
        proj_grad_kernel,
        [((half, n_dp, own, width), BF), ((half, n_dp, own, width), F32)],
        me, attended, d_low,
        scratch=[pltpu.VMEM((width, width), F32)],
    )
    d_heads, *parts = lax.optimization_barrier((d_heads, *core_sum(me, near, keep)))
    proj_chips = to_chips(parts)
    d_packed, d_normed = call(
        attend_back_kernel,
        [((length, 3 * part), BF), ((n_dp, rows, width), BF)],
        me, d_heads, probs, packed, qkv,
        scratch=[pltpu.VMEM((length, length), BF)],
        head_dim=head_dim,
    )
    d_own = swap(d_normed, "dp")
    near, keep = call(
        qkv_grad_kernel,
        [((half, n_dp, own, cols), BF), ((half, n_dp, own, cols), F32)],
        me, normed1, unit1, d_packed, d_normed, normed2, d_logits, sums,
        scratch=[pltpu.VMEM((width, cols), F32), pltpu.VMEM((128, width), F32)],
        experts=experts,
    )
    near, keep, *proj_chips = lax.optimization_barrier((near, keep, *proj_chips))
    qkv_chips = to_chips(core_sum(me, near, keep))
    d_own, *qkv_chips = lax.optimization_barrier((d_own, *qkv_chips))
    summed = call(
        chip_sum_kernel, [((n_dp, own, cols + width), BF)], me, *qkv_chips, *proj_chips
    )[0]
    owned_qkv, owned_proj, owned_router, owned_gains, owned_biases = call(
        weights_end_kernel,
        [
            ((own, 3 * width), F32),
            ((own, width), F32),
            ((own, experts), F32),
            ((2, own), F32),
            ((5, own), F32),
        ],
        me, swap(summed, "dp"),
        scratch=[pltpu.VMEM((128, 128), F32)],
    )
    grad_tokens = call(tokens_end_kernel, [((rows, width), F32)], me, d_own, x, vectors, d_mixed)[0]
    return (
        outputs[None],
        grad_tokens[None],
        owned_qkv,
        owned_proj,
        owned_router,
        owned_gains,
        owned_biases,
        grad_up[None],
        grad_up_bias,
        grad_down[None],
        grad_down_bias,
    )


def solution(mesh):
    line = P(("dp", "expert"), None)
    across = P(None, ("dp", "expert"))
    act = P("expert", "dp", None)
    return jax.shard_map(
        shards,
        mesh=mesh,
        in_specs=(
            act,
            line,
            line,
            line,
            across,
            across,
            P("expert", None, "dp"),
            P("expert", "dp"),
            act,
            P("expert", "dp"),
            act,
            act,
            P("expert", None),
            P("expert", None),
            act,
        ),
        out_specs=(
            act,
            act,
            line,
            line,
            line,
            across,
            across,
            P("expert", None, "dp"),
            P("expert", "dp"),
            act,
            P("expert", "dp"),
        ),
        check_vma=False,
    )
```

```python
import functools

import jax
import jax.numpy as jnp
from jax import lax
from jax.experimental import pallas as pl
from jax.experimental.pallas import tpu as pltpu
from jax.sharding import PartitionSpec as P

H = 16
NSEG = 7
EPS = 1e-05
NEG = -1e30
BF = jnp.bfloat16
F32 = jnp.float32
I32 = jnp.int32


def mm(a, b, ca=1, cb=0):
    return lax.dot_general(a, b, (((ca,), (cb,)), ((), ())), preferred_element_type=F32)


def placed(kernel):
    def body(*refs):
        kernel((lax.axis_index("dp"), lax.axis_index("expert")), *refs)

    return body


def call(kernel, outs, *args, scratch=(), **static):
    vmem = pl.BlockSpec(memory_space=pltpu.VMEM)
    return pl.pallas_call(
        placed(functools.partial(kernel, **static)),
        out_shape=[jax.ShapeDtypeStruct(s, d) for s, d in outs],
        in_specs=[vmem] * len(args),
        out_specs=[vmem] * len(outs),
        scratch_shapes=list(scratch),
        name=kernel.__name__,
    )(*args)


def ahead(x, step):
    n = lax.axis_size("dp")
    return lax.ppermute(x, "dp", [(i, (i + step) % n) for i in range(n)])


def flip(x, bits):
    n = lax.axis_size("expert")
    return lax.ppermute(x, "expert", [(i, i ^ bits) for i in range(n)])


def swap(x, axis):
    return lax.all_to_all(x, axis, split_axis=0, concat_axis=0, tiled=True)


def along(blocks, sign=1):
    return [blocks[0]] + [ahead(blocks[j], sign * j) for j in range(1, len(blocks))]


def spread(x):
    n = lax.axis_size("dp")
    if n != 4:
        return [x] + [ahead(x, j) for j in range(1, n)]
    far = lax.ppermute(x, "dp", [(0, 2), (1, 3), (2, 0), (3, 1)])
    up = lax.ppermute(x, "dp", [(0, 1), (1, 2), (2, 3)])
    down = lax.ppermute(x, "dp", [(1, 0), (2, 1), (3, 2)])
    end = lax.ppermute(far, "dp", [(1, 0), (2, 3)])
    return [x, up, down, far, end]


def place(me, blocks, put):
    d, n = me[0], len(blocks)
    if n != 5:
        for j, block in enumerate(blocks):
            put(block, (d + n - j) % n)
        return
    own, up, down, far, end = blocks
    put(own, d)
    pl.when(d > 0)(lambda: put(up, d - 1))
    pl.when(d < 3)(lambda: put(down, d + 1))
    put(far, d ^ 2)
    pl.when((d == 0) | (d == 3))(lambda: put(end, d ^ 3))


def gather_experts(x):
    n = lax.axis_size("expert")
    mine = [x] + [flip(x, 2 * k) for k in range(1, n // 2)]
    out = []
    for block in mine:
        out += [block, flip(block, 1)]
    return out


def normalise(values):
    mean = jnp.mean(values, axis=-1, keepdims=True)
    centred = values - mean
    scale = lax.rsqrt(jnp.mean(centred * centred, axis=-1, keepdims=True) + EPS)
    return centred * scale, scale


def norm_back(upstream, gain, unit, scale):
    e = upstream * gain
    return scale * (
        e - jnp.mean(e, axis=-1, keepdims=True) - unit * jnp.mean(e * unit, axis=-1, keepdims=True)
    )


def lanes(shape, dim):
    return lax.broadcasted_iota(I32, shape, dim)


def softmax_of(logits, experts):
    logits = jnp.where(lanes(logits.shape, 1) < experts, logits, NEG)
    top = jnp.max(logits, axis=-1, keepdims=True)
    weight = jnp.exp(logits - top)
    return weight / jnp.sum(weight, axis=-1, keepdims=True)


def weights_kernel(me, qkv, router, gains, biases, out, turned, *, n_dp):
    own, width = qkv.shape[0], qkv.shape[1] // 3
    part = width // n_dp
    experts = router.shape[0]
    turned[...] = jnp.zeros_like(turned)
    turned[:experts, :own] = router[...].astype(F32)
    turned[experts : experts + 2, :own] = gains[...].astype(F32)
    turned[experts + 2 : experts + 7, :own] = biases[...].astype(F32)
    small = turned[...].T[:own].astype(BF)
    for d in range(n_dp):
        for i in range(3):
            out[d, :, i * part : (i + 1) * part] = qkv[
                :, i * width + d * part : i * width + (d + 1) * part
            ]
        out[d, :, 3 * part :] = small


def slots_kernel(
    me, parents, route, order, cotangent, seg, grads, tableT, route_out, rank_out, bias, *, pad, capacity, experts
):
    tok = route.shape[1]
    rt = jnp.broadcast_to(route[...].astype(F32), (tok, tok))
    r = rt.T
    route_out[...] = r[:, 0:1].astype(I32)
    o = jnp.broadcast_to(order[...].astype(F32), (tok, tok))
    ot = o.T
    same = r == rt
    rank = jnp.sum(jnp.where(same & (o < ot), 1.0, 0.0), axis=1, keepdims=True)
    rank_row = jnp.sum(jnp.where(same & (ot < o), 1.0, 0.0), axis=0, keepdims=True)
    rank_out[...] = rank.astype(I32)
    key = jnp.where(rank_row < capacity, rt[0:1] * pad + rank_row, -1.0).astype(I32)
    table = jnp.where(lanes((experts * pad, tok), 0) == key, 1.0, 0.0).astype(BF)
    tableT[...] = table
    grads[...] = mm(table, cotangent[...]).astype(BF)
    length = seg.shape[1]
    masks = [jnp.int32(1)]
    for s in range(1, NSEG):
        up = jnp.int32(0)
        for a in range(s):
            up = jnp.where(parents[0, s] == a, masks[a], up)
        masks.append(up | (1 << s))
    block = 128
    keys = seg[...]
    for i in range(length // block):
        col = jnp.broadcast_to(seg[:, i * block : (i + 1) * block].astype(F32), (block, block)).T
        col = jnp.broadcast_to(col[:, 0:1], (block, length)).astype(I32)
        mine = jnp.zeros((block, length), I32)
        for s in range(NSEG):
            mine = jnp.where(col == s, masks[s], mine)
        ok = jnp.zeros((block, length), I32)
        for s in range(NSEG):
            ok = jnp.where(keys == s, mine & (1 << s), ok)
        seen = lanes((block, length), 1) <= lanes((block, length), 0) + i * block
        bias[i * block : (i + 1) * block] = jnp.where(seen & (ok > 0), 0.0, NEG)


def pack_kernel(me, rows, out, *, pad, capacity):
    n_out, n_in = out.shape[0], rows.shape[0]
    r, c = lanes((n_out, n_in), 0), lanes((n_out, n_in), 1)
    pick = jnp.zeros((n_out, n_in), jnp.bool_)
    for e in range(n_in // pad):
        inside = (r >= e * capacity) & (r < (e + 1) * capacity)
        pick = pick | (inside & (c - e * pad == r - e * capacity))
    out[...] = mm(jnp.where(pick, 1.0, 0.0).astype(BF), rows[...]).astype(BF)


def assemble_kernel(me, *refs):
    out = refs[-1]
    for k, block in enumerate(refs[:-1]):
        e = me[1] ^ k
        for d in range(block.shape[0]):
            out[d, e] = block[d]


def attend_kernel(me, qkv, bias, *refs, n_dp, head_dim, experts):
    tokens, (normed, unit, packed, probs, attended, vectors) = refs[:-6], refs[-6:]
    rows, width = tokens[0].shape
    part = width // n_dp
    small = qkv[:, 3 * part :].astype(F32).T
    vectors[...] = small[experts : experts + 8]
    gain, shift = vectors[0:1], vectors[2:3]
    parts = [jnp.zeros((1, part), F32)] * 2
    for d in range(n_dp):
        for i in range(2):
            here = vectors[3 + i : 4 + i, d * part : (d + 1) * part]
            parts[i] = parts[i] + jnp.where(me[0] == d, here, 0.0)

    def put(block, d):
        base = pl.multiple_of(d * rows, rows)
        centred, _ = normalise(block[...].astype(F32))
        unit[pl.ds(base, rows)] = centred
        normed[pl.ds(base, rows)] = (centred * gain + shift).astype(BF)

    place(me, tokens, put)
    raw = mm(normed[...], qkv[:, : 3 * part])
    packed[:, :part] = (raw[:, :part] + parts[0]).astype(BF)
    packed[:, part : 2 * part] = raw[:, part : 2 * part].astype(BF)
    packed[:, 2 * part :] = (raw[:, 2 * part :] + parts[1]).astype(BF)
    scale = head_dim ** (-0.5)
    length = rows * n_dp
    for h in range(part // head_dim):
        q = packed[:, h * head_dim : (h + 1) * head_dim]
        k = packed[:, part + h * head_dim : part + (h + 1) * head_dim]
        v = packed[:, 2 * part + h * head_dim : 2 * part + (h + 1) * head_dim]
        for i in range(n_dp):
            lo, hi = i * rows, (i + 1) * rows
            s = mm(q[lo:hi], k[:hi], 1, 1) * scale + bias[lo:hi, :hi]
            top = jnp.max(s, axis=-1, keepdims=True)
            p = jnp.exp(s - top)
            p = (p * (1.0 / jnp.sum(p, axis=-1, keepdims=True))).astype(BF)
            probs[h, lo:hi, :hi] = p
            if hi < length:
                probs[h, lo:hi, hi:] = jnp.zeros((rows, length - hi), BF)
            attended[i, :, h * head_dim : (h + 1) * head_dim] = mm(p, v[:hi]).astype(BF)


def mix_kernel(me, tokens, attended, proj, qkv, vectors, tableT, mixed, normed, p, sent, *, experts):
    n_dp, rows, part = attended.shape
    total = tokens[...].astype(F32) + vectors[5:6]
    for d in range(n_dp):
        total = total + mm(attended[d], proj[d * part : (d + 1) * part])
    mixed[...] = total
    unit, _ = normalise(total)
    low = (unit * vectors[1:2] + vectors[6:7]).astype(BF)
    normed[...] = low
    p[...] = softmax_of(mm(low, qkv[:, 3 * part :]), experts)
    sent[...] = mm(tableT[...], low).astype(BF)


def expert_kernel(
    me, qkv, up, down, up_bias, down_bias, slots, grads,
    both, act_out, d_pre_out, d_rows, g_up_bias, acc_r, acc_s, *, n_dp, experts,
):
    f = pl.program_id(0)
    each, width = slots.shape
    part = width // n_dp

    @pl.when(f == 0)
    def _():
        p = softmax_of(mm(slots[...], qkv[:, 3 * part :]), experts)
        gate = jnp.sum(jnp.where(lanes(p.shape, 1) == me[1], p, 0.0), axis=-1, keepdims=True)
        d_rows[...] = (gate * grads[...].astype(F32)).astype(BF)
        acc_s[...] = jnp.zeros_like(acc_s)
        for d in range(n_dp):
            acc_r[:, d * part : (d + 1) * part] = jnp.broadcast_to(
                jnp.where(me[0] == d, down_bias[...].astype(F32), 0.0), (each, part)
            )

    u = mm(slots[...], up[...]) + up_bias[...].astype(F32)
    c, a = 0.7978845608028654, 0.044715
    t = jnp.tanh(c * (u + a * (u * u * u)))
    act = (0.5 * u * (1.0 + t)).astype(BF)
    slope = 0.5 * (1.0 + t) + 0.5 * u * (1.0 - t * t) * (c * (1.0 + 3.0 * a * (u * u)))
    d_pre = mm(d_rows[...], down[...], 1, 1) * slope
    g_up_bias[...] = jnp.sum(d_pre, axis=0, keepdims=True)
    low = d_pre.astype(BF)
    act_out[...] = act
    d_pre_out[...] = low
    acc_r[...] += mm(act, down[...])
    acc_s[...] += mm(low, up[...], 1, 1)

    @pl.when(f == pl.num_programs(0) - 1)
    def _():
        both[:each] = acc_r[...].astype(BF)
        both[each:] = acc_s[...].astype(BF)


def expert_call(qkv, up, down, up_bias, down_bias, slots, grads, n_dp, experts):
    each, width = slots.shape
    ff = up.shape[1]
    chunk = min(ff, 256)
    whole = pl.BlockSpec(memory_space=pltpu.VMEM)
    across = pl.BlockSpec((each, chunk), lambda f: (0, f))
    row = pl.BlockSpec((1, chunk), lambda f: (0, f))
    return pl.pallas_call(
        placed(functools.partial(expert_kernel, n_dp=n_dp, experts=experts)),
        grid=(ff // chunk,),
        out_shape=[
            jax.ShapeDtypeStruct((2 * each, width), BF),
            jax.ShapeDtypeStruct((each, ff), BF),
            jax.ShapeDtypeStruct((each, ff), BF),
            jax.ShapeDtypeStruct((each, width), BF),
            jax.ShapeDtypeStruct((1, ff), F32),
        ],
        in_specs=[
            whole,
            pl.BlockSpec((width, chunk), lambda f: (0, f)),
            pl.BlockSpec((chunk, width), lambda f: (f, 0)),
            row,
            whole,
            whole,
            whole,
        ],
        out_specs=[whole, across, across, whole, row],
        scratch_shapes=[pltpu.VMEM((each, width), F32), pltpu.VMEM((each, width), F32)],
        name="expert_kernel",
    )(qkv, up, down, up_bias, down_bias, slots, grads)


def expert_grad_kernel(me, *refs, n_dp):
    slots, act, d_pre, d_rows, up_bias = (refs[i * n_dp : (i + 1) * n_dp] for i in range(5))
    grad_up, grad_down, g_up_bias, g_down_bias = refs[5 * n_dp :]
    grad_up[...] = sum(mm(a[...], b[...], 0, 0) for a, b in zip(slots, d_pre))
    grad_down[...] = sum(mm(a[...], b[...], 0, 0) for a, b in zip(act, d_rows))

    @pl.when(pl.program_id(0) == 0)
    def _():
        g_up_bias[...] = sum_of(up_bias)
        sums = sum(jnp.sum(r[...].astype(F32), axis=0, keepdims=True) for r in d_rows)
        part = g_down_bias.shape[1]
        own = jnp.zeros((1, part), F32)
        for d in range(n_dp):
            own = own + jnp.where(me[0] == d, sums[:, d * part : (d + 1) * part], 0.0)
        g_down_bias[...] = own


def expert_grads(slots, act, d_pre, d_rows, up_bias, part):
    n_dp = len(slots)
    each, width = slots[0].shape
    ff = act[0].shape[1]
    steps = 4
    whole = pl.BlockSpec(memory_space=pltpu.VMEM)
    return pl.pallas_call(
        placed(functools.partial(expert_grad_kernel, n_dp=n_dp)),
        grid=(steps,),
        out_shape=[
            jax.ShapeDtypeStruct((width, ff), F32),
            jax.ShapeDtypeStruct((ff, width), F32),
            jax.ShapeDtypeStruct((1, ff), F32),
            jax.ShapeDtypeStruct((1, part), F32),
        ],
        in_specs=[pl.BlockSpec((each, width // steps), lambda f: (0, f))] * n_dp
        + [pl.BlockSpec((each, ff // steps), lambda f: (0, f))] * n_dp
        + [whole] * (3 * n_dp),
        out_specs=[
            pl.BlockSpec((width // steps, ff), lambda f: (f, 0)),
            pl.BlockSpec((ff // steps, width), lambda f: (f, 0)),
            whole,
            whole,
        ],
        name="expert_grad_kernel",
    )(*slots, *act, *d_pre, *d_rows, *up_bias)


def sum_of(refs):
    total = refs[0][...].astype(F32)
    for ref in refs[1:]:
        total = total + ref[...].astype(F32)
    return total


def line_sum_kernel(me, *refs, pad, capacity):
    out = refs[-1]
    two, width = refs[0].shape
    total = sum_of(refs[:-1])
    n_out = out.shape[0]
    r, c = lanes((n_out, two), 0), lanes((n_out, two), 1)
    pick = jnp.zeros((n_out, two), jnp.bool_)
    for e in range(n_out // (2 * pad)):
        for w in range(2):
            row, col = e * 2 * pad + w * pad, w * (two // 2) + e * capacity
            inside = (r >= row) & (r < row + capacity)
            pick = pick | (inside & (r - row == c - col))
    out[...] = mm(jnp.where(pick, 1.0, 0.0).astype(BF), total.astype(BF)).astype(BF)


def combine_kernel(
    me, back, route, rank, mixed, p, cotangent, qkv, vectors, proj,
    outputs, d_mixed, d_low_out, d_att, d_logits_out, sums, *, pad, capacity, experts, part,
):
    tok, width = mixed.shape
    n_back = back.shape[0]
    r, k = route[...], rank[...]
    key = jnp.where(k < capacity, r * (2 * pad) + k, -4 * pad * experts)
    slot = lanes((tok, n_back), 1)
    combined = mm(jnp.where(slot == key, 1.0, 0.0).astype(BF), back[...])
    d_slot = mm(jnp.where(slot == key + pad, 1.0, 0.0).astype(BF), back[...])
    hot = jnp.where(lanes(p.shape, 1) == r, 1.0, 0.0)
    gate = jnp.sum(p[...] * hot, axis=-1, keepdims=True)
    g = cotangent[...].astype(F32)
    outputs[...] = (mixed[...] + gate * combined).astype(BF)
    d_gate = jnp.sum(g * combined, axis=-1, keepdims=True)
    d_logits = (p[...] * (d_gate * hot - d_gate * gate)).astype(BF)
    d_logits_out[...] = d_logits
    d_normed = d_slot + mm(d_logits, qkv[:, 3 * part :], 1, 1)
    unit, scale = normalise(mixed[...])
    sums[0:1] = jnp.sum(d_normed * unit, axis=0, keepdims=True)
    sums[1:2] = jnp.sum(d_normed, axis=0, keepdims=True)
    d = g + norm_back(d_normed, vectors[1:2], unit, scale)
    sums[2:3] = jnp.sum(d, axis=0, keepdims=True)
    d_mixed[...] = d
    low = d.astype(BF)
    d_low_out[...] = low
    for i in range(d_att.shape[0]):
        d_att[i] = mm(low, proj[i * part : (i + 1) * part], 1, 1).astype(BF)


def share(me, whole, near, keep):
    half, n_dp, own, _ = near.shape
    for q in range(half):
        for d in range(n_dp):
            row = d * 2 * half * own
            other = pl.multiple_of(row + (me[1] ^ (2 * q + 1)) * own, own)
            same = pl.multiple_of(row + (me[1] ^ (2 * q)) * own, own)
            near[q, d] = whole[pl.ds(other, own)].astype(BF)
            keep[q, d] = whole[pl.ds(same, own)]


def proj_grad_kernel(me, attended, d_low, near, keep, whole):
    n_dp, rows, part = attended.shape
    for d in range(n_dp):
        whole[d * part : (d + 1) * part] = mm(attended[d], d_low[...], 0, 0)
    share(me, whole, near, keep)


def core_sum_kernel(me, keep, came, first, *rest):
    first[...] = keep[0] + came[0].astype(F32)
    for q, out in enumerate(rest):
        out[...] = (keep[q + 1] + came[q + 1].astype(F32)).astype(BF)


def chip_sum_kernel(me, *refs):
    out, half = refs[-1], (len(refs) - 1) // 2
    wide = refs[0].shape[2]
    out[:, :, :wide] = sum_of(refs[:half]).astype(BF)
    out[:, :, wide:] = sum_of(refs[half:-1]).astype(BF)


def core_sum(near, keep):
    half = near.shape[0]
    shape = near.shape[1:]
    return call(core_sum_kernel, [(shape, F32)] + [(shape, BF)] * (half - 1), keep, flip(near, 1))


def to_chips(parts):
    return [parts[0]] + [flip(part, 2 * (q + 1)) for q, part in enumerate(parts[1:])]


def attend_back_kernel(me, d_att, probs, packed, qkv, d_packed, d_normed, d_scores, *, head_dim):
    n_dp, rows, part = d_att.shape
    length = n_dp * rows
    scale = head_dim ** (-0.5)
    for h in range(part // head_dim):
        a, b = h * head_dim, (h + 1) * head_dim
        q, k, v = packed[:, a:b], packed[:, part + a : part + b], packed[:, 2 * part + a : 2 * part + b]
        g = jnp.concatenate([d_att[i, :, a:b] for i in range(n_dp)], axis=0)
        for i in range(n_dp):
            lo, hi = i * rows, (i + 1) * rows
            dp = mm(g[lo:hi], v[:hi], 1, 1)
            p = probs[h, lo:hi, :hi].astype(F32)
            delta = jnp.sum(p * dp, axis=-1, keepdims=True)
            ds = (p * (dp - delta)).astype(BF)
            d_scores[lo:hi, :hi] = ds
            if hi < length:
                d_scores[lo:hi, hi:] = jnp.zeros((rows, length - hi), BF)
            d_packed[lo:hi, a:b] = (mm(ds, k[:hi]) * scale).astype(BF)
        d_packed[:, part + a : part + b] = (mm(d_scores[...], q, 0, 0) * scale).astype(BF)
        d_packed[:, 2 * part + a : 2 * part + b] = mm(probs[h], g, 0, 0).astype(BF)
    for i in range(n_dp):
        d_normed[i] = mm(d_packed[i * rows : (i + 1) * rows], qkv[:, : 3 * part], 1, 1).astype(BF)


def qkv_grad_kernel(
    me, normed, unit, d_packed, d_normed, token_normed, d_logits, sums, near, keep, whole, turned, *, experts
):
    n_dp, rows, width = d_normed.shape
    part = width // n_dp
    whole[:, : 3 * part] = mm(normed[...], d_packed[...], 0, 0)
    gain = jnp.zeros((1, width), F32)
    shift = jnp.zeros((1, width), F32)
    for i in range(n_dp):
        d = d_normed[i].astype(F32)
        gain = gain + jnp.sum(d * unit[i * rows : (i + 1) * rows], axis=0, keepdims=True)
        shift = shift + jnp.sum(d, axis=0, keepdims=True)
    columns = jnp.sum(d_packed[...].astype(F32), axis=0, keepdims=True)
    turned[...] = jnp.zeros_like(turned)
    e = experts
    turned[e : e + 1] = gain
    turned[e + 1 : e + 2] = sums[0:1]
    turned[e + 2 : e + 3] = shift
    for d in range(n_dp):
        here = me[0] == d
        turned[e + 3 : e + 4, d * part : (d + 1) * part] = jnp.where(here, columns[:, :part], 0.0)
        turned[e + 4 : e + 5, d * part : (d + 1) * part] = jnp.where(here, columns[:, 2 * part :], 0.0)
    turned[e + 5 : e + 6] = sums[2:3]
    turned[e + 6 : e + 7] = sums[1:2]
    whole[:, 3 * part :] = turned[...].T + mm(token_normed[...], d_logits[...], 0, 0)
    share(me, whole, near, keep)


def weights_end_kernel(me, came, qkv, proj, router, gains, biases, wide):
    n_dp, own, _ = came.shape
    width = proj.shape[1]
    part = width // n_dp
    experts = router.shape[0]
    edge = 3 * part
    total = jnp.zeros((own, 128), F32)
    rows = jnp.zeros((own, width), F32)
    for d in range(n_dp):
        for i in range(3):
            qkv[:, i * width + d * part : i * width + (d + 1) * part] = came[
                d, :, i * part : (i + 1) * part
            ].astype(F32)
        total = total + came[d, :, edge : edge + 128].astype(F32)
        rows = rows + came[d, :, edge + 128 :].astype(F32)
    proj[...] = rows
    wide[...] = jnp.zeros_like(wide)
    wide[:own] = total
    flat = wide[...].T
    router[...] = flat[:experts, :own]
    gains[...] = flat[experts : experts + 2, :own]
    biases[...] = flat[experts + 2 : experts + 7, :own]


def tokens_end_kernel(me, came, tokens, vectors, d_mixed, out):
    total = came[0].astype(F32)
    for d in range(1, came.shape[0]):
        total = total + came[d].astype(F32)
    unit, scale = normalise(tokens[...].astype(F32))
    out[...] = d_mixed[...] + norm_back(total, vectors[0:1], unit, scale)


def shards(
    tokens,
    qkv_weight,
    proj_weight,
    router_weight,
    norm_gains,
    biases,
    up_weight,
    up_bias,
    down_weight,
    down_bias,
    routes,
    slot_order,
    segments,
    parents,
    cotangent,
):
    n_dp, n_ex = lax.axis_size("dp"), lax.axis_size("expert")
    rows, width = tokens.shape[1], tokens.shape[2]
    part = width // n_dp
    head_dim = width // H
    own = qkv_weight.shape[0]
    experts = router_weight.shape[1]
    capacity = (9 * rows + 8 * experts - 1) // (8 * experts)
    pad = -(-capacity // 8) * 8
    length = n_dp * rows
    each = n_ex * capacity
    cols = 3 * part + 128
    x = tokens[0]

    token_blocks = spread(x)
    columns = call(
        weights_kernel,
        [((n_dp, own, cols), BF)],
        qkv_weight, router_weight.T, norm_gains, biases,
        scratch=[pltpu.VMEM((128, 128), F32)],
        n_dp=n_dp,
    )[0]
    qkv_blocks = gather_experts(swap(columns, "dp"))
    smem = pl.BlockSpec(memory_space=pltpu.SMEM)
    vmem = pl.BlockSpec(memory_space=pltpu.VMEM)
    grads_out, tableT, route, rank, bias = pl.pallas_call(
        placed(functools.partial(slots_kernel, pad=pad, capacity=capacity, experts=experts)),
        out_shape=[
            jax.ShapeDtypeStruct((n_ex * pad, width), BF),
            jax.ShapeDtypeStruct((n_ex * pad, rows), BF),
            jax.ShapeDtypeStruct((rows, 1), I32),
            jax.ShapeDtypeStruct((rows, 1), I32),
            jax.ShapeDtypeStruct((length, length), F32),
        ],
        in_specs=[smem] + [vmem] * 4,
        out_specs=[vmem] * 5,
        name="slots_kernel",
    )(parents, routes.reshape(1, rows), slot_order[0], cotangent[0], segments)

    def dispatch(rows_out):
        came = swap(rows_out.reshape(n_ex, pad, width), "expert").reshape(n_ex * pad, width)
        mine = call(pack_kernel, [((each, width), BF)], came, pad=pad, capacity=capacity)[0]
        return mine

    grads_in = dispatch(grads_out)
    proj_blocks = gather_experts(swap(jnp.broadcast_to(proj_weight, (n_dp, own, width)), "dp"))
    grads_in, bias = lax.optimization_barrier((grads_in, bias))
    grads = along([grads_in] * n_dp)
    qkv = call(assemble_kernel, [((n_dp, n_ex, own, cols), BF)], *qkv_blocks)[0].reshape(width, cols)
    normed1, unit1, packed, probs, att_out, vectors = call(
        attend_kernel,
        [
            ((length, width), BF),
            ((length, width), F32),
            ((length, 3 * part), BF),
            ((part // head_dim, length, length), BF),
            ((n_dp, rows, part), BF),
            ((8, width), F32),
        ],
        qkv, bias, *token_blocks,
        n_dp=n_dp, head_dim=head_dim, experts=experts,
    )
    early = [j for j in range(1, n_dp) if j != n_dp // 2]
    att_out, *came = lax.optimization_barrier((att_out, *[grads[j] for j in early]))
    for j, block in zip(early, came):
        grads[j] = block
    attended = swap(att_out, "dp")
    proj = call(assemble_kernel, [((n_dp, n_ex, own, width), BF)], *proj_blocks)[0].reshape(width, width)
    mixed, normed2, p, sent = call(
        mix_kernel,
        [((rows, width), F32), ((rows, width), BF), ((rows, 128), F32), ((n_ex * pad, width), BF)],
        x, attended, proj, qkv, vectors, tableT,
        experts=experts,
    )
    mine, grads = lax.optimization_barrier((dispatch(sent), grads))
    slots = along([mine] * n_dp)
    order = [0] + early + [n_dp // 2]
    done = {}
    came = [None] * n_dp
    for i, j in enumerate(order):
        if i > 0:
            last = order[i - 1]
            slots[j], *done[last] = lax.optimization_barrier((slots[j], *done[last]))
        done[j] = expert_call(
            qkv, up_weight[0], down_weight[0], up_bias, down_bias, slots[j], grads[j], n_dp, experts
        )
        came[j] = ahead(done[j][0], -j) if j else done[j][0]
    act, d_pre, d_rows, g_up_bias = ([done[j][i] for j in range(n_dp)] for i in range(1, 5))
    grad_up, grad_down, grad_up_bias, grad_down_bias = expert_grads(
        slots, act, d_pre, d_rows, g_up_bias, part
    )
    grad_up, grad_down, *came = lax.optimization_barrier((grad_up, grad_down, *came))
    summed = call(line_sum_kernel, [((n_ex * 2 * pad, width), BF)], *came, pad=pad, capacity=capacity)[0]
    back = swap(summed.reshape(n_ex, 2 * pad, width), "expert").reshape(n_ex * 2 * pad, width)
    outputs, d_mixed, d_low, d_att, d_logits, sums = call(
        combine_kernel,
        [
            ((rows, width), BF),
            ((rows, width), F32),
            ((rows, width), BF),
            ((n_dp, rows, part), BF),
            ((rows, 128), BF),
            ((8, width), F32),
        ],
        back, route, rank, mixed, p, cotangent[0], qkv, vectors, proj,
        pad=pad, capacity=capacity, experts=experts, part=part,
    )
    d_heads = swap(d_att, "dp")
    half = n_ex // 2
    near, keep = call(
        proj_grad_kernel,
        [((half, n_dp, own, width), BF), ((half, n_dp, own, width), F32)],
        attended, d_low,
        scratch=[pltpu.VMEM((width, width), F32)],
    )
    d_heads, *parts = lax.optimization_barrier((d_heads, *core_sum(near, keep)))
    proj_chips = to_chips(parts)
    d_packed, d_normed = call(
        attend_back_kernel,
        [((length, 3 * part), BF), ((n_dp, rows, width), BF)],
        d_heads, probs, packed, qkv,
        scratch=[pltpu.VMEM((length, length), BF)],
        head_dim=head_dim,
    )
    d_packed, *proj_chips = lax.optimization_barrier((d_packed, *proj_chips))
    near, keep = call(
        qkv_grad_kernel,
        [((half, n_dp, own, cols), BF), ((half, n_dp, own, cols), F32)],
        normed1, unit1, d_packed, d_normed, normed2, d_logits, sums,
        scratch=[pltpu.VMEM((width, cols), F32), pltpu.VMEM((128, width), F32)],
        experts=experts,
    )
    near, d_normed = lax.optimization_barrier((near, d_normed))
    d_own = swap(d_normed, "dp")
    qkv_chips = to_chips(core_sum(near, keep))
    d_own, *qkv_chips = lax.optimization_barrier((d_own, *qkv_chips))
    summed = call(
        chip_sum_kernel, [((n_dp, own, cols + width), BF)], *qkv_chips, *proj_chips
    )[0]
    owned_qkv, owned_proj, owned_router, owned_gains, owned_biases = call(
        weights_end_kernel,
        [
            ((own, 3 * width), F32),
            ((own, width), F32),
            ((experts, own), F32),
            ((2, own), F32),
            ((5, own), F32),
        ],
        swap(summed, "dp"),
        scratch=[pltpu.VMEM((128, 128), F32)],
    )
    grad_tokens = call(tokens_end_kernel, [((rows, width), F32)], d_own, x, vectors, d_mixed)[0]
    return (
        outputs[None],
        grad_tokens[None],
        owned_qkv,
        owned_proj,
        owned_router.T,
        owned_gains,
        owned_biases,
        grad_up[None],
        grad_up_bias,
        grad_down[None],
        grad_down_bias,
    )


def solution(mesh):
    line = P(("dp", "expert"), None)
    across = P(None, ("dp", "expert"))
    act = P("expert", "dp", None)
    return jax.shard_map(
        shards,
        mesh=mesh,
        in_specs=(
            act,
            line,
            line,
            line,
            across,
            across,
            P("expert", None, "dp"),
            P("expert", "dp"),
            act,
            P("expert", "dp"),
            act,
            act,
            P("expert", None),
            P("expert", None),
            act,
        ),
        out_specs=(
            act,
            act,
            line,
            line,
            line,
            across,
            across,
            P("expert", None, "dp"),
            P("expert", "dp"),
            act,
            P("expert", "dp"),
        ),
        check_vma=False,
    )
```

```python
import functools

import jax
import jax.numpy as jnp
import numpy as np
from jax import lax
from jax.experimental import pallas as pl
from jax.experimental.pallas import tpu as pltpu
from jax.sharding import PartitionSpec as P

H = 16
NSEG = 7
EPS = 1e-05
NEG = -1e30
BF = jnp.bfloat16
F32 = jnp.float32
I32 = jnp.int32


def mm(a, b, ca=1, cb=0):
    return lax.dot_general(a, b, (((ca,), (cb,)), ((), ())), preferred_element_type=F32)


def placed(kernel):
    def body(*refs):
        kernel((lax.axis_index("dp"), lax.axis_index("expert")), *refs)

    return body


PARAMS = pltpu.CompilerParams(vmem_limit_bytes=24 << 20)


def far(*arrays):
    return [pltpu.with_memory_space_constraint(x, pltpu.HBM) for x in arrays]


def call(kernel, outs, *args, scratch=(), **static):
    vmem = pl.BlockSpec(memory_space=pltpu.VMEM)
    return pl.pallas_call(
        placed(functools.partial(kernel, **static)),
        out_shape=[o if isinstance(o, pl.MemoryRef) else jax.ShapeDtypeStruct(*o) for o in outs],
        in_specs=[vmem] * len(args),
        out_specs=[vmem] * len(outs),
        scratch_shapes=list(scratch),
        compiler_params=PARAMS,
        name=kernel.__name__,
    )(*args)


def ahead(x, step):
    n = lax.axis_size("dp")
    return lax.ppermute(x, "dp", [(i, (i + step) % n) for i in range(n)])


def flip(x, bits):
    n = lax.axis_size("expert")
    return lax.ppermute(x, "expert", [(i, i ^ bits) for i in range(n)])


def swap(x, axis):
    return lax.all_to_all(x, axis, split_axis=0, concat_axis=0, tiled=True)


def along(blocks, sign=1):
    return [blocks[0]] + [ahead(blocks[j], sign * j) for j in range(1, len(blocks))]


def across(x, bits):
    n = lax.axis_size("dp")
    return lax.ppermute(x, "dp", [(i, i ^ bits) for i in range(n)])


def spread(x, hold=None):
    n = lax.axis_size("dp")
    out = [[x]] + [[across(x, k)] for k in range(1, n - 1)]
    if n != 4:
        return out + [[across(x, n - 1)]]
    own = lax.ppermute(x, "dp", [(1, 2), (2, 1)])
    if hold is not None:
        out[2] = [hold(out[2][0])]
    return out + [[own, lax.ppermute(out[2][0], "dp", [(1, 0), (2, 3)])]]


def added(refs):
    return refs[0][...] if len(refs) == 1 else refs[0][...] + refs[1][...]


def split(refs, counts):
    out, at = [], 0
    for count in counts:
        out.append(refs[at : at + count])
        at += count
    return out


def gather_experts(x):
    n = lax.axis_size("expert")
    mine = [x] + [flip(x, 2 * k) for k in range(1, n // 2)]
    out = []
    for block in mine:
        out += [block, flip(block, 1)]
    return out


def normalise(values):
    mean = jnp.mean(values, axis=-1, keepdims=True)
    centred = values - mean
    scale = lax.rsqrt(jnp.mean(centred * centred, axis=-1, keepdims=True) + EPS)
    return centred * scale, scale


def norm_back(upstream, gain, unit, scale):
    e = upstream * gain
    return scale * (
        e - jnp.mean(e, axis=-1, keepdims=True) - unit * jnp.mean(e * unit, axis=-1, keepdims=True)
    )


def lanes(shape, dim):
    return lax.broadcasted_iota(I32, shape, dim)


def softmax_of(logits, experts):
    logits = jnp.where(lanes(logits.shape, 1) < experts, logits, NEG)
    top = jnp.max(logits, axis=-1, keepdims=True)
    weight = jnp.exp(logits - top)
    return weight / jnp.sum(weight, axis=-1, keepdims=True)


def weights_kernel(me, qkv, router, gains, biases, out, turned, *, n_dp):
    own, width = qkv.shape[0], qkv.shape[1] // 3
    part = width // n_dp
    experts = router.shape[0]
    turned[...] = jnp.zeros_like(turned)
    turned[:experts, :own] = router[...].astype(F32)
    turned[experts : experts + 2, :own] = gains[...].astype(F32)
    turned[experts + 2 : experts + 7, :own] = biases[...].astype(F32)
    small = turned[...].T[:own].astype(BF)
    for d in range(n_dp):
        for i in range(3):
            out[d, :, i * part : (i + 1) * part] = qkv[
                :, i * width + d * part : i * width + (d + 1) * part
            ]
        out[d, :, 3 * part :] = small


def slots_kernel(
    me, parents, route, order, cotangent, seg, grads, tableT, route_out, rank_out, bias, *, pad, capacity, experts
):
    tok = route.shape[1]
    rt = jnp.broadcast_to(route[...].astype(F32), (tok, tok))
    r = rt.T
    route_out[...] = r[:, 0:1].astype(I32)
    o = jnp.broadcast_to(order[...].astype(F32), (tok, tok))
    ot = o.T
    same = r == rt
    rank = jnp.sum(jnp.where(same & (o < ot), 1.0, 0.0), axis=1, keepdims=True)
    rank_row = jnp.sum(jnp.where(same & (ot < o), 1.0, 0.0), axis=0, keepdims=True)
    rank_out[...] = rank.astype(I32)
    key = jnp.where(rank_row < capacity, rt[0:1] * pad + rank_row, -1.0).astype(I32)
    table = jnp.where(lanes((experts * pad, tok), 0) == key, 1.0, 0.0).astype(BF)
    tableT[...] = table
    grads[...] = mm(table, cotangent[...]).astype(BF)
    length = seg.shape[1]
    masks = [jnp.int32(1)]
    for s in range(1, NSEG):
        up = jnp.int32(0)
        for a in range(s):
            up = jnp.where(parents[0, s] == a, masks[a], up)
        masks.append(up | (1 << s))
    block = 128
    mine = jnp.zeros((1, length), I32)
    for s in range(NSEG):
        mine = jnp.where(seg[...] == s, masks[s], mine)
    for i in range(length // block):
        col = jnp.broadcast_to(seg[:, i * block : (i + 1) * block].astype(F32), (block, block)).T
        bit = jnp.left_shift(1, jnp.broadcast_to(col[:, 0:1], (block, length)).astype(I32))
        seen = lanes((block, length), 0) + i * block <= lanes((block, length), 1)
        bias[i * block : (i + 1) * block] = jnp.where(seen & ((mine & bit) != 0), 0.0, NEG).astype(BF)


def pack_kernel(me, pick, rows, out):
    out[...] = mm(pick[...], rows[...]).astype(BF)


def pack_picks(n_ex, pad, capacity):
    pick = np.zeros((n_ex * capacity, n_ex * pad), np.float32)
    for e in range(n_ex):
        for c in range(capacity):
            pick[e * capacity + c, e * pad + c] = 1
    return jnp.asarray(pick, BF)


def line_picks(n_ex, pair, capacity):
    pick = np.zeros((n_ex * pair, 2 * n_ex * capacity), np.float32)
    for e in range(n_ex):
        for w in range(2):
            for c in range(capacity):
                pick[e * pair + w * capacity + c, (w * n_ex + e) * capacity + c] = 1
    return jnp.asarray(pick, BF)


def assemble_kernel(me, *refs):
    out = refs[-1]
    for k, block in enumerate(refs[:-1]):
        e = me[1] ^ k
        for d in range(block.shape[0]):
            out[d, e] = block[d]


def assembled(me, blocks, whole):
    own = blocks[0].shape[1]
    n_ex = len(blocks)
    for k, block in enumerate(blocks):
        for d in range(block.shape[0]):
            row = pl.multiple_of((d * n_ex + (me[1] ^ k)) * own, own)
            whole[pl.ds(row, own)] = block[d]


def attend_kernel(me, bias, *refs, counts, n_ex, head_dim, experts):
    blocks, refs = refs[:n_ex], refs[n_ex:]
    tokens, (normed, packed, probs, attended, vectors, small, qkv) = split(refs, counts), refs[-7:]
    n_dp = len(counts)
    rows, width = tokens[0][0].shape
    part = width // n_dp
    assembled(me, blocks, qkv)
    few = qkv[:, 3 * part :]
    small[...] = few
    vectors[...] = few.astype(F32).T[experts : experts + 8]
    gain, shift = vectors[0:1], vectors[2:3]
    parts = [jnp.zeros((1, part), F32)] * 2
    for d in range(n_dp):
        for i in range(2):
            here = vectors[3 + i : 4 + i, d * part : (d + 1) * part]
            parts[i] = parts[i] + jnp.where(me[0] == d, here, 0.0)

    for k, blocks in enumerate(tokens):
        base = pl.multiple_of((me[0] ^ k) * rows, rows)
        unit, _ = normalise(added(blocks).astype(F32))
        normed[pl.ds(base, rows)] = (unit * gain + shift).astype(BF)

    raw = mm(normed[...], qkv[:, : 3 * part])
    packed[:, :part] = (raw[:, :part] + parts[0]).astype(BF)
    packed[:, part : 2 * part] = raw[:, part : 2 * part].astype(BF)
    packed[:, 2 * part :] = (raw[:, 2 * part :] + parts[1]).astype(BF)
    scale = head_dim ** (-0.5)
    for h in range(part // head_dim):
        q = packed[:, h * head_dim : (h + 1) * head_dim]
        k = packed[:, part + h * head_dim : part + (h + 1) * head_dim]
        vt = packed[:, 2 * part + h * head_dim : 2 * part + (h + 1) * head_dim].T
        for i in range(n_dp):
            lo, hi = i * rows, (i + 1) * rows
            s = mm(k[:hi], q[lo:hi], 1, 1) * scale + bias[:hi, lo:hi].astype(F32)
            p = jnp.exp(s - jnp.max(s, axis=0, keepdims=True))
            p = (p * (1.0 / jnp.sum(p, axis=0, keepdims=True))).astype(BF)
            probs[h, :hi, lo:hi] = p
            attended[i, :, h * head_dim : (h + 1) * head_dim] = mm(vt[:, :hi], p).T.astype(BF)


def mix_kernel(me, tokens, attended, proj, small, vectors, tableT, mixed, normed, p, sent, *, experts):
    n_dp, rows, part = attended.shape
    total = tokens[...].astype(F32) + vectors[5:6]
    for d in range(n_dp):
        total = total + mm(attended[d], proj[d * part : (d + 1) * part])
    mixed[...] = total
    unit, _ = normalise(total)
    low = (unit * vectors[1:2] + vectors[6:7]).astype(BF)
    normed[...] = low
    p[...] = softmax_of(mm(low, small[...]), experts)
    sent[...] = mm(tableT[...], low).astype(BF)


def expert_kernel(
    me, small, up, down, up_bias, down_bias, *refs, counts, n_dp, experts
):
    came, grads, (both, slots, act_out, d_pre_out, d_rows, g_up_bias, acc_r, acc_s) = split(refs, [*counts, 8])
    f = pl.program_id(0)
    each, width = slots.shape
    part = width // n_dp

    @pl.when(f == 0)
    def _():
        slots[...] = added(came)
        p = softmax_of(mm(slots[...], small[...]), experts)
        gate = jnp.sum(jnp.where(lanes(p.shape, 1) == me[1], p, 0.0), axis=-1, keepdims=True)
        d_rows[...] = (gate * added(grads).astype(F32)).astype(BF)
        acc_s[...] = jnp.zeros_like(acc_s)
        for d in range(n_dp):
            acc_r[:, d * part : (d + 1) * part] = jnp.broadcast_to(
                jnp.where(me[0] == d, down_bias[...].astype(F32), 0.0), (each, part)
            )

    u = mm(slots[...], up[...]) + up_bias[...].astype(F32)
    c, a = 0.7978845608028654, 0.044715
    t = jnp.tanh(c * (u + a * (u * u * u)))
    act = (0.5 * u * (1.0 + t)).astype(BF)
    slope = 0.5 * (1.0 + t) + 0.5 * u * (1.0 - t * t) * (c * (1.0 + 3.0 * a * (u * u)))
    d_pre = mm(d_rows[...], down[...], 1, 1) * slope
    g_up_bias[...] = jnp.sum(d_pre, axis=0, keepdims=True)
    low = d_pre.astype(BF)
    act_out[...] = act
    d_pre_out[...] = low
    acc_r[...] += mm(act, down[...])
    acc_s[...] += mm(low, up[...], 1, 1)

    @pl.when(f == pl.num_programs(0) - 1)
    def _():
        both[:each] = acc_r[...].astype(BF)
        both[each:] = acc_s[...].astype(BF)


def expert_call(small, up, down, up_bias, down_bias, slots, grads, n_dp, experts):
    each, width = slots[0].shape
    ff = up.shape[1]
    chunk = min(ff, 256)
    whole = pl.BlockSpec(memory_space=pltpu.VMEM)
    wide = pl.BlockSpec((each, chunk), lambda f: (0, f))
    row = pl.BlockSpec((1, chunk), lambda f: (0, f))
    return pl.pallas_call(
        placed(
            functools.partial(
                expert_kernel, counts=(len(slots), len(grads)), n_dp=n_dp, experts=experts
            )
        ),
        grid=(ff // chunk,),
        out_shape=[
            pltpu.HBM((2 * each, width), BF),
            jax.ShapeDtypeStruct((each, width), BF),
            jax.ShapeDtypeStruct((each, ff), BF),
            jax.ShapeDtypeStruct((each, ff), BF),
            jax.ShapeDtypeStruct((each, width), BF),
            jax.ShapeDtypeStruct((1, ff), F32),
        ],
        in_specs=[
            whole,
            pl.BlockSpec((width, chunk), lambda f: (0, f)),
            pl.BlockSpec((chunk, width), lambda f: (f, 0)),
            row,
            whole,
        ]
        + [whole] * (len(slots) + len(grads)),
        out_specs=[whole, whole, wide, wide, whole, row],
        scratch_shapes=[pltpu.VMEM((each, width), F32), pltpu.VMEM((each, width), F32)],
        compiler_params=PARAMS,
        name="expert_kernel",
    )(small, up, down, up_bias, down_bias, *slots, *grads)


def expert_grad_kernel(me, *refs, n_dp):
    slots, act, d_pre, d_rows, up_bias = (refs[i * n_dp : (i + 1) * n_dp] for i in range(5))
    grad_up, grad_down, g_up_bias, g_down_bias = refs[5 * n_dp :]
    grad_up[...] = sum(mm(a[...], b[...], 0, 0) for a, b in zip(slots, d_pre))
    grad_down[...] = sum(mm(a[...], b[...], 0, 0) for a, b in zip(act, d_rows))

    @pl.when(pl.program_id(0) == 0)
    def _():
        g_up_bias[...] = sum_of(up_bias)
        sums = sum(jnp.sum(r[...].astype(F32), axis=0, keepdims=True) for r in d_rows)
        part = g_down_bias.shape[1]
        own = jnp.zeros((1, part), F32)
        for d in range(n_dp):
            own = own + jnp.where(me[0] == d, sums[:, d * part : (d + 1) * part], 0.0)
        g_down_bias[...] = own


def expert_grads(slots, act, d_pre, d_rows, up_bias, part):
    n_dp = len(slots)
    each, width = slots[0].shape
    ff = act[0].shape[1]
    steps = 4
    whole = pl.BlockSpec(memory_space=pltpu.VMEM)
    return pl.pallas_call(
        placed(functools.partial(expert_grad_kernel, n_dp=n_dp)),
        grid=(steps,),
        out_shape=[
            pltpu.HBM((width, ff), F32),
            pltpu.HBM((ff, width), F32),
            jax.ShapeDtypeStruct((1, ff), F32),
            jax.ShapeDtypeStruct((1, part), F32),
        ],
        in_specs=[pl.BlockSpec((each, width // steps), lambda f: (0, f))] * n_dp
        + [pl.BlockSpec((each, ff // steps), lambda f: (0, f))] * n_dp
        + [whole] * (3 * n_dp),
        out_specs=[
            pl.BlockSpec((width // steps, ff), lambda f: (f, 0)),
            pl.BlockSpec((ff // steps, width), lambda f: (f, 0)),
            whole,
            whole,
        ],
        compiler_params=PARAMS,
        name="expert_grad_kernel",
    )(*slots, *act, *d_pre, *d_rows, *up_bias)


def sum_of(refs):
    total = refs[0][...].astype(F32)
    for ref in refs[1:]:
        total = total + ref[...].astype(F32)
    return total


def line_sum_kernel(me, pick, *refs):
    refs[-1][...] = mm(pick[...], sum_of(refs[:-1]).astype(BF)).astype(BF)


def combine_kernel(
    me, back, route, rank, mixed, p, cotangent, small, vectors, proj,
    outputs, d_mixed, d_low_out, d_att, d_logits_out, sums, *, pair, capacity, experts, part,
):
    tok, width = mixed.shape
    n_back = back.shape[0]
    r, k = route[...], rank[...]
    key = jnp.where(k < capacity, r * pair + k, -2 * pair * experts)
    slot = lanes((tok, n_back), 1)
    combined = mm(jnp.where(slot == key, 1.0, 0.0).astype(BF), back[...])
    d_slot = mm(jnp.where(slot == key + capacity, 1.0, 0.0).astype(BF), back[...])
    hot = jnp.where(lanes(p.shape, 1) == r, 1.0, 0.0)
    gate = jnp.sum(p[...] * hot, axis=-1, keepdims=True)
    g = cotangent[...].astype(F32)
    outputs[...] = (mixed[...] + gate * combined).astype(BF)
    d_gate = jnp.sum(g * combined, axis=-1, keepdims=True)
    d_logits = (p[...] * (d_gate * hot - d_gate * gate)).astype(BF)
    d_logits_out[...] = d_logits
    d_normed = d_slot + mm(d_logits, small[...], 1, 1)
    unit, scale = normalise(mixed[...])
    sums[0:1] = jnp.sum(d_normed * unit, axis=0, keepdims=True)
    sums[1:2] = jnp.sum(d_normed, axis=0, keepdims=True)
    d = g + norm_back(d_normed, vectors[1:2], unit, scale)
    sums[2:3] = jnp.sum(d, axis=0, keepdims=True)
    d_mixed[...] = d
    low = d.astype(BF)
    d_low_out[...] = low
    for i in range(d_att.shape[0]):
        d_att[i] = mm(low, proj[i * part : (i + 1) * part], 1, 1).astype(BF)


def share(me, whole, near, keep):
    half, n_dp, own, _ = near.shape
    for q in range(half):
        for d in range(n_dp):
            row = d * 2 * half * own
            other = pl.multiple_of(row + (me[1] ^ (2 * q + 1)) * own, own)
            same = pl.multiple_of(row + (me[1] ^ (2 * q)) * own, own)
            near[q, d] = whole[pl.ds(other, own)].astype(BF)
            keep[q, d] = whole[pl.ds(same, own)].astype(BF)


def proj_grad_kernel(me, attended, d_low, near, keep, whole):
    n_dp, rows, part = attended.shape
    for d in range(n_dp):
        whole[d * part : (d + 1) * part] = mm(attended[d], d_low[...], 0, 0)
    share(me, whole, near, keep)


def core_sum_kernel(me, keep, came, first, *rest):
    for q, out in enumerate([first, *rest]):
        out[...] = (keep[q].astype(F32) + came[q].astype(F32)).astype(BF)


def chip_sum_kernel(me, *refs, n_dp):
    outs, total = refs[-1 - n_dp : -1], refs[-1]
    parts = refs[: -1 - n_dp]
    half = len(parts) // 2
    wide = parts[0].shape[2]
    total[:, :, :wide] = sum_of(parts[:half]).astype(BF)
    total[:, :, wide:] = sum_of(parts[half:]).astype(BF)
    for j in range(n_dp):
        outs[j][...] = total[(me[0] + j) % n_dp]


def core_sum(near, keep):
    half = near.shape[0]
    shape = near.shape[1:]
    return call(core_sum_kernel, [(shape, BF)] + [pltpu.HBM(shape, BF)] * (half - 1), keep, flip(near, 1))


def to_chips(parts):
    return [parts[0]] + [flip(part, 2 * (q + 1)) for q, part in enumerate(parts[1:])]


def attend_back_kernel(me, d_att, probs, packed, *refs, head_dim):
    blocks, (d_packed, d_normed, d_scores, qkv) = refs[:-4], refs[-4:]
    n_dp, rows, part = d_att.shape
    scale = head_dim ** (-0.5)
    assembled(me, blocks, qkv)
    for h in range(part // head_dim):
        a, b = h * head_dim, (h + 1) * head_dim
        q, k, v = packed[:, a:b], packed[:, part + a : part + b], packed[:, 2 * part + a : 2 * part + b]
        kt = k.T
        g = jnp.concatenate([d_att[i, :, a:b] for i in range(n_dp)], axis=0)
        for i in range(n_dp):
            lo, hi = i * rows, (i + 1) * rows
            dp = mm(v[:hi], g[lo:hi], 1, 1)
            p = probs[h, :hi, lo:hi].astype(F32)
            delta = jnp.sum(p * dp, axis=0, keepdims=True)
            ds = (p * (dp - delta)).astype(BF)
            d_scores[:hi, lo:hi] = ds
            d_packed[lo:hi, a:b] = (mm(kt[:, :hi], ds).T * scale).astype(BF)
        for i in range(n_dp):
            lo, hi = i * rows, (i + 1) * rows
            d_packed[lo:hi, part + a : part + b] = (mm(d_scores[lo:hi, lo:], q[lo:]) * scale).astype(BF)
            d_packed[lo:hi, 2 * part + a : 2 * part + b] = mm(probs[h, lo:hi, lo:], g[lo:]).astype(BF)
    for i in range(n_dp):
        d_normed[i] = mm(d_packed[i * rows : (i + 1) * rows], qkv[:, : 3 * part], 1, 1).astype(BF)


def qkv_grad_kernel(
    me, normed, vectors, d_packed, d_normed, token_normed, d_logits, sums, near, keep, whole, turned, *, experts
):
    n_dp, rows, width = d_normed.shape
    part = width // n_dp
    whole[:, : 3 * part] = mm(normed[...], d_packed[...], 0, 0)
    gain = jnp.zeros((1, width), F32)
    shift = jnp.zeros((1, width), F32)
    for i in range(n_dp):
        d = d_normed[i].astype(F32)
        gain = gain + jnp.sum(d * normed[i * rows : (i + 1) * rows].astype(F32), axis=0, keepdims=True)
        shift = shift + jnp.sum(d, axis=0, keepdims=True)
    gain = (gain - vectors[2:3] * shift) / vectors[0:1]
    columns = jnp.sum(d_packed[...].astype(F32), axis=0, keepdims=True)
    turned[...] = jnp.zeros_like(turned)
    e = experts
    turned[e : e + 1] = gain
    turned[e + 1 : e + 2] = sums[0:1]
    turned[e + 2 : e + 3] = shift
    for d in range(n_dp):
        here = me[0] == d
        turned[e + 3 : e + 4, d * part : (d + 1) * part] = jnp.where(here, columns[:, :part], 0.0)
        turned[e + 4 : e + 5, d * part : (d + 1) * part] = jnp.where(here, columns[:, 2 * part :], 0.0)
    turned[e + 5 : e + 6] = sums[2:3]
    turned[e + 6 : e + 7] = sums[1:2]
    whole[:, 3 * part :] = turned[...].T + mm(token_normed[...], d_logits[...], 0, 0)
    share(me, whole, near, keep)


def weights_end_kernel(me, *refs):
    (qkv, proj, router, gains, biases, wide, came), blocks = refs[-7:], refs[:-7]
    n_dp, own, _ = came.shape
    for j in range(n_dp):
        came[(me[0] + n_dp - j) % n_dp] = blocks[j][...]
    width = proj.shape[1]
    part = width // n_dp
    experts = router.shape[0]
    edge = 3 * part
    total = jnp.zeros((own, 128), F32)
    rows = jnp.zeros((own, width), F32)
    for d in range(n_dp):
        for i in range(3):
            qkv[:, i * width + d * part : i * width + (d + 1) * part] = came[
                d, :, i * part : (i + 1) * part
            ].astype(F32)
        total = total + came[d, :, edge : edge + 128].astype(F32)
        rows = rows + came[d, :, edge + 128 :].astype(F32)
    proj[...] = rows
    wide[...] = jnp.zeros_like(wide)
    wide[:own] = total
    flat = wide[...].T
    router[...] = flat[:experts, :own]
    gains[...] = flat[experts : experts + 2, :own]
    biases[...] = flat[experts + 2 : experts + 7, :own]


def tokens_end_kernel(me, came, tokens, vectors, d_mixed, out):
    total = came[0].astype(F32)
    for d in range(1, came.shape[0]):
        total = total + came[d].astype(F32)
    unit, scale = normalise(tokens[...].astype(F32))
    out[...] = d_mixed[...] + norm_back(total, vectors[0:1], unit, scale)


def shards(
    tokens,
    qkv_weight,
    proj_weight,
    router_weight,
    norm_gains,
    biases,
    up_weight,
    up_bias,
    down_weight,
    down_bias,
    routes,
    slot_order,
    segments,
    parents,
    cotangent,
):
    n_dp, n_ex = lax.axis_size("dp"), lax.axis_size("expert")
    rows, width = tokens.shape[1], tokens.shape[2]
    part = width // n_dp
    head_dim = width // H
    own = qkv_weight.shape[0]
    experts = router_weight.shape[1]
    capacity = (9 * rows + 8 * experts - 1) // (8 * experts)
    pad = -(-capacity // 8) * 8
    pair = -(-capacity // 4) * 8
    length = n_dp * rows
    each = n_ex * capacity
    cols = 3 * part + 128
    x = tokens[0]

    token_blocks = spread(x)
    columns = call(
        weights_kernel,
        [pltpu.HBM((n_dp, own, cols), BF)],
        *far(qkv_weight, router_weight.T, norm_gains, biases),
        scratch=[pltpu.VMEM((128, 128), F32)],
        n_dp=n_dp,
    )[0]
    qkv_blocks = gather_experts(swap(columns, "dp"))
    smem = pl.BlockSpec(memory_space=pltpu.SMEM)
    vmem = pl.BlockSpec(memory_space=pltpu.VMEM)
    grads_out, tableT, route, rank, bias = pl.pallas_call(
        placed(functools.partial(slots_kernel, pad=pad, capacity=capacity, experts=experts)),
        out_shape=[
            pltpu.HBM((n_ex * pad, width), BF),
            pltpu.HBM((n_ex * pad, rows), BF),
            pltpu.HBM((rows, 1), I32),
            pltpu.HBM((rows, 1), I32),
            jax.ShapeDtypeStruct((length, length), BF),
        ],
        in_specs=[smem] + [vmem] * 4,
        out_specs=[vmem] * 5,
        compiler_params=PARAMS,
        name="slots_kernel",
    )(parents, *far(routes.reshape(1, rows), slot_order[0], cotangent[0], segments))

    def dispatch(rows_out):
        came = swap(rows_out.reshape(n_ex, pad, width), "expert").reshape(n_ex * pad, width)
        mine = call(pack_kernel, [pltpu.HBM((each, width), BF)], *far(pack_picks(n_ex, pad, capacity)), came)[0]
        return mine

    grads_in = dispatch(grads_out)
    proj_blocks = gather_experts(swap(jnp.broadcast_to(proj_weight, (n_dp, own, width)), "dp"))
    grads_in, bias = lax.optimization_barrier((grads_in, bias))
    grads = spread(grads_in)
    normed1, packed, probs, att_out, vectors, small = call(
        attend_kernel,
        [
            pltpu.HBM((length, width), BF),
            pltpu.HBM((length, 3 * part), BF),
            pltpu.HBM((part // head_dim, length, length), BF),
            pltpu.HBM((n_dp, rows, part), BF),
            ((8, width), F32),
            ((width, 128), BF),
        ],
        bias, *far(*qkv_blocks, *sum(token_blocks, [])),
        scratch=[pltpu.VMEM((width, cols), BF)],
        counts=[len(b) for b in token_blocks], n_ex=n_ex, head_dim=head_dim, experts=experts,
    )
    early = list(range(1, n_dp - 1))
    att_out, *came = lax.optimization_barrier((att_out, *[grads[k][0] for k in early]))
    for k, block in zip(early, came):
        grads[k] = [block]
    attended = swap(att_out, "dp")
    proj = call(assemble_kernel, [((n_dp, n_ex, own, width), BF)], *proj_blocks)[0].reshape(width, width)
    mixed, normed2, p, sent = call(
        mix_kernel,
        [pltpu.HBM((rows, width), F32), pltpu.HBM((rows, width), BF), pltpu.HBM((rows, 128), F32), pltpu.HBM((n_ex * pad, width), BF)],
        *far(x), attended, proj, small, vectors, *far(tableT),
        experts=experts,
    )
    mine = dispatch(sent)
    grads = lax.optimization_barrier(grads)
    def expert(slots, k):
        return expert_call(
            small, up_weight[0], down_weight[0], up_bias, down_bias, slots, grads[k], n_dp, experts
        )

    done = {0: expert([mine], 0)}

    def after_own(block):
        block, done[0] = lax.optimization_barrier((block, done[0]))
        return block

    slots = spread(mine, after_own)
    came = [done[0][0]] + [None] * (n_dp - 1)
    last = 0
    for k in [2, 1, 3] if n_dp == 4 else range(1, n_dp):
        slots[k], done[last] = lax.optimization_barrier((slots[k], done[last]))
        done[k] = expert(slots[k], k)
        came[k] = across(done[k][0], k)
        last = k
    came[0] = done[0][0]
    all_slots, act, d_pre, d_rows, g_up_bias = ([done[k][i] for k in range(n_dp)] for i in range(1, 6))
    grad_up, grad_down, grad_up_bias, grad_down_bias = expert_grads(
        all_slots, act, d_pre, d_rows, g_up_bias, part
    )
    grad_up, grad_down, *came = lax.optimization_barrier((grad_up, grad_down, *came))
    summed = call(line_sum_kernel, [pltpu.HBM((n_ex * pair, width), BF)], *far(line_picks(n_ex, pair, capacity)), *came)[0]
    back = swap(summed.reshape(n_ex, pair, width), "expert").reshape(n_ex * pair, width)
    outputs, d_mixed, d_low, d_att, d_logits, sums = call(
        combine_kernel,
        [
            pltpu.HBM((rows, width), BF),
            pltpu.HBM((rows, width), F32),
            ((rows, width), BF),
            pltpu.HBM((n_dp, rows, part), BF),
            pltpu.HBM((rows, 128), BF),
            pltpu.HBM((8, width), F32),
        ],
        back, *far(route, rank, mixed, p, cotangent[0]), small, vectors, proj,
        pair=pair, capacity=capacity, experts=experts, part=part,
    )
    d_heads = swap(d_att, "dp")
    half = n_ex // 2
    near, keep = call(
        proj_grad_kernel,
        [pltpu.HBM((half, n_dp, own, width), BF), ((half, n_dp, own, width), BF)],
        *far(attended), d_low,
        scratch=[pltpu.VMEM((width, width), F32)],
    )
    d_heads, *parts = lax.optimization_barrier((d_heads, *core_sum(near, keep)))
    proj_chips = to_chips(parts)
    d_packed, d_normed = call(
        attend_back_kernel,
        [((length, 3 * part), BF), pltpu.HBM((n_dp, rows, width), BF)],
        d_heads, *far(probs, packed, *qkv_blocks),
        scratch=[pltpu.VMEM((length, length), BF), pltpu.VMEM((width, cols), BF)],
        head_dim=head_dim,
    )
    d_packed, *proj_chips = lax.optimization_barrier((d_packed, *proj_chips))
    near, keep = call(
        qkv_grad_kernel,
        [pltpu.HBM((half, n_dp, own, cols), BF), ((half, n_dp, own, cols), BF)],
        *far(normed1), vectors, d_packed, *far(d_normed, normed2, d_logits, sums),
        scratch=[pltpu.VMEM((width, cols), F32), pltpu.VMEM((128, width), F32)],
        experts=experts,
    )
    near, d_normed = lax.optimization_barrier((near, d_normed))
    d_own = swap(d_normed, "dp")
    qkv_chips = to_chips(core_sum(near, keep))
    summed = call(
        chip_sum_kernel, [pltpu.HBM((own, cols + width), BF)] * n_dp, *qkv_chips, *proj_chips,
        scratch=[pltpu.VMEM((n_dp, own, cols + width), BF)], n_dp=n_dp,
    )
    d_own, *summed = lax.optimization_barrier((d_own, *summed))
    owned_qkv, owned_proj, owned_router, owned_gains, owned_biases = call(
        weights_end_kernel,
        [
            pltpu.HBM((own, 3 * width), F32),
            pltpu.HBM((own, width), F32),
            pltpu.HBM((experts, own), F32),
            pltpu.HBM((2, own), F32),
            pltpu.HBM((5, own), F32),
        ],
        *along(summed),
        scratch=[pltpu.VMEM((128, 128), F32), pltpu.VMEM((n_dp, own, cols + width), BF)],
    )
    grad_tokens = call(tokens_end_kernel, [pltpu.HBM((rows, width), F32)], d_own, *far(x), vectors, *far(d_mixed))[0]
    return (
        outputs[None],
        grad_tokens[None],
        owned_qkv,
        owned_proj,
        owned_router.T,
        owned_gains,
        owned_biases,
        grad_up[None],
        grad_up_bias,
        grad_down[None],
        grad_down_bias,
    )


def solution(mesh):
    line = P(("dp", "expert"), None)
    across = P(None, ("dp", "expert"))
    act = P("expert", "dp", None)
    return jax.shard_map(
        shards,
        mesh=mesh,
        in_specs=(
            act,
            line,
            line,
            line,
            across,
            across,
            P("expert", None, "dp"),
            P("expert", "dp"),
            act,
            P("expert", "dp"),
            act,
            act,
            P("expert", None),
            P("expert", None),
            act,
        ),
        out_specs=(
            act,
            act,
            line,
            line,
            line,
            across,
            across,
            P("expert", None, "dp"),
            P("expert", "dp"),
            act,
            P("expert", "dp"),
        ),
        check_vma=False,
    )
```

```python
import functools

import jax
import jax.numpy as jnp
import numpy as np
from jax import lax
from jax.experimental import pallas as pl
from jax.experimental.pallas import tpu as pltpu
from jax.sharding import PartitionSpec as P

H = 16
NSEG = 7
EPS = 1e-05
NEG = -1e30
BF = jnp.bfloat16
F32 = jnp.float32
I32 = jnp.int32


def mm(a, b, ca=1, cb=0):
    return lax.dot_general(a, b, (((ca,), (cb,)), ((), ())), preferred_element_type=F32)


def placed(kernel):
    def body(*refs):
        kernel((lax.axis_index("dp"), lax.axis_index("expert")), *refs)

    return body


PARAMS = pltpu.CompilerParams(vmem_limit_bytes=24 << 20)


def far(*arrays):
    return [pltpu.with_memory_space_constraint(x, pltpu.HBM) for x in arrays]


def call(kernel, outs, *args, scratch=(), **static):
    vmem = pl.BlockSpec(memory_space=pltpu.VMEM)
    return pl.pallas_call(
        placed(functools.partial(kernel, **static)),
        out_shape=[o if isinstance(o, pl.MemoryRef) else jax.ShapeDtypeStruct(*o) for o in outs],
        in_specs=[vmem] * len(args),
        out_specs=[vmem] * len(outs),
        scratch_shapes=list(scratch),
        compiler_params=PARAMS,
        name=kernel.__name__,
    )(*args)


def ahead(x, step):
    n = lax.axis_size("dp")
    return lax.ppermute(x, "dp", [(i, (i + step) % n) for i in range(n)])


def flip(x, bits):
    n = lax.axis_size("expert")
    return lax.ppermute(x, "expert", [(i, i ^ bits) for i in range(n)])


def swap(x, axis):
    return lax.all_to_all(x, axis, split_axis=0, concat_axis=0, tiled=True)


def along(blocks, sign=1):
    return [blocks[0]] + [ahead(blocks[j], sign * j) for j in range(1, len(blocks))]


def across(x, bits):
    n = lax.axis_size("dp")
    return lax.ppermute(x, "dp", [(i, i ^ bits) for i in range(n)])


def spread(x, hold=None):
    n = lax.axis_size("dp")
    out = [[x]] + [[across(x, k)] for k in range(1, n - 1)]
    if n != 4:
        return out + [[across(x, n - 1)]]
    own = lax.ppermute(x, "dp", [(1, 2), (2, 1)])
    if hold is not None:
        out[2] = [hold(out[2][0])]
    return out + [[own, lax.ppermute(out[2][0], "dp", [(1, 0), (2, 3)])]]


def added(refs):
    return refs[0][...] if len(refs) == 1 else refs[0][...] + refs[1][...]


def split(refs, counts):
    out, at = [], 0
    for count in counts:
        out.append(refs[at : at + count])
        at += count
    return out


def gather_experts(x):
    n = lax.axis_size("expert")
    mine = [x] + [flip(x, 2 * k) for k in range(1, n // 2)]
    out = []
    for block in mine:
        out += [block, flip(block, 1)]
    return out


def normalise(values):
    mean = jnp.mean(values, axis=-1, keepdims=True)
    centred = values - mean
    scale = lax.rsqrt(jnp.mean(centred * centred, axis=-1, keepdims=True) + EPS)
    return centred * scale, scale


def norm_back(upstream, gain, unit, scale):
    e = upstream * gain
    return scale * (
        e - jnp.mean(e, axis=-1, keepdims=True) - unit * jnp.mean(e * unit, axis=-1, keepdims=True)
    )


def lanes(shape, dim):
    return lax.broadcasted_iota(I32, shape, dim)


def softmax_of(logits, experts):
    logits = jnp.where(lanes(logits.shape, 1) < experts, logits, NEG)
    top = jnp.max(logits, axis=-1, keepdims=True)
    weight = jnp.exp(logits - top)
    return weight / jnp.sum(weight, axis=-1, keepdims=True)


def weights_kernel(me, qkv, router, gains, biases, out, turned, *, n_dp):
    own, width = qkv.shape[0], qkv.shape[1] // 3
    part = width // n_dp
    experts = router.shape[0]
    turned[...] = jnp.zeros_like(turned)
    turned[:experts, :own] = router[...].astype(F32)
    turned[experts : experts + 2, :own] = gains[...].astype(F32)
    turned[experts + 2 : experts + 7, :own] = biases[...].astype(F32)
    small = turned[...].T[:own].astype(BF)
    for d in range(n_dp):
        for i in range(3):
            out[d, :, i * part : (i + 1) * part] = qkv[
                :, i * width + d * part : i * width + (d + 1) * part
            ]
        out[d, :, 3 * part :] = small


def slots_kernel(
    me, parents, route, order, cotangent, seg, grads, tableT, route_out, rank_out, bias, *, pad, capacity, experts
):
    tok = route.shape[1]
    rt = jnp.broadcast_to(route[...].astype(F32), (tok, tok))
    r = rt.T
    route_out[...] = r[:, 0:1].astype(I32)
    o = jnp.broadcast_to(order[...].astype(F32), (tok, tok))
    ot = o.T
    same = r == rt
    rank = jnp.sum(jnp.where(same & (o < ot), 1.0, 0.0), axis=1, keepdims=True)
    rank_row = jnp.sum(jnp.where(same & (ot < o), 1.0, 0.0), axis=0, keepdims=True)
    rank_out[...] = rank.astype(I32)
    key = jnp.where(rank_row < capacity, rt[0:1] * pad + rank_row, -1.0).astype(I32)
    table = jnp.where(lanes((experts * pad, tok), 0) == key, 1.0, 0.0).astype(BF)
    tableT[...] = table
    grads[...] = mm(table, cotangent[...]).astype(BF)
    length = seg.shape[1]
    masks = [jnp.int32(1)]
    for s in range(1, NSEG):
        up = jnp.int32(0)
        for a in range(s):
            up = jnp.where(parents[0, s] == a, masks[a], up)
        masks.append(up | (1 << s))
    block = 128
    mine = jnp.zeros((1, length), I32)
    for s in range(NSEG):
        mine = jnp.where(seg[...] == s, masks[s], mine)
    for i in range(length // block):
        col = jnp.broadcast_to(seg[:, i * block : (i + 1) * block].astype(F32), (block, block)).T
        bit = jnp.left_shift(1, jnp.broadcast_to(col[:, 0:1], (block, length)).astype(I32))
        seen = lanes((block, length), 0) + i * block <= lanes((block, length), 1)
        bias[i * block : (i + 1) * block] = jnp.where(seen & ((mine & bit) != 0), 0.0, NEG).astype(BF)


def pack_kernel(me, pick, rows, out):
    out[...] = mm(pick[...], rows[...]).astype(BF)


def pack_picks(n_ex, pad, capacity):
    pick = np.zeros((n_ex * capacity, n_ex * pad), np.float32)
    for e in range(n_ex):
        for c in range(capacity):
            pick[e * capacity + c, e * pad + c] = 1
    return jnp.asarray(pick, BF)


def line_picks(n_ex, pair, capacity):
    pick = np.zeros((n_ex * pair, 2 * n_ex * capacity), np.float32)
    for e in range(n_ex):
        for w in range(2):
            for c in range(capacity):
                pick[e * pair + w * capacity + c, (w * n_ex + e) * capacity + c] = 1
    return jnp.asarray(pick, BF)


def assemble_kernel(me, *refs):
    out = refs[-1]
    for k, block in enumerate(refs[:-1]):
        e = me[1] ^ k
        for d in range(block.shape[0]):
            out[d, e] = block[d]


def assembled(me, blocks, whole):
    own = blocks[0].shape[1]
    n_ex = len(blocks)
    for k, block in enumerate(blocks):
        for d in range(block.shape[0]):
            row = pl.multiple_of((d * n_ex + (me[1] ^ k)) * own, own)
            whole[pl.ds(row, own)] = block[d]


def attend_kernel(me, bias, *refs, counts, n_ex, head_dim, experts):
    blocks, refs = refs[:n_ex], refs[n_ex:]
    tokens, (normed, packed, probs, attended, vectors, small, qkv) = split(refs, counts), refs[-7:]
    n_dp = len(counts)
    rows, width = tokens[0][0].shape
    part = width // n_dp
    assembled(me, blocks, qkv)
    few = qkv[:, 3 * part :]
    small[...] = few
    vectors[...] = few.astype(F32).T[experts : experts + 8]
    gain, shift = vectors[0:1], vectors[2:3]
    parts = [jnp.zeros((1, part), F32)] * 2
    for d in range(n_dp):
        for i in range(2):
            here = vectors[3 + i : 4 + i, d * part : (d + 1) * part]
            parts[i] = parts[i] + jnp.where(me[0] == d, here, 0.0)

    for k, blocks in enumerate(tokens):
        base = pl.multiple_of((me[0] ^ k) * rows, rows)
        unit, _ = normalise(added(blocks).astype(F32))
        normed[pl.ds(base, rows)] = (unit * gain + shift).astype(BF)

    raw = mm(normed[...], qkv[:, : 3 * part])
    packed[:, :part] = (raw[:, :part] + parts[0]).astype(BF)
    packed[:, part : 2 * part] = raw[:, part : 2 * part].astype(BF)
    packed[:, 2 * part :] = (raw[:, 2 * part :] + parts[1]).astype(BF)
    scale = head_dim ** (-0.5)
    for h in range(part // head_dim):
        q = packed[:, h * head_dim : (h + 1) * head_dim]
        k = packed[:, part + h * head_dim : part + (h + 1) * head_dim]
        vt = packed[:, 2 * part + h * head_dim : 2 * part + (h + 1) * head_dim].T
        for i in range(0, n_dp, 2):
            lo, hi = i * rows, (i + 2) * rows
            s = mm(k[:hi], q[lo:hi], 1, 1) * scale + bias[:hi, lo:hi].astype(F32)
            p = jnp.exp(s - jnp.max(s, axis=0, keepdims=True))
            p = (p * (1.0 / jnp.sum(p, axis=0, keepdims=True))).astype(BF)
            probs[h, :hi, lo:hi] = p
            out = mm(vt[:, :hi], p).T.astype(BF)
            attended[i, :, h * head_dim : (h + 1) * head_dim] = out[:rows]
            attended[i + 1, :, h * head_dim : (h + 1) * head_dim] = out[rows:]


def mix_kernel(me, tokens, attended, proj, small, vectors, tableT, mixed, normed, p, sent, *, experts):
    n_dp, rows, part = attended.shape
    total = tokens[...].astype(F32) + vectors[5:6]
    for d in range(n_dp):
        total = total + mm(attended[d], proj[d * part : (d + 1) * part])
    mixed[...] = total
    unit, _ = normalise(total)
    low = (unit * vectors[1:2] + vectors[6:7]).astype(BF)
    normed[...] = low
    p[...] = softmax_of(mm(low, small[...]), experts)
    sent[...] = mm(tableT[...], low).astype(BF)


def expert_kernel(
    me, small, up, down, up_bias, down_bias, *refs, counts, n_dp, experts
):
    came, grads, (both, slots, act_out, d_pre_out, d_rows, g_up_bias, acc_r, acc_s) = split(refs, [*counts, 8])
    f = pl.program_id(0)
    each, width = slots.shape
    part = width // n_dp

    @pl.when(f == 0)
    def _():
        slots[...] = added(came)
        p = softmax_of(mm(slots[...], small[...]), experts)
        gate = jnp.sum(jnp.where(lanes(p.shape, 1) == me[1], p, 0.0), axis=-1, keepdims=True)
        d_rows[...] = (gate * added(grads).astype(F32)).astype(BF)
        acc_s[...] = jnp.zeros_like(acc_s)
        for d in range(n_dp):
            acc_r[:, d * part : (d + 1) * part] = jnp.broadcast_to(
                jnp.where(me[0] == d, down_bias[...].astype(F32), 0.0), (each, part)
            )

    u = mm(slots[...], up[...]) + up_bias[...].astype(F32)
    c, a = 0.7978845608028654, 0.044715
    t = jnp.tanh(c * (u + a * (u * u * u)))
    act = (0.5 * u * (1.0 + t)).astype(BF)
    slope = 0.5 * (1.0 + t) + 0.5 * u * (1.0 - t * t) * (c * (1.0 + 3.0 * a * (u * u)))
    d_pre = mm(d_rows[...], down[...], 1, 1) * slope
    g_up_bias[...] = jnp.sum(d_pre, axis=0, keepdims=True)
    low = d_pre.astype(BF)
    act_out[...] = act
    d_pre_out[...] = low
    acc_r[...] += mm(act, down[...])
    acc_s[...] += mm(low, up[...], 1, 1)

    @pl.when(f == pl.num_programs(0) - 1)
    def _():
        both[:each] = acc_r[...].astype(BF)
        both[each:] = acc_s[...].astype(BF)


def expert_call(small, up, down, up_bias, down_bias, slots, grads, n_dp, experts):
    each, width = slots[0].shape
    ff = up.shape[1]
    chunk = min(ff, 256)
    whole = pl.BlockSpec(memory_space=pltpu.VMEM)
    wide = pl.BlockSpec((each, chunk), lambda f: (0, f))
    row = pl.BlockSpec((1, chunk), lambda f: (0, f))
    return pl.pallas_call(
        placed(
            functools.partial(
                expert_kernel, counts=(len(slots), len(grads)), n_dp=n_dp, experts=experts
            )
        ),
        grid=(ff // chunk,),
        out_shape=[
            pltpu.HBM((2 * each, width), BF),
            jax.ShapeDtypeStruct((each, width), BF),
            jax.ShapeDtypeStruct((each, ff), BF),
            jax.ShapeDtypeStruct((each, ff), BF),
            jax.ShapeDtypeStruct((each, width), BF),
            jax.ShapeDtypeStruct((1, ff), F32),
        ],
        in_specs=[
            whole,
            pl.BlockSpec((width, chunk), lambda f: (0, f)),
            pl.BlockSpec((chunk, width), lambda f: (f, 0)),
            row,
            whole,
        ]
        + [whole] * (len(slots) + len(grads)),
        out_specs=[whole, whole, wide, wide, whole, row],
        scratch_shapes=[pltpu.VMEM((each, width), F32), pltpu.VMEM((each, width), F32)],
        compiler_params=PARAMS,
        name="expert_kernel",
    )(small, up, down, up_bias, down_bias, *slots, *grads)


def expert_grad_kernel(me, *refs, n_dp):
    slots, act, d_pre, d_rows, up_bias = (refs[i * n_dp : (i + 1) * n_dp] for i in range(5))
    grad_up, grad_down, g_up_bias, g_down_bias = refs[5 * n_dp :]
    grad_up[...] = sum(mm(a[...], b[...], 0, 0) for a, b in zip(slots, d_pre))
    grad_down[...] = sum(mm(a[...], b[...], 0, 0) for a, b in zip(act, d_rows))

    @pl.when(pl.program_id(0) == 0)
    def _():
        g_up_bias[...] = sum_of(up_bias)
        sums = sum(jnp.sum(r[...].astype(F32), axis=0, keepdims=True) for r in d_rows)
        part = g_down_bias.shape[1]
        own = jnp.zeros((1, part), F32)
        for d in range(n_dp):
            own = own + jnp.where(me[0] == d, sums[:, d * part : (d + 1) * part], 0.0)
        g_down_bias[...] = own


def expert_grads(slots, act, d_pre, d_rows, up_bias, part):
    n_dp = len(slots)
    each, width = slots[0].shape
    ff = act[0].shape[1]
    steps = 4
    whole = pl.BlockSpec(memory_space=pltpu.VMEM)
    return pl.pallas_call(
        placed(functools.partial(expert_grad_kernel, n_dp=n_dp)),
        grid=(steps,),
        out_shape=[
            pltpu.HBM((width, ff), F32),
            pltpu.HBM((ff, width), F32),
            jax.ShapeDtypeStruct((1, ff), F32),
            jax.ShapeDtypeStruct((1, part), F32),
        ],
        in_specs=[pl.BlockSpec((each, width // steps), lambda f: (0, f))] * n_dp
        + [pl.BlockSpec((each, ff // steps), lambda f: (0, f))] * n_dp
        + [whole] * (3 * n_dp),
        out_specs=[
            pl.BlockSpec((width // steps, ff), lambda f: (f, 0)),
            pl.BlockSpec((ff // steps, width), lambda f: (f, 0)),
            whole,
            whole,
        ],
        compiler_params=PARAMS,
        name="expert_grad_kernel",
    )(*slots, *act, *d_pre, *d_rows, *up_bias)


def sum_of(refs):
    total = refs[0][...].astype(F32)
    for ref in refs[1:]:
        total = total + ref[...].astype(F32)
    return total


def line_sum_kernel(me, pick, *refs):
    refs[-1][...] = mm(pick[...], sum_of(refs[:-1]).astype(BF)).astype(BF)


def combine_kernel(
    me, back, route, rank, mixed, p, cotangent, small, vectors, proj,
    outputs, d_mixed, d_low_out, d_att, d_logits_out, sums, *, pair, capacity, experts, part,
):
    tok, width = mixed.shape
    n_back = back.shape[0]
    r, k = route[...], rank[...]
    key = jnp.where(k < capacity, r * pair + k, -2 * pair * experts)
    slot = lanes((tok, n_back), 1)
    combined = mm(jnp.where(slot == key, 1.0, 0.0).astype(BF), back[...])
    d_slot = mm(jnp.where(slot == key + capacity, 1.0, 0.0).astype(BF), back[...])
    hot = jnp.where(lanes(p.shape, 1) == r, 1.0, 0.0)
    gate = jnp.sum(p[...] * hot, axis=-1, keepdims=True)
    g = cotangent[...].astype(F32)
    outputs[...] = (mixed[...] + gate * combined).astype(BF)
    d_gate = jnp.sum(g * combined, axis=-1, keepdims=True)
    d_logits = (p[...] * (d_gate * hot - d_gate * gate)).astype(BF)
    d_logits_out[...] = d_logits
    d_normed = d_slot + mm(d_logits, small[...], 1, 1)
    unit, scale = normalise(mixed[...])
    sums[0:1] = jnp.sum(d_normed * unit, axis=0, keepdims=True)
    sums[1:2] = jnp.sum(d_normed, axis=0, keepdims=True)
    d = g + norm_back(d_normed, vectors[1:2], unit, scale)
    sums[2:3] = jnp.sum(d, axis=0, keepdims=True)
    d_mixed[...] = d
    low = d.astype(BF)
    d_low_out[...] = low
    for i in range(d_att.shape[0]):
        d_att[i] = mm(low, proj[i * part : (i + 1) * part], 1, 1).astype(BF)


def share(me, whole, near, keep):
    half, n_dp, own, _ = near.shape
    for q in range(half):
        for d in range(n_dp):
            row = d * 2 * half * own
            other = pl.multiple_of(row + (me[1] ^ (2 * q + 1)) * own, own)
            same = pl.multiple_of(row + (me[1] ^ (2 * q)) * own, own)
            near[q, d] = whole[pl.ds(other, own)].astype(BF)
            keep[q, d] = whole[pl.ds(same, own)].astype(BF)


def proj_grad_kernel(me, attended, d_low, near, keep, whole):
    n_dp, rows, part = attended.shape
    for d in range(n_dp):
        whole[d * part : (d + 1) * part] = mm(attended[d], d_low[...], 0, 0)
    share(me, whole, near, keep)


def core_sum_kernel(me, keep, came, first, *rest):
    for q, out in enumerate([first, *rest]):
        out[...] = (keep[q].astype(F32) + came[q].astype(F32)).astype(BF)


def chip_sum_kernel(me, *refs, n_dp):
    outs, total = refs[-1 - n_dp : -1], refs[-1]
    parts = refs[: -1 - n_dp]
    half = len(parts) // 2
    wide = parts[0].shape[2]
    total[:, :, :wide] = sum_of(parts[:half]).astype(BF)
    total[:, :, wide:] = sum_of(parts[half:]).astype(BF)
    for j in range(n_dp):
        outs[j][...] = total[(me[0] + j) % n_dp]


def core_sum(near, keep):
    half = near.shape[0]
    shape = near.shape[1:]
    return call(core_sum_kernel, [(shape, BF)] + [pltpu.HBM(shape, BF)] * (half - 1), keep, flip(near, 1))


def to_chips(parts):
    return [parts[0]] + [flip(part, 2 * (q + 1)) for q, part in enumerate(parts[1:])]


def attend_back_kernel(me, d_att, probs, packed, *refs, head_dim):
    blocks, (d_packed, d_normed, d_scores, qkv) = refs[:-4], refs[-4:]
    n_dp, rows, part = d_att.shape
    scale = head_dim ** (-0.5)
    assembled(me, blocks, qkv)
    for h in range(part // head_dim):
        a, b = h * head_dim, (h + 1) * head_dim
        q, k, v = packed[:, a:b], packed[:, part + a : part + b], packed[:, 2 * part + a : 2 * part + b]
        kt = k.T
        g = jnp.concatenate([d_att[i, :, a:b] for i in range(n_dp)], axis=0)
        for i in range(0, n_dp, 2):
            lo, hi = i * rows, (i + 2) * rows
            dp = mm(v[:hi], g[lo:hi], 1, 1)
            p = probs[h, :hi, lo:hi].astype(F32)
            delta = jnp.sum(p * dp, axis=0, keepdims=True)
            ds = (p * (dp - delta)).astype(BF)
            d_scores[:hi, lo:hi] = ds
            d_packed[lo:hi, a:b] = (mm(kt[:, :hi], ds).T * scale).astype(BF)
        for i in range(0, n_dp, 2):
            lo, hi = i * rows, (i + 2) * rows
            d_packed[lo:hi, part + a : part + b] = (mm(d_scores[lo:hi, lo:], q[lo:]) * scale).astype(BF)
            d_packed[lo:hi, 2 * part + a : 2 * part + b] = mm(probs[h, lo:hi, lo:], g[lo:]).astype(BF)
    for i in range(n_dp):
        d_normed[i] = mm(d_packed[i * rows : (i + 1) * rows], qkv[:, : 3 * part], 1, 1).astype(BF)


def qkv_grad_kernel(
    me, normed, vectors, d_packed, d_normed, token_normed, d_logits, sums, near, keep, whole, turned, *, experts
):
    n_dp, rows, width = d_normed.shape
    part = width // n_dp
    whole[:, : 3 * part] = mm(normed[...], d_packed[...], 0, 0)
    gain = jnp.zeros((1, width), F32)
    shift = jnp.zeros((1, width), F32)
    for i in range(n_dp):
        d = d_normed[i].astype(F32)
        gain = gain + jnp.sum(d * normed[i * rows : (i + 1) * rows].astype(F32), axis=0, keepdims=True)
        shift = shift + jnp.sum(d, axis=0, keepdims=True)
    gain = (gain - vectors[2:3] * shift) / vectors[0:1]
    columns = jnp.sum(d_packed[...].astype(F32), axis=0, keepdims=True)
    turned[...] = jnp.zeros_like(turned)
    e = experts
    turned[e : e + 1] = gain
    turned[e + 1 : e + 2] = sums[0:1]
    turned[e + 2 : e + 3] = shift
    for d in range(n_dp):
        here = me[0] == d
        turned[e + 3 : e + 4, d * part : (d + 1) * part] = jnp.where(here, columns[:, :part], 0.0)
        turned[e + 4 : e + 5, d * part : (d + 1) * part] = jnp.where(here, columns[:, 2 * part :], 0.0)
    turned[e + 5 : e + 6] = sums[2:3]
    turned[e + 6 : e + 7] = sums[1:2]
    whole[:, 3 * part :] = turned[...].T + mm(token_normed[...], d_logits[...], 0, 0)
    share(me, whole, near, keep)


def weights_end_kernel(me, *refs):
    (qkv, proj, router, gains, biases, wide, came), blocks = refs[-7:], refs[:-7]
    n_dp, own, _ = came.shape
    for j in range(n_dp):
        came[(me[0] + n_dp - j) % n_dp] = blocks[j][...]
    width = proj.shape[1]
    part = width // n_dp
    experts = router.shape[0]
    edge = 3 * part
    total = jnp.zeros((own, 128), F32)
    rows = jnp.zeros((own, width), F32)
    for d in range(n_dp):
        for i in range(3):
            qkv[:, i * width + d * part : i * width + (d + 1) * part] = came[
                d, :, i * part : (i + 1) * part
            ].astype(F32)
        total = total + came[d, :, edge : edge + 128].astype(F32)
        rows = rows + came[d, :, edge + 128 :].astype(F32)
    proj[...] = rows
    wide[...] = jnp.zeros_like(wide)
    wide[:own] = total
    flat = wide[...].T
    router[...] = flat[:experts, :own]
    gains[...] = flat[experts : experts + 2, :own]
    biases[...] = flat[experts + 2 : experts + 7, :own]


def tokens_end_kernel(me, came, tokens, vectors, d_mixed, out):
    total = came[0].astype(F32)
    for d in range(1, came.shape[0]):
        total = total + came[d].astype(F32)
    unit, scale = normalise(tokens[...].astype(F32))
    out[...] = d_mixed[...] + norm_back(total, vectors[0:1], unit, scale)


def shards(
    tokens,
    qkv_weight,
    proj_weight,
    router_weight,
    norm_gains,
    biases,
    up_weight,
    up_bias,
    down_weight,
    down_bias,
    routes,
    slot_order,
    segments,
    parents,
    cotangent,
):
    n_dp, n_ex = lax.axis_size("dp"), lax.axis_size("expert")
    rows, width = tokens.shape[1], tokens.shape[2]
    part = width // n_dp
    head_dim = width // H
    own = qkv_weight.shape[0]
    experts = router_weight.shape[1]
    capacity = (9 * rows + 8 * experts - 1) // (8 * experts)
    pad = -(-capacity // 8) * 8
    pair = -(-capacity // 4) * 8
    length = n_dp * rows
    each = n_ex * capacity
    cols = 3 * part + 128
    x = tokens[0]

    token_blocks = spread(x)
    columns = call(
        weights_kernel,
        [pltpu.HBM((n_dp, own, cols), BF)],
        *far(qkv_weight, router_weight.T, norm_gains, biases),
        scratch=[pltpu.VMEM((128, 128), F32)],
        n_dp=n_dp,
    )[0]
    qkv_blocks = gather_experts(swap(columns, "dp"))
    smem = pl.BlockSpec(memory_space=pltpu.SMEM)
    vmem = pl.BlockSpec(memory_space=pltpu.VMEM)
    grads_out, tableT, route, rank, bias = pl.pallas_call(
        placed(functools.partial(slots_kernel, pad=pad, capacity=capacity, experts=experts)),
        out_shape=[
            pltpu.HBM((n_ex * pad, width), BF),
            pltpu.HBM((n_ex * pad, rows), BF),
            pltpu.HBM((rows, 1), I32),
            pltpu.HBM((rows, 1), I32),
            jax.ShapeDtypeStruct((length, length), BF),
        ],
        in_specs=[smem] + [vmem] * 4,
        out_specs=[vmem] * 5,
        compiler_params=PARAMS,
        name="slots_kernel",
    )(parents, *far(routes.reshape(1, rows), slot_order[0], cotangent[0], segments))

    def dispatch(rows_out):
        came = swap(rows_out.reshape(n_ex, pad, width), "expert").reshape(n_ex * pad, width)
        mine = call(pack_kernel, [pltpu.HBM((each, width), BF)], *far(pack_picks(n_ex, pad, capacity)), came)[0]
        return mine

    grads_in = dispatch(grads_out)
    proj_blocks = gather_experts(swap(jnp.broadcast_to(proj_weight, (n_dp, own, width)), "dp"))
    grads_in, bias = lax.optimization_barrier((grads_in, bias))
    grads = spread(grads_in)
    normed1, packed, probs, att_out, vectors, small = call(
        attend_kernel,
        [
            pltpu.HBM((length, width), BF),
            pltpu.HBM((length, 3 * part), BF),
            pltpu.HBM((part // head_dim, length, length), BF),
            pltpu.HBM((n_dp, rows, part), BF),
            ((8, width), F32),
            ((width, 128), BF),
        ],
        bias, *far(*qkv_blocks, *sum(token_blocks, [])),
        scratch=[pltpu.VMEM((width, cols), BF)],
        counts=[len(b) for b in token_blocks], n_ex=n_ex, head_dim=head_dim, experts=experts,
    )
    early = list(range(1, n_dp - 1))
    att_out, *came = lax.optimization_barrier((att_out, *[grads[k][0] for k in early]))
    for k, block in zip(early, came):
        grads[k] = [block]
    attended = swap(att_out, "dp")
    proj = call(assemble_kernel, [((n_dp, n_ex, own, width), BF)], *proj_blocks)[0].reshape(width, width)
    mixed, normed2, p, sent = call(
        mix_kernel,
        [pltpu.HBM((rows, width), F32), pltpu.HBM((rows, width), BF), pltpu.HBM((rows, 128), F32), pltpu.HBM((n_ex * pad, width), BF)],
        *far(x), attended, proj, small, vectors, *far(tableT),
        experts=experts,
    )
    mine = dispatch(sent)
    grads = lax.optimization_barrier(grads)
    def expert(slots, k):
        return expert_call(
            small, up_weight[0], down_weight[0], up_bias, down_bias, slots, grads[k], n_dp, experts
        )

    done = {0: expert([mine], 0)}

    def after_own(block):
        block, done[0] = lax.optimization_barrier((block, done[0]))
        return block

    slots = spread(mine, after_own)
    came = [done[0][0]] + [None] * (n_dp - 1)
    last = 0
    for k in [2, 1, 3] if n_dp == 4 else range(1, n_dp):
        slots[k], done[last] = lax.optimization_barrier((slots[k], done[last]))
        done[k] = expert(slots[k], k)
        came[k] = across(done[k][0], k)
        last = k
    came[0] = done[0][0]
    all_slots, act, d_pre, d_rows, g_up_bias = ([done[k][i] for k in range(n_dp)] for i in range(1, 6))
    grad_up, grad_down, grad_up_bias, grad_down_bias = expert_grads(
        all_slots, act, d_pre, d_rows, g_up_bias, part
    )
    grad_up, grad_down, *came = lax.optimization_barrier((grad_up, grad_down, *came))
    summed = call(line_sum_kernel, [pltpu.HBM((n_ex * pair, width), BF)], *far(line_picks(n_ex, pair, capacity)), *came)[0]
    back = swap(summed.reshape(n_ex, pair, width), "expert").reshape(n_ex * pair, width)
    outputs, d_mixed, d_low, d_att, d_logits, sums = call(
        combine_kernel,
        [
            pltpu.HBM((rows, width), BF),
            pltpu.HBM((rows, width), F32),
            ((rows, width), BF),
            pltpu.HBM((n_dp, rows, part), BF),
            pltpu.HBM((rows, 128), BF),
            pltpu.HBM((8, width), F32),
        ],
        back, *far(route, rank, mixed, p, cotangent[0]), small, vectors, proj,
        pair=pair, capacity=capacity, experts=experts, part=part,
    )
    d_heads = swap(d_att, "dp")
    half = n_ex // 2
    near, keep = call(
        proj_grad_kernel,
        [pltpu.HBM((half, n_dp, own, width), BF), ((half, n_dp, own, width), BF)],
        *far(attended), d_low,
        scratch=[pltpu.VMEM((width, width), F32)],
    )
    d_heads, *parts = lax.optimization_barrier((d_heads, *core_sum(near, keep)))
    proj_chips = to_chips(parts)
    d_packed, d_normed = call(
        attend_back_kernel,
        [((length, 3 * part), BF), pltpu.HBM((n_dp, rows, width), BF)],
        d_heads, *far(probs, packed, *qkv_blocks),
        scratch=[pltpu.VMEM((length, length), BF), pltpu.VMEM((width, cols), BF)],
        head_dim=head_dim,
    )
    d_packed, *proj_chips = lax.optimization_barrier((d_packed, *proj_chips))
    near, keep = call(
        qkv_grad_kernel,
        [pltpu.HBM((half, n_dp, own, cols), BF), ((half, n_dp, own, cols), BF)],
        *far(normed1), vectors, d_packed, *far(d_normed, normed2, d_logits, sums),
        scratch=[pltpu.VMEM((width, cols), F32), pltpu.VMEM((128, width), F32)],
        experts=experts,
    )
    near, d_normed = lax.optimization_barrier((near, d_normed))
    d_own = swap(d_normed, "dp")
    qkv_chips = to_chips(core_sum(near, keep))
    summed = call(
        chip_sum_kernel, [pltpu.HBM((own, cols + width), BF)] * n_dp, *qkv_chips, *proj_chips,
        scratch=[pltpu.VMEM((n_dp, own, cols + width), BF)], n_dp=n_dp,
    )
    summed = along(summed)
    d_own, summed[1] = lax.optimization_barrier((d_own, summed[1]))
    owned_qkv, owned_proj, owned_router, owned_gains, owned_biases = call(
        weights_end_kernel,
        [
            pltpu.HBM((own, 3 * width), F32),
            pltpu.HBM((own, width), F32),
            pltpu.HBM((experts, own), F32),
            pltpu.HBM((2, own), F32),
            pltpu.HBM((5, own), F32),
        ],
        *summed,
        scratch=[pltpu.VMEM((128, 128), F32), pltpu.VMEM((n_dp, own, cols + width), BF)],
    )
    grad_tokens = call(tokens_end_kernel, [pltpu.HBM((rows, width), F32)], d_own, *far(x), vectors, *far(d_mixed))[0]
    return (
        outputs[None],
        grad_tokens[None],
        owned_qkv,
        owned_proj,
        owned_router.T,
        owned_gains,
        owned_biases,
        grad_up[None],
        grad_up_bias,
        grad_down[None],
        grad_down_bias,
    )


def solution(mesh):
    line = P(("dp", "expert"), None)
    across = P(None, ("dp", "expert"))
    act = P("expert", "dp", None)
    return jax.shard_map(
        shards,
        mesh=mesh,
        in_specs=(
            act,
            line,
            line,
            line,
            across,
            across,
            P("expert", None, "dp"),
            P("expert", "dp"),
            act,
            P("expert", "dp"),
            act,
            act,
            P("expert", None),
            P("expert", None),
            act,
        ),
        out_specs=(
            act,
            act,
            line,
            line,
            line,
            across,
            across,
            P("expert", None, "dp"),
            P("expert", "dp"),
            act,
            P("expert", "dp"),
        ),
        check_vma=False,
    )
```

```python
import functools

import jax
import jax.numpy as jnp
import numpy as np
from jax import lax
from jax.experimental import pallas as pl
from jax.experimental.pallas import tpu as pltpu
from jax.sharding import PartitionSpec as P

H = 16
NSEG = 7
EPS = 1e-05
NEG = -1e30
BF = jnp.bfloat16
F32 = jnp.float32
I32 = jnp.int32


def mm(a, b, ca=1, cb=0):
    return lax.dot_general(a, b, (((ca,), (cb,)), ((), ())), preferred_element_type=F32)


def placed(kernel):
    def body(*refs):
        kernel((lax.axis_index("dp"), lax.axis_index("expert")), *refs)

    return body


PARAMS = pltpu.CompilerParams(vmem_limit_bytes=24 << 20)


def far(*arrays):
    return [pltpu.with_memory_space_constraint(x, pltpu.HBM) for x in arrays]


def call(kernel, outs, *args, scratch=(), **static):
    vmem = pl.BlockSpec(memory_space=pltpu.VMEM)
    return pl.pallas_call(
        placed(functools.partial(kernel, **static)),
        out_shape=[o if isinstance(o, pl.MemoryRef) else jax.ShapeDtypeStruct(*o) for o in outs],
        in_specs=[vmem] * len(args),
        out_specs=[vmem] * len(outs),
        scratch_shapes=list(scratch),
        compiler_params=PARAMS,
        name=kernel.__name__,
    )(*args)


def ahead(x, step):
    n = lax.axis_size("dp")
    return lax.ppermute(x, "dp", [(i, (i + step) % n) for i in range(n)])


def flip(x, bits):
    n = lax.axis_size("expert")
    return lax.ppermute(x, "expert", [(i, i ^ bits) for i in range(n)])


def swap(x, axis):
    return lax.all_to_all(x, axis, split_axis=0, concat_axis=0, tiled=True)


def along(blocks, sign=1):
    return [blocks[0]] + [ahead(blocks[j], sign * j) for j in range(1, len(blocks))]


def across(x, bits):
    n = lax.axis_size("dp")
    return lax.ppermute(x, "dp", [(i, i ^ bits) for i in range(n)])


def spread(x, hold=None):
    n = lax.axis_size("dp")
    out = [[x]] + [[across(x, k)] for k in range(1, n - 1)]
    if n != 4:
        return out + [[across(x, n - 1)]]
    own = lax.ppermute(x, "dp", [(1, 2), (2, 1)])
    if hold is not None:
        out[2] = [hold(out[2][0])]
    return out + [[own, lax.ppermute(out[2][0], "dp", [(1, 0), (2, 3)])]]


def added(refs):
    return refs[0][...] if len(refs) == 1 else refs[0][...] + refs[1][...]


def split(refs, counts):
    out, at = [], 0
    for count in counts:
        out.append(refs[at : at + count])
        at += count
    return out


def gather_experts(x):
    n = lax.axis_size("expert")
    mine = [x] + [flip(x, 2 * k) for k in range(1, n // 2)]
    out = []
    for block in mine:
        out += [block, flip(block, 1)]
    return out


def normalise(values):
    mean = jnp.mean(values, axis=-1, keepdims=True)
    centred = values - mean
    scale = lax.rsqrt(jnp.mean(centred * centred, axis=-1, keepdims=True) + EPS)
    return centred * scale, scale


def norm_back(upstream, gain, unit, scale):
    e = upstream * gain
    return scale * (
        e - jnp.mean(e, axis=-1, keepdims=True) - unit * jnp.mean(e * unit, axis=-1, keepdims=True)
    )


def lanes(shape, dim):
    return lax.broadcasted_iota(I32, shape, dim)


def softmax_of(logits, experts):
    logits = jnp.where(lanes(logits.shape, 1) < experts, logits, NEG)
    top = jnp.max(logits, axis=-1, keepdims=True)
    weight = jnp.exp(logits - top)
    return weight / jnp.sum(weight, axis=-1, keepdims=True)


def weights_kernel(me, qkv, proj, router, gains, biases, out, rows, turned, *, n_dp):
    own, width = qkv.shape[0], qkv.shape[1] // 3
    part = width // n_dp
    experts = router.shape[0]
    turned[...] = jnp.zeros_like(turned)
    turned[:experts, :own] = router[...].astype(F32)
    turned[experts : experts + 2, :own] = gains[...].astype(F32)
    turned[experts + 2 : experts + 7, :own] = biases[...].astype(F32)
    small = turned[...].T[:own].astype(BF)
    for d in range(n_dp):
        for i in range(3):
            out[d, :, i * part : (i + 1) * part] = qkv[
                :, i * width + d * part : i * width + (d + 1) * part
            ]
        out[d, :, 3 * part :] = small
        rows[d] = proj[...]


def slots_kernel(
    me, parents, route, order, cotangent, seg, grads, tableT, route_out, rank_out, bias, *, pad, capacity, experts
):
    tok = route.shape[1]
    rt = jnp.broadcast_to(route[...].astype(F32), (tok, tok))
    r = rt.T
    route_out[...] = r[:, 0:1].astype(I32)
    o = jnp.broadcast_to(order[...].astype(F32), (tok, tok))
    ot = o.T
    same = r == rt
    rank = jnp.sum(jnp.where(same & (o < ot), 1.0, 0.0), axis=1, keepdims=True)
    rank_row = jnp.sum(jnp.where(same & (ot < o), 1.0, 0.0), axis=0, keepdims=True)
    rank_out[...] = rank.astype(I32)
    key = jnp.where(rank_row < capacity, rt[0:1] * pad + rank_row, -1.0).astype(I32)
    table = jnp.where(lanes((experts * pad, tok), 0) == key, 1.0, 0.0).astype(BF)
    tableT[...] = table
    grads[...] = mm(table, cotangent[...]).astype(BF)
    length = seg.shape[1]
    masks = [jnp.int32(1)]
    for s in range(1, NSEG):
        up = jnp.int32(0)
        for a in range(s):
            up = jnp.where(parents[0, s] == a, masks[a], up)
        masks.append(up | (1 << s))
    block = 128
    mine = jnp.zeros((1, length), I32)
    for s in range(NSEG):
        mine = jnp.where(seg[...] == s, masks[s], mine)
    for i in range(length // block):
        col = jnp.broadcast_to(seg[:, i * block : (i + 1) * block].astype(F32), (block, block)).T
        bit = jnp.left_shift(1, jnp.broadcast_to(col[:, 0:1], (block, length)).astype(I32))
        seen = lanes((block, length), 0) + i * block <= lanes((block, length), 1)
        bias[i * block : (i + 1) * block] = jnp.where(seen & ((mine & bit) != 0), 0.0, NEG).astype(BF)


def pack_kernel(me, pick, rows, out):
    out[...] = mm(pick[...], rows[...]).astype(BF)


def pack_picks(n_ex, pad, capacity):
    pick = np.zeros((n_ex * capacity, n_ex * pad), np.float32)
    for e in range(n_ex):
        for c in range(capacity):
            pick[e * capacity + c, e * pad + c] = 1
    return jnp.asarray(pick, BF)


def line_picks(n_ex, pair, capacity):
    pick = np.zeros((n_ex * pair, 2 * n_ex * capacity), np.float32)
    for e in range(n_ex):
        for w in range(2):
            for c in range(capacity):
                pick[e * pair + w * capacity + c, (w * n_ex + e) * capacity + c] = 1
    return jnp.asarray(pick, BF)


def assemble_kernel(me, *refs):
    out = refs[-1]
    for k, block in enumerate(refs[:-1]):
        e = me[1] ^ k
        for d in range(block.shape[0]):
            out[d, e] = block[d]


def assembled(me, blocks, whole):
    own = blocks[0].shape[1]
    n_ex = len(blocks)
    for k, block in enumerate(blocks):
        for d in range(block.shape[0]):
            row = pl.multiple_of((d * n_ex + (me[1] ^ k)) * own, own)
            whole[pl.ds(row, own)] = block[d]


def attend_kernel(me, bias, *refs, counts, n_ex, head_dim, experts):
    blocks, refs = refs[:n_ex], refs[n_ex:]
    tokens, (normed, packed, probs, attended, vectors, small, qkv) = split(refs, counts), refs[-7:]
    n_dp = len(counts)
    rows, width = tokens[0][0].shape
    part = width // n_dp
    assembled(me, blocks, qkv)
    few = qkv[:, 3 * part :]
    small[...] = few
    vectors[...] = few.astype(F32).T[experts : experts + 8]
    gain, shift = vectors[0:1], vectors[2:3]
    parts = [jnp.zeros((1, part), F32)] * 2
    for d in range(n_dp):
        for i in range(2):
            here = vectors[3 + i : 4 + i, d * part : (d + 1) * part]
            parts[i] = parts[i] + jnp.where(me[0] == d, here, 0.0)

    for k, blocks in enumerate(tokens):
        base = pl.multiple_of((me[0] ^ k) * rows, rows)
        unit, _ = normalise(added(blocks).astype(F32))
        normed[pl.ds(base, rows)] = (unit * gain + shift).astype(BF)

    raw = mm(normed[...], qkv[:, : 3 * part])
    packed[:, :part] = (raw[:, :part] + parts[0]).astype(BF)
    packed[:, part : 2 * part] = raw[:, part : 2 * part].astype(BF)
    packed[:, 2 * part :] = (raw[:, 2 * part :] + parts[1]).astype(BF)
    scale = head_dim ** (-0.5)
    for h in range(part // head_dim):
        q = packed[:, h * head_dim : (h + 1) * head_dim]
        k = packed[:, part + h * head_dim : part + (h + 1) * head_dim]
        vt = packed[:, 2 * part + h * head_dim : 2 * part + (h + 1) * head_dim].T
        for i in range(0, n_dp, 2):
            lo, hi = i * rows, (i + 2) * rows
            s = mm(k[:hi], q[lo:hi], 1, 1) * scale + bias[:hi, lo:hi].astype(F32)
            p = jnp.exp(s - jnp.max(s, axis=0, keepdims=True))
            p = (p * (1.0 / jnp.sum(p, axis=0, keepdims=True))).astype(BF)
            probs[h, :hi, lo:hi] = p
            out = mm(vt[:, :hi], p).T.astype(BF)
            attended[i, :, h * head_dim : (h + 1) * head_dim] = out[:rows]
            attended[i + 1, :, h * head_dim : (h + 1) * head_dim] = out[rows:]


def mix_kernel(me, tokens, attended, proj, small, vectors, tableT, mixed, normed, p, sent, *, experts):
    n_dp, rows, part = attended.shape
    total = tokens[...].astype(F32) + vectors[5:6]
    for d in range(n_dp):
        total = total + mm(attended[d], proj[d * part : (d + 1) * part])
    mixed[...] = total
    unit, _ = normalise(total)
    low = (unit * vectors[1:2] + vectors[6:7]).astype(BF)
    normed[...] = low
    p[...] = softmax_of(mm(low, small[...]), experts)
    sent[...] = mm(tableT[...], low).astype(BF)


def expert_kernel(
    me, small, up, down, up_bias, down_bias, *refs, counts, n_dp, experts
):
    came, grads, (both, slots, act_out, d_pre_out, d_rows, g_up_bias, acc_r, acc_s) = split(refs, [*counts, 8])
    f = pl.program_id(0)
    each, width = slots.shape
    part = width // n_dp

    @pl.when(f == 0)
    def _():
        slots[...] = added(came)
        p = softmax_of(mm(slots[...], small[...]), experts)
        gate = jnp.sum(jnp.where(lanes(p.shape, 1) == me[1], p, 0.0), axis=-1, keepdims=True)
        d_rows[...] = (gate * added(grads).astype(F32)).astype(BF)
        acc_s[...] = jnp.zeros_like(acc_s)
        for d in range(n_dp):
            acc_r[:, d * part : (d + 1) * part] = jnp.broadcast_to(
                jnp.where(me[0] == d, down_bias[...].astype(F32), 0.0), (each, part)
            )

    u = mm(slots[...], up[...]) + up_bias[...].astype(F32)
    c, a = 0.7978845608028654, 0.044715
    t = jnp.tanh(c * (u + a * (u * u * u)))
    act = (0.5 * u * (1.0 + t)).astype(BF)
    slope = 0.5 * (1.0 + t) + 0.5 * u * (1.0 - t * t) * (c * (1.0 + 3.0 * a * (u * u)))
    d_pre = mm(d_rows[...], down[...], 1, 1) * slope
    g_up_bias[...] = jnp.sum(d_pre, axis=0, keepdims=True)
    low = d_pre.astype(BF)
    act_out[...] = act
    d_pre_out[...] = low
    acc_r[...] += mm(act, down[...])
    acc_s[...] += mm(low, up[...], 1, 1)

    @pl.when(f == pl.num_programs(0) - 1)
    def _():
        both[:each] = acc_r[...].astype(BF)
        both[each:] = acc_s[...].astype(BF)


def expert_call(small, up, down, up_bias, down_bias, slots, grads, n_dp, experts):
    each, width = slots[0].shape
    ff = up.shape[1]
    chunk = min(ff, 256)
    whole = pl.BlockSpec(memory_space=pltpu.VMEM)
    wide = pl.BlockSpec((each, chunk), lambda f: (0, f))
    row = pl.BlockSpec((1, chunk), lambda f: (0, f))
    return pl.pallas_call(
        placed(
            functools.partial(
                expert_kernel, counts=(len(slots), len(grads)), n_dp=n_dp, experts=experts
            )
        ),
        grid=(ff // chunk,),
        out_shape=[
            pltpu.HBM((2 * each, width), BF),
            jax.ShapeDtypeStruct((each, width), BF),
            jax.ShapeDtypeStruct((each, ff), BF),
            jax.ShapeDtypeStruct((each, ff), BF),
            jax.ShapeDtypeStruct((each, width), BF),
            jax.ShapeDtypeStruct((1, ff), F32),
        ],
        in_specs=[
            whole,
            pl.BlockSpec((width, chunk), lambda f: (0, f)),
            pl.BlockSpec((chunk, width), lambda f: (f, 0)),
            row,
            whole,
        ]
        + [whole] * (len(slots) + len(grads)),
        out_specs=[whole, whole, wide, wide, whole, row],
        scratch_shapes=[pltpu.VMEM((each, width), F32), pltpu.VMEM((each, width), F32)],
        compiler_params=PARAMS,
        name="expert_kernel",
    )(small, up, down, up_bias, down_bias, *slots, *grads)


def expert_grad_kernel(me, *refs, n_dp):
    slots, act, d_pre, d_rows, up_bias = (refs[i * n_dp : (i + 1) * n_dp] for i in range(5))
    grad_up, grad_down, g_up_bias, g_down_bias = refs[5 * n_dp :]
    grad_up[...] = sum(mm(a[...], b[...], 0, 0) for a, b in zip(slots, d_pre))
    grad_down[...] = sum(mm(a[...], b[...], 0, 0) for a, b in zip(act, d_rows))

    @pl.when(pl.program_id(0) == 0)
    def _():
        g_up_bias[...] = sum_of(up_bias)
        sums = sum(jnp.sum(r[...].astype(F32), axis=0, keepdims=True) for r in d_rows)
        part = g_down_bias.shape[1]
        own = jnp.zeros((1, part), F32)
        for d in range(n_dp):
            own = own + jnp.where(me[0] == d, sums[:, d * part : (d + 1) * part], 0.0)
        g_down_bias[...] = own


def expert_grads(slots, act, d_pre, d_rows, up_bias, part):
    n_dp = len(slots)
    each, width = slots[0].shape
    ff = act[0].shape[1]
    steps = 4
    whole = pl.BlockSpec(memory_space=pltpu.VMEM)
    return pl.pallas_call(
        placed(functools.partial(expert_grad_kernel, n_dp=n_dp)),
        grid=(steps,),
        out_shape=[
            pltpu.HBM((width, ff), F32),
            pltpu.HBM((ff, width), F32),
            jax.ShapeDtypeStruct((1, ff), F32),
            jax.ShapeDtypeStruct((1, part), F32),
        ],
        in_specs=[pl.BlockSpec((each, width // steps), lambda f: (0, f))] * n_dp
        + [pl.BlockSpec((each, ff // steps), lambda f: (0, f))] * n_dp
        + [whole] * (3 * n_dp),
        out_specs=[
            pl.BlockSpec((width // steps, ff), lambda f: (f, 0)),
            pl.BlockSpec((ff // steps, width), lambda f: (f, 0)),
            whole,
            whole,
        ],
        compiler_params=PARAMS,
        name="expert_grad_kernel",
    )(*slots, *act, *d_pre, *d_rows, *up_bias)


def sum_of(refs):
    total = refs[0][...].astype(F32)
    for ref in refs[1:]:
        total = total + ref[...].astype(F32)
    return total


def line_sum_kernel(me, pick, *refs):
    refs[-1][...] = mm(pick[...], sum_of(refs[:-1]).astype(BF)).astype(BF)


def combine_kernel(
    me, back, route, rank, mixed, p, cotangent, small, vectors, proj,
    outputs, d_mixed, d_low_out, d_att, d_logits_out, sums, *, pair, capacity, experts, part,
):
    tok, width = mixed.shape
    n_back = back.shape[0]
    r, k = route[...], rank[...]
    key = jnp.where(k < capacity, r * pair + k, -2 * pair * experts)
    slot = lanes((tok, n_back), 1)
    combined = mm(jnp.where(slot == key, 1.0, 0.0).astype(BF), back[...])
    d_slot = mm(jnp.where(slot == key + capacity, 1.0, 0.0).astype(BF), back[...])
    hot = jnp.where(lanes(p.shape, 1) == r, 1.0, 0.0)
    gate = jnp.sum(p[...] * hot, axis=-1, keepdims=True)
    g = cotangent[...].astype(F32)
    outputs[...] = (mixed[...] + gate * combined).astype(BF)
    d_gate = jnp.sum(g * combined, axis=-1, keepdims=True)
    d_logits = (p[...] * (d_gate * hot - d_gate * gate)).astype(BF)
    d_logits_out[...] = d_logits
    d_normed = d_slot + mm(d_logits, small[...], 1, 1)
    unit, scale = normalise(mixed[...])
    sums[0:1] = jnp.sum(d_normed * unit, axis=0, keepdims=True)
    sums[1:2] = jnp.sum(d_normed, axis=0, keepdims=True)
    d = g + norm_back(d_normed, vectors[1:2], unit, scale)
    sums[2:3] = jnp.sum(d, axis=0, keepdims=True)
    d_mixed[...] = d
    low = d.astype(BF)
    d_low_out[...] = low
    for i in range(d_att.shape[0]):
        d_att[i] = mm(low, proj[i * part : (i + 1) * part], 1, 1).astype(BF)


def share(me, whole, near, keep):
    half, n_dp, own, _ = near.shape
    for q in range(half):
        for d in range(n_dp):
            row = d * 2 * half * own
            other = pl.multiple_of(row + (me[1] ^ (2 * q + 1)) * own, own)
            same = pl.multiple_of(row + (me[1] ^ (2 * q)) * own, own)
            near[q, d] = whole[pl.ds(other, own)].astype(BF)
            keep[q, d] = whole[pl.ds(same, own)].astype(BF)


def proj_grad_kernel(me, attended, d_low, near, keep, whole):
    n_dp, rows, part = attended.shape
    for d in range(n_dp):
        whole[d * part : (d + 1) * part] = mm(attended[d], d_low[...], 0, 0)
    share(me, whole, near, keep)


def core_sum_kernel(me, keep, came, first, *rest):
    for q, out in enumerate([first, *rest]):
        out[...] = (keep[q].astype(F32) + came[q].astype(F32)).astype(BF)


def chip_sum_kernel(me, *refs, n_dp):
    outs, total = refs[-1 - n_dp : -1], refs[-1]
    parts = refs[: -1 - n_dp]
    half = len(parts) // 2
    wide = parts[0].shape[2]
    total[:, :, :wide] = sum_of(parts[:half]).astype(BF)
    total[:, :, wide:] = sum_of(parts[half:]).astype(BF)
    for j in range(n_dp):
        outs[j][...] = total[(me[0] + j) % n_dp]


def core_sum(near, keep):
    half = near.shape[0]
    shape = near.shape[1:]
    return call(core_sum_kernel, [(shape, BF)] + [pltpu.HBM(shape, BF)] * (half - 1), keep, flip(near, 1))


def to_chips(parts):
    return [parts[0]] + [flip(part, 2 * (q + 1)) for q, part in enumerate(parts[1:])]


def attend_back_kernel(me, d_att, probs, packed, *refs, head_dim):
    blocks, (d_packed, d_normed, d_scores, qkv) = refs[:-4], refs[-4:]
    n_dp, rows, part = d_att.shape
    scale = head_dim ** (-0.5)
    assembled(me, blocks, qkv)
    for h in range(part // head_dim):
        a, b = h * head_dim, (h + 1) * head_dim
        q, k, v = packed[:, a:b], packed[:, part + a : part + b], packed[:, 2 * part + a : 2 * part + b]
        kt = k.T
        g = jnp.concatenate([d_att[i, :, a:b] for i in range(n_dp)], axis=0)
        for i in range(0, n_dp, 2):
            lo, hi = i * rows, (i + 2) * rows
            dp = mm(v[:hi], g[lo:hi], 1, 1)
            p = probs[h, :hi, lo:hi].astype(F32)
            delta = jnp.sum(p * dp, axis=0, keepdims=True)
            ds = (p * (dp - delta)).astype(BF)
            d_scores[:hi, lo:hi] = ds
            d_packed[lo:hi, a:b] = (mm(kt[:, :hi], ds).T * scale).astype(BF)
        for i in range(0, n_dp, 2):
            lo, hi = i * rows, (i + 2) * rows
            d_packed[lo:hi, part + a : part + b] = (mm(d_scores[lo:hi, lo:], q[lo:]) * scale).astype(BF)
            d_packed[lo:hi, 2 * part + a : 2 * part + b] = mm(probs[h, lo:hi, lo:], g[lo:]).astype(BF)
    for i in range(n_dp):
        d_normed[i] = mm(d_packed[i * rows : (i + 1) * rows], qkv[:, : 3 * part], 1, 1).astype(BF)


def qkv_grad_kernel(
    me, normed, vectors, d_packed, d_normed, token_normed, d_logits, sums, near, keep, whole, turned, *, experts
):
    n_dp, rows, width = d_normed.shape
    part = width // n_dp
    whole[:, : 3 * part] = mm(normed[...], d_packed[...], 0, 0)
    gain = jnp.zeros((1, width), F32)
    shift = jnp.zeros((1, width), F32)
    for i in range(n_dp):
        d = d_normed[i].astype(F32)
        gain = gain + jnp.sum(d * normed[i * rows : (i + 1) * rows].astype(F32), axis=0, keepdims=True)
        shift = shift + jnp.sum(d, axis=0, keepdims=True)
    gain = (gain - vectors[2:3] * shift) / vectors[0:1]
    columns = jnp.sum(d_packed[...].astype(F32), axis=0, keepdims=True)
    turned[...] = jnp.zeros_like(turned)
    e = experts
    turned[e : e + 1] = gain
    turned[e + 1 : e + 2] = sums[0:1]
    turned[e + 2 : e + 3] = shift
    for d in range(n_dp):
        here = me[0] == d
        turned[e + 3 : e + 4, d * part : (d + 1) * part] = jnp.where(here, columns[:, :part], 0.0)
        turned[e + 4 : e + 5, d * part : (d + 1) * part] = jnp.where(here, columns[:, 2 * part :], 0.0)
    turned[e + 5 : e + 6] = sums[2:3]
    turned[e + 6 : e + 7] = sums[1:2]
    whole[:, 3 * part :] = turned[...].T + mm(token_normed[...], d_logits[...], 0, 0)
    share(me, whole, near, keep)


def weights_end_kernel(me, *refs):
    (qkv, proj, router, gains, biases, wide, came), blocks = refs[-7:], refs[:-7]
    n_dp, own, _ = came.shape
    for j in range(n_dp):
        came[(me[0] + n_dp - j) % n_dp] = blocks[j][...]
    width = proj.shape[1]
    part = width // n_dp
    experts = router.shape[0]
    edge = 3 * part
    total = jnp.zeros((own, 128), F32)
    rows = jnp.zeros((own, width), F32)
    for d in range(n_dp):
        for i in range(3):
            qkv[:, i * width + d * part : i * width + (d + 1) * part] = came[
                d, :, i * part : (i + 1) * part
            ].astype(F32)
        total = total + came[d, :, edge : edge + 128].astype(F32)
        rows = rows + came[d, :, edge + 128 :].astype(F32)
    proj[...] = rows
    wide[...] = jnp.zeros_like(wide)
    wide[:own] = total
    flat = wide[...].T
    router[...] = flat[:experts, :own]
    gains[...] = flat[experts : experts + 2, :own]
    biases[...] = flat[experts + 2 : experts + 7, :own]


def tokens_end_kernel(me, came, tokens, vectors, d_mixed, out):
    total = came[0].astype(F32)
    for d in range(1, came.shape[0]):
        total = total + came[d].astype(F32)
    unit, scale = normalise(tokens[...].astype(F32))
    out[...] = d_mixed[...] + norm_back(total, vectors[0:1], unit, scale)


def shards(
    tokens,
    qkv_weight,
    proj_weight,
    router_weight,
    norm_gains,
    biases,
    up_weight,
    up_bias,
    down_weight,
    down_bias,
    routes,
    slot_order,
    segments,
    parents,
    cotangent,
):
    n_dp, n_ex = lax.axis_size("dp"), lax.axis_size("expert")
    rows, width = tokens.shape[1], tokens.shape[2]
    part = width // n_dp
    head_dim = width // H
    own = qkv_weight.shape[0]
    experts = router_weight.shape[1]
    capacity = (9 * rows + 8 * experts - 1) // (8 * experts)
    pad = -(-capacity // 8) * 8
    pair = -(-capacity // 4) * 8
    length = n_dp * rows
    each = n_ex * capacity
    cols = 3 * part + 128
    x = tokens[0]

    token_blocks = spread(x)
    columns, proj_rows = call(
        weights_kernel,
        [pltpu.HBM((n_dp, own, cols), BF), pltpu.HBM((n_dp, own, width), BF)],
        *far(qkv_weight, proj_weight, router_weight.T, norm_gains, biases),
        scratch=[pltpu.VMEM((128, 128), F32)],
        n_dp=n_dp,
    )
    qkv_blocks = gather_experts(swap(columns, "dp"))
    smem = pl.BlockSpec(memory_space=pltpu.SMEM)
    vmem = pl.BlockSpec(memory_space=pltpu.VMEM)
    grads_out, tableT, route, rank, bias = pl.pallas_call(
        placed(functools.partial(slots_kernel, pad=pad, capacity=capacity, experts=experts)),
        out_shape=[
            pltpu.HBM((n_ex * pad, width), BF),
            pltpu.HBM((n_ex * pad, rows), BF),
            pltpu.HBM((rows, 1), I32),
            pltpu.HBM((rows, 1), I32),
            jax.ShapeDtypeStruct((length, length), BF),
        ],
        in_specs=[smem] + [vmem] * 4,
        out_specs=[vmem] * 5,
        compiler_params=PARAMS,
        name="slots_kernel",
    )(parents, *far(routes.reshape(1, rows), slot_order[0], cotangent[0], segments))

    def dispatch(rows_out):
        came = swap(rows_out.reshape(n_ex, pad, width), "expert").reshape(n_ex * pad, width)
        mine = call(pack_kernel, [pltpu.HBM((each, width), BF)], *far(pack_picks(n_ex, pad, capacity)), came)[0]
        return mine

    grads_in = dispatch(grads_out)
    proj_blocks = gather_experts(swap(proj_rows, "dp"))
    grads_in, bias = lax.optimization_barrier((grads_in, bias))
    grads = spread(grads_in)
    normed1, packed, probs, att_out, vectors, small = call(
        attend_kernel,
        [
            pltpu.HBM((length, width), BF),
            pltpu.HBM((length, 3 * part), BF),
            pltpu.HBM((part // head_dim, length, length), BF),
            pltpu.HBM((n_dp, rows, part), BF),
            ((8, width), F32),
            ((width, 128), BF),
        ],
        bias, *far(*qkv_blocks, *sum(token_blocks, [])),
        scratch=[pltpu.VMEM((width, cols), BF)],
        counts=[len(b) for b in token_blocks], n_ex=n_ex, head_dim=head_dim, experts=experts,
    )
    early = list(range(1, n_dp - 1))
    att_out, *came = lax.optimization_barrier((att_out, *[grads[k][0] for k in early]))
    for k, block in zip(early, came):
        grads[k] = [block]
    attended = swap(att_out, "dp")
    proj = call(assemble_kernel, [pltpu.HBM((n_dp, n_ex, own, width), BF)], *proj_blocks)[0].reshape(width, width)
    mixed, normed2, p, sent = call(
        mix_kernel,
        [pltpu.HBM((rows, width), F32), pltpu.HBM((rows, width), BF), pltpu.HBM((rows, 128), F32), pltpu.HBM((n_ex * pad, width), BF)],
        *far(x), attended, *far(proj), small, vectors, *far(tableT),
        experts=experts,
    )
    mine = dispatch(sent)
    grads = lax.optimization_barrier(grads)
    def expert(slots, k):
        return expert_call(
            small, up_weight[0], down_weight[0], up_bias, down_bias, slots, grads[k], n_dp, experts
        )

    done = {0: expert([mine], 0)}

    def after_own(block):
        block, done[0] = lax.optimization_barrier((block, done[0]))
        return block

    slots = spread(mine, after_own)
    came = [done[0][0]] + [None] * (n_dp - 1)
    last = 0
    for k in [2, 1, 3] if n_dp == 4 else range(1, n_dp):
        slots[k], done[last] = lax.optimization_barrier((slots[k], done[last]))
        done[k] = expert(slots[k], k)
        came[k] = across(done[k][0], k)
        last = k
    came[0] = done[0][0]
    all_slots, act, d_pre, d_rows, g_up_bias = ([done[k][i] for k in range(n_dp)] for i in range(1, 6))
    grad_up, grad_down, grad_up_bias, grad_down_bias = expert_grads(
        all_slots, act, d_pre, d_rows, g_up_bias, part
    )
    grad_up, grad_down, *came = lax.optimization_barrier((grad_up, grad_down, *came))
    summed = call(line_sum_kernel, [pltpu.HBM((n_ex * pair, width), BF)], *far(line_picks(n_ex, pair, capacity)), *came)[0]
    back = swap(summed.reshape(n_ex, pair, width), "expert").reshape(n_ex * pair, width)
    outputs, d_mixed, d_low, d_att, d_logits, sums = call(
        combine_kernel,
        [
            pltpu.HBM((rows, width), BF),
            pltpu.HBM((rows, width), F32),
            ((rows, width), BF),
            pltpu.HBM((n_dp, rows, part), BF),
            pltpu.HBM((rows, 128), BF),
            pltpu.HBM((8, width), F32),
        ],
        back, *far(route, rank, mixed, p, cotangent[0]), small, vectors, *far(proj),
        pair=pair, capacity=capacity, experts=experts, part=part,
    )
    d_heads = swap(d_att, "dp")
    half = n_ex // 2
    near, keep = call(
        proj_grad_kernel,
        [pltpu.HBM((half, n_dp, own, width), BF), ((half, n_dp, own, width), BF)],
        *far(attended), d_low,
        scratch=[pltpu.VMEM((width, width), F32)],
    )
    d_heads, *parts = lax.optimization_barrier((d_heads, *core_sum(near, keep)))
    proj_chips = to_chips(parts)
    d_packed, d_normed = call(
        attend_back_kernel,
        [((length, 3 * part), BF), pltpu.HBM((n_dp, rows, width), BF)],
        d_heads, *far(probs, packed, *qkv_blocks),
        scratch=[pltpu.VMEM((length, length), BF), pltpu.VMEM((width, cols), BF)],
        head_dim=head_dim,
    )
    d_packed, *proj_chips = lax.optimization_barrier((d_packed, *proj_chips))
    near, keep = call(
        qkv_grad_kernel,
        [pltpu.HBM((half, n_dp, own, cols), BF), ((half, n_dp, own, cols), BF)],
        *far(normed1), vectors, d_packed, *far(d_normed, normed2, d_logits, sums),
        scratch=[pltpu.VMEM((width, cols), F32), pltpu.VMEM((128, width), F32)],
        experts=experts,
    )
    near, d_normed = lax.optimization_barrier((near, d_normed))
    d_own = swap(d_normed, "dp")
    qkv_chips = to_chips(core_sum(near, keep))
    summed = call(
        chip_sum_kernel, [pltpu.HBM((own, cols + width), BF)] * n_dp, *qkv_chips, *proj_chips,
        scratch=[pltpu.VMEM((n_dp, own, cols + width), BF)], n_dp=n_dp,
    )
    summed = along(summed)
    d_own, summed[1] = lax.optimization_barrier((d_own, summed[1]))
    owned_qkv, owned_proj, owned_router, owned_gains, owned_biases = call(
        weights_end_kernel,
        [
            pltpu.HBM((own, 3 * width), F32),
            pltpu.HBM((own, width), F32),
            pltpu.HBM((experts, own), F32),
            pltpu.HBM((2, own), F32),
            pltpu.HBM((5, own), F32),
        ],
        *summed,
        scratch=[pltpu.VMEM((128, 128), F32), pltpu.VMEM((n_dp, own, cols + width), BF)],
    )
    grad_tokens = call(tokens_end_kernel, [pltpu.HBM((rows, width), F32)], d_own, *far(x), vectors, *far(d_mixed))[0]
    return (
        outputs[None],
        grad_tokens[None],
        owned_qkv,
        owned_proj,
        owned_router.T,
        owned_gains,
        owned_biases,
        grad_up[None],
        grad_up_bias,
        grad_down[None],
        grad_down_bias,
    )


def solution(mesh):
    line = P(("dp", "expert"), None)
    across = P(None, ("dp", "expert"))
    act = P("expert", "dp", None)
    return jax.shard_map(
        shards,
        mesh=mesh,
        in_specs=(
            act,
            line,
            line,
            line,
            across,
            across,
            P("expert", None, "dp"),
            P("expert", "dp"),
            act,
            P("expert", "dp"),
            act,
            act,
            P("expert", None),
            P("expert", None),
            act,
        ),
        out_specs=(
            act,
            act,
            line,
            line,
            line,
            across,
            across,
            P("expert", None, "dp"),
            P("expert", "dp"),
            act,
            P("expert", "dp"),
        ),
        check_vma=False,
    )
```

```python
import functools

import jax
import jax.numpy as jnp
import numpy as np
from jax import lax
from jax.experimental import pallas as pl
from jax.experimental.pallas import tpu as pltpu
from jax.sharding import PartitionSpec as P

H = 16
NSEG = 7
EPS = 1e-05
NEG = -1e30
BF = jnp.bfloat16
F32 = jnp.float32
I32 = jnp.int32


def mm(a, b, ca=1, cb=0):
    return lax.dot_general(a, b, (((ca,), (cb,)), ((), ())), preferred_element_type=F32)


def placed(kernel):
    def body(*refs):
        kernel((lax.axis_index("dp"), lax.axis_index("expert")), *refs)

    return body


PARAMS = pltpu.CompilerParams(vmem_limit_bytes=24 << 20)


def far(*arrays):
    return [pltpu.with_memory_space_constraint(x, pltpu.HBM) for x in arrays]


def call(kernel, outs, *args, scratch=(), **static):
    vmem = pl.BlockSpec(memory_space=pltpu.VMEM)
    return pl.pallas_call(
        placed(functools.partial(kernel, **static)),
        out_shape=[o if isinstance(o, pl.MemoryRef) else jax.ShapeDtypeStruct(*o) for o in outs],
        in_specs=[vmem] * len(args),
        out_specs=[vmem] * len(outs),
        scratch_shapes=list(scratch),
        compiler_params=PARAMS,
        name=kernel.__name__,
    )(*args)


def ahead(x, step):
    n = lax.axis_size("dp")
    return lax.ppermute(x, "dp", [(i, (i + step) % n) for i in range(n)])


def flip(x, bits):
    n = lax.axis_size("expert")
    return lax.ppermute(x, "expert", [(i, i ^ bits) for i in range(n)])


def swap(x, axis):
    return lax.all_to_all(x, axis, split_axis=0, concat_axis=0, tiled=True)


def along(blocks, sign=1):
    return [blocks[0]] + [ahead(blocks[j], sign * j) for j in range(1, len(blocks))]


def across(x, bits):
    n = lax.axis_size("dp")
    return lax.ppermute(x, "dp", [(i, i ^ bits) for i in range(n)])


def spread(x, hold=None):
    n = lax.axis_size("dp")
    out = [[x]] + [[across(x, k)] for k in range(1, n - 1)]
    if n != 4:
        return out + [[across(x, n - 1)]]
    own = lax.ppermute(x, "dp", [(1, 2), (2, 1)])
    if hold is not None:
        out[2] = [hold(out[2][0])]
    return out + [[own, lax.ppermute(out[2][0], "dp", [(1, 0), (2, 3)])]]


def added(refs):
    return refs[0][...] if len(refs) == 1 else refs[0][...] + refs[1][...]


def split(refs, counts):
    out, at = [], 0
    for count in counts:
        out.append(refs[at : at + count])
        at += count
    return out


def gather_experts(x):
    n = lax.axis_size("expert")
    mine = [x] + [flip(x, 2 * k) for k in range(1, n // 2)]
    out = []
    for block in mine:
        out += [block, flip(block, 1)]
    return out


def normalise(values):
    mean = jnp.mean(values, axis=-1, keepdims=True)
    centred = values - mean
    scale = lax.rsqrt(jnp.mean(centred * centred, axis=-1, keepdims=True) + EPS)
    return centred * scale, scale


def norm_back(upstream, gain, unit, scale):
    e = upstream * gain
    return scale * (
        e - jnp.mean(e, axis=-1, keepdims=True) - unit * jnp.mean(e * unit, axis=-1, keepdims=True)
    )


def lanes(shape, dim):
    return lax.broadcasted_iota(I32, shape, dim)


def softmax_of(logits, experts):
    logits = jnp.where(lanes(logits.shape, 1) < experts, logits, NEG)
    top = jnp.max(logits, axis=-1, keepdims=True)
    weight = jnp.exp(logits - top)
    return weight / jnp.sum(weight, axis=-1, keepdims=True)


def weights_kernel(me, qkv, proj, router, gains, biases, out, rows, turned, *, n_dp):
    own, width = qkv.shape[0], qkv.shape[1] // 3
    part = width // n_dp
    experts = router.shape[0]
    turned[...] = jnp.zeros_like(turned)
    turned[:experts, :own] = router[...].astype(F32)
    turned[experts : experts + 2, :own] = gains[...].astype(F32)
    turned[experts + 2 : experts + 7, :own] = biases[...].astype(F32)
    small = turned[...].T[:own].astype(BF)
    for d in range(n_dp):
        for i in range(3):
            out[d, :, i * part : (i + 1) * part] = qkv[
                :, i * width + d * part : i * width + (d + 1) * part
            ]
        out[d, :, 3 * part :] = small
        rows[d] = proj[...]


def slots_kernel(
    me, parents, route, order, cotangent, seg, grads, tableT, route_out, rank_out, bias, *, pad, capacity, experts
):
    tok = route.shape[1]
    rt = jnp.broadcast_to(route[...].astype(F32), (tok, tok))
    r = rt.T
    route_out[...] = r[:, 0:1].astype(I32)
    o = jnp.broadcast_to(order[...].astype(F32), (tok, tok))
    ot = o.T
    same = r == rt
    rank = jnp.sum(jnp.where(same & (o < ot), 1.0, 0.0), axis=1, keepdims=True)
    rank_row = jnp.sum(jnp.where(same & (ot < o), 1.0, 0.0), axis=0, keepdims=True)
    rank_out[...] = rank.astype(I32)
    key = jnp.where(rank_row < capacity, rt[0:1] * pad + rank_row, -1.0).astype(I32)
    table = jnp.where(lanes((experts * pad, tok), 0) == key, 1.0, 0.0).astype(BF)
    tableT[...] = table
    grads[...] = mm(table, cotangent[...]).astype(BF)
    length = seg.shape[1]
    masks = [jnp.int32(1)]
    for s in range(1, NSEG):
        up = jnp.int32(0)
        for a in range(s):
            up = jnp.where(parents[0, s] == a, masks[a], up)
        masks.append(up | (1 << s))
    block = 128
    mine = jnp.zeros((1, length), I32)
    for s in range(NSEG):
        mine = jnp.where(seg[...] == s, masks[s], mine)
    for i in range(length // block):
        col = jnp.broadcast_to(seg[:, i * block : (i + 1) * block].astype(F32), (block, block)).T
        bit = jnp.left_shift(1, jnp.broadcast_to(col[:, 0:1], (block, length)).astype(I32))
        seen = lanes((block, length), 0) + i * block <= lanes((block, length), 1)
        bias[i * block : (i + 1) * block] = jnp.where(seen & ((mine & bit) != 0), 0.0, NEG).astype(BF)


def pack_kernel(me, pick, rows, out):
    out[...] = mm(pick[...], rows[...]).astype(BF)


def pack_picks(n_ex, pad, capacity):
    pick = np.zeros((n_ex * capacity, n_ex * pad), np.float32)
    for e in range(n_ex):
        for c in range(capacity):
            pick[e * capacity + c, e * pad + c] = 1
    return jnp.asarray(pick, BF)


def line_picks(n_ex, pair, capacity):
    pick = np.zeros((n_ex * pair, 2 * n_ex * capacity), np.float32)
    for e in range(n_ex):
        for w in range(2):
            for c in range(capacity):
                pick[e * pair + w * capacity + c, (w * n_ex + e) * capacity + c] = 1
    return jnp.asarray(pick, BF)


def assemble_kernel(me, *refs):
    out = refs[-1]
    for k, block in enumerate(refs[:-1]):
        e = me[1] ^ k
        for d in range(block.shape[0]):
            out[d, e] = block[d]


def assembled(me, blocks, whole):
    own = blocks[0].shape[1]
    n_ex = len(blocks)
    for k, block in enumerate(blocks):
        for d in range(block.shape[0]):
            row = pl.multiple_of((d * n_ex + (me[1] ^ k)) * own, own)
            whole[pl.ds(row, own)] = block[d]


def attend_kernel(me, bias, *refs, counts, n_ex, head_dim, experts):
    blocks, refs = refs[:n_ex], refs[n_ex:]
    tokens, (normed, packed, probs, attended, vectors, small, qkv) = split(refs, counts), refs[-7:]
    n_dp = len(counts)
    rows, width = tokens[0][0].shape
    part = width // n_dp
    assembled(me, blocks, qkv)
    few = qkv[:, 3 * part :]
    small[...] = few
    vectors[...] = few.astype(F32).T[experts : experts + 8]
    gain, shift = vectors[0:1], vectors[2:3]
    parts = [jnp.zeros((1, part), F32)] * 2
    for d in range(n_dp):
        for i in range(2):
            here = vectors[3 + i : 4 + i, d * part : (d + 1) * part]
            parts[i] = parts[i] + jnp.where(me[0] == d, here, 0.0)

    for k, blocks in enumerate(tokens):
        base = pl.multiple_of((me[0] ^ k) * rows, rows)
        unit, _ = normalise(added(blocks).astype(F32))
        normed[pl.ds(base, rows)] = (unit * gain + shift).astype(BF)

    raw = mm(normed[...], qkv[:, : 3 * part])
    packed[:, :part] = (raw[:, :part] + parts[0]).astype(BF)
    packed[:, part : 2 * part] = raw[:, part : 2 * part].astype(BF)
    packed[:, 2 * part :] = (raw[:, 2 * part :] + parts[1]).astype(BF)
    scale = head_dim ** (-0.5)
    for h in range(part // head_dim):
        q = packed[:, h * head_dim : (h + 1) * head_dim]
        k = packed[:, part + h * head_dim : part + (h + 1) * head_dim]
        vt = packed[:, 2 * part + h * head_dim : 2 * part + (h + 1) * head_dim].T
        for i in range(0, n_dp, 2):
            lo, hi = i * rows, (i + 2) * rows
            s = mm(k[:hi], q[lo:hi], 1, 1) * scale + bias[:hi, lo:hi].astype(F32)
            p = jnp.exp(s - jnp.max(s, axis=0, keepdims=True))
            p = (p * (1.0 / jnp.sum(p, axis=0, keepdims=True))).astype(BF)
            probs[h, :hi, lo:hi] = p
            out = mm(vt[:, :hi], p).T.astype(BF)
            attended[i, :, h * head_dim : (h + 1) * head_dim] = out[:rows]
            attended[i + 1, :, h * head_dim : (h + 1) * head_dim] = out[rows:]


def mix_kernel(me, tokens, attended, proj, small, vectors, tableT, mixed, normed, p, sent, *, experts):
    n_dp, rows, part = attended.shape
    total = tokens[...].astype(F32) + vectors[5:6]
    for d in range(n_dp):
        total = total + mm(attended[d], proj[d * part : (d + 1) * part])
    mixed[...] = total
    unit, _ = normalise(total)
    low = (unit * vectors[1:2] + vectors[6:7]).astype(BF)
    normed[...] = low
    p[...] = softmax_of(mm(low, small[...]), experts)
    sent[...] = mm(tableT[...], low).astype(BF)


def expert_kernel(
    me, small, up, down, up_bias, down_bias, *refs, counts, n_dp, experts
):
    came, grads, (both, slots, act_out, d_pre_out, d_rows, g_up_bias, acc_r, acc_s) = split(refs, [*counts, 8])
    f = pl.program_id(0)
    each, width = slots.shape
    part = width // n_dp

    @pl.when(f == 0)
    def _():
        slots[...] = added(came)
        p = softmax_of(mm(slots[...], small[...]), experts)
        gate = jnp.sum(jnp.where(lanes(p.shape, 1) == me[1], p, 0.0), axis=-1, keepdims=True)
        d_rows[...] = (gate * added(grads).astype(F32)).astype(BF)
        acc_s[...] = jnp.zeros_like(acc_s)
        for d in range(n_dp):
            acc_r[:, d * part : (d + 1) * part] = jnp.broadcast_to(
                jnp.where(me[0] == d, down_bias[...].astype(F32), 0.0), (each, part)
            )

    u = mm(slots[...], up[...]) + up_bias[...].astype(F32)
    c, a = 0.7978845608028654, 0.044715
    t = jnp.tanh(c * (u + a * (u * u * u)))
    act = (0.5 * u * (1.0 + t)).astype(BF)
    slope = 0.5 * (1.0 + t) + 0.5 * u * (1.0 - t * t) * (c * (1.0 + 3.0 * a * (u * u)))
    d_pre = mm(d_rows[...], down[...], 1, 1) * slope
    g_up_bias[...] = jnp.sum(d_pre, axis=0, keepdims=True)
    low = d_pre.astype(BF)
    act_out[...] = act
    d_pre_out[...] = low
    acc_r[...] += mm(act, down[...])
    acc_s[...] += mm(low, up[...], 1, 1)

    @pl.when(f == pl.num_programs(0) - 1)
    def _():
        both[:each] = acc_r[...].astype(BF)
        both[each:] = acc_s[...].astype(BF)


def expert_call(small, up, down, up_bias, down_bias, slots, grads, n_dp, experts):
    each, width = slots[0].shape
    ff = up.shape[1]
    chunk = min(ff, 256)
    whole = pl.BlockSpec(memory_space=pltpu.VMEM)
    wide = pl.BlockSpec((each, chunk), lambda f: (0, f))
    row = pl.BlockSpec((1, chunk), lambda f: (0, f))
    return pl.pallas_call(
        placed(
            functools.partial(
                expert_kernel, counts=(len(slots), len(grads)), n_dp=n_dp, experts=experts
            )
        ),
        grid=(ff // chunk,),
        out_shape=[
            pltpu.HBM((2 * each, width), BF),
            jax.ShapeDtypeStruct((each, width), BF),
            jax.ShapeDtypeStruct((each, ff), BF),
            jax.ShapeDtypeStruct((each, ff), BF),
            jax.ShapeDtypeStruct((each, width), BF),
            jax.ShapeDtypeStruct((1, ff), F32),
        ],
        in_specs=[
            whole,
            pl.BlockSpec((width, chunk), lambda f: (0, f)),
            pl.BlockSpec((chunk, width), lambda f: (f, 0)),
            row,
            whole,
        ]
        + [whole] * (len(slots) + len(grads)),
        out_specs=[whole, whole, wide, wide, whole, row],
        scratch_shapes=[pltpu.VMEM((each, width), F32), pltpu.VMEM((each, width), F32)],
        compiler_params=PARAMS,
        name="expert_kernel",
    )(small, up, down, up_bias, down_bias, *slots, *grads)


def expert_grad_kernel(me, *refs, n_dp):
    slots, act, d_pre, d_rows, up_bias = (refs[i * n_dp : (i + 1) * n_dp] for i in range(5))
    grad_up, grad_down, g_up_bias, g_down_bias = refs[5 * n_dp :]
    grad_up[...] = sum(mm(a[...], b[...], 0, 0) for a, b in zip(slots, d_pre))
    grad_down[...] = sum(mm(a[...], b[...], 0, 0) for a, b in zip(act, d_rows))

    @pl.when(pl.program_id(0) == 0)
    def _():
        g_up_bias[...] = sum_of(up_bias)
        sums = sum(jnp.sum(r[...].astype(F32), axis=0, keepdims=True) for r in d_rows)
        part = g_down_bias.shape[1]
        own = jnp.zeros((1, part), F32)
        for d in range(n_dp):
            own = own + jnp.where(me[0] == d, sums[:, d * part : (d + 1) * part], 0.0)
        g_down_bias[...] = own


def expert_grads(slots, act, d_pre, d_rows, up_bias, part):
    n_dp = len(slots)
    each, width = slots[0].shape
    ff = act[0].shape[1]
    steps = 4
    whole = pl.BlockSpec(memory_space=pltpu.VMEM)
    return pl.pallas_call(
        placed(functools.partial(expert_grad_kernel, n_dp=n_dp)),
        grid=(steps,),
        out_shape=[
            pltpu.HBM((width, ff), F32),
            pltpu.HBM((ff, width), F32),
            jax.ShapeDtypeStruct((1, ff), F32),
            jax.ShapeDtypeStruct((1, part), F32),
        ],
        in_specs=[pl.BlockSpec((each, width // steps), lambda f: (0, f))] * n_dp
        + [pl.BlockSpec((each, ff // steps), lambda f: (0, f))] * n_dp
        + [whole] * (3 * n_dp),
        out_specs=[
            pl.BlockSpec((width // steps, ff), lambda f: (f, 0)),
            pl.BlockSpec((ff // steps, width), lambda f: (f, 0)),
            whole,
            whole,
        ],
        compiler_params=PARAMS,
        name="expert_grad_kernel",
    )(*slots, *act, *d_pre, *d_rows, *up_bias)


def sum_of(refs):
    total = refs[0][...].astype(F32)
    for ref in refs[1:]:
        total = total + ref[...].astype(F32)
    return total


def line_sum_kernel(me, pick, *refs):
    refs[-1][...] = mm(pick[...], sum_of(refs[:-1]).astype(BF)).astype(BF)


def combine_kernel(
    me, back, route, rank, mixed, p, cotangent, small, vectors, proj,
    outputs, d_mixed, d_low_out, d_att, d_logits_out, sums, *, pair, capacity, experts, part,
):
    tok, width = mixed.shape
    n_back = back.shape[0]
    r, k = route[...], rank[...]
    key = jnp.where(k < capacity, r * pair + k, -2 * pair * experts)
    slot = lanes((tok, n_back), 1)
    combined = mm(jnp.where(slot == key, 1.0, 0.0).astype(BF), back[...])
    d_slot = mm(jnp.where(slot == key + capacity, 1.0, 0.0).astype(BF), back[...])
    hot = jnp.where(lanes(p.shape, 1) == r, 1.0, 0.0)
    gate = jnp.sum(p[...] * hot, axis=-1, keepdims=True)
    g = cotangent[...].astype(F32)
    outputs[...] = (mixed[...] + gate * combined).astype(BF)
    d_gate = jnp.sum(g * combined, axis=-1, keepdims=True)
    d_logits = (p[...] * (d_gate * hot - d_gate * gate)).astype(BF)
    d_logits_out[...] = d_logits
    d_normed = d_slot + mm(d_logits, small[...], 1, 1)
    unit, scale = normalise(mixed[...])
    sums[0:1] = jnp.sum(d_normed * unit, axis=0, keepdims=True)
    sums[1:2] = jnp.sum(d_normed, axis=0, keepdims=True)
    d = g + norm_back(d_normed, vectors[1:2], unit, scale)
    sums[2:3] = jnp.sum(d, axis=0, keepdims=True)
    d_mixed[...] = d
    low = d.astype(BF)
    d_low_out[...] = low
    for i in range(d_att.shape[0]):
        d_att[i] = mm(low, proj[i * part : (i + 1) * part], 1, 1).astype(BF)


def share(me, whole, near, keep):
    half, n_dp, own, _ = near.shape
    for q in range(half):
        for d in range(n_dp):
            row = d * 2 * half * own
            other = pl.multiple_of(row + (me[1] ^ (2 * q + 1)) * own, own)
            same = pl.multiple_of(row + (me[1] ^ (2 * q)) * own, own)
            near[q, d] = whole[pl.ds(other, own)].astype(BF)
            keep[q, d] = whole[pl.ds(same, own)].astype(BF)


def proj_grad_kernel(me, attended, d_low, near, keep, whole):
    n_dp, rows, part = attended.shape
    for d in range(n_dp):
        whole[d * part : (d + 1) * part] = mm(attended[d], d_low[...], 0, 0)
    share(me, whole, near, keep)


def core_sum_kernel(me, keep, came, first, *rest):
    for q, out in enumerate([first, *rest]):
        out[...] = (keep[q].astype(F32) + came[q].astype(F32)).astype(BF)


def chip_sum_kernel(me, *refs, n_dp):
    outs, total = refs[-1 - n_dp : -1], refs[-1]
    parts = refs[: -1 - n_dp]
    half = len(parts) // 2
    wide = parts[0].shape[2]
    total[:, :, :wide] = sum_of(parts[:half]).astype(BF)
    total[:, :, wide:] = sum_of(parts[half:]).astype(BF)
    for j in range(n_dp):
        outs[j][...] = total[(me[0] + j) % n_dp]


def core_sum(near, keep):
    half = near.shape[0]
    shape = near.shape[1:]
    return call(core_sum_kernel, [(shape, BF)] + [pltpu.HBM(shape, BF)] * (half - 1), keep, flip(near, 1))


def to_chips(parts):
    return [parts[0]] + [flip(part, 2 * (q + 1)) for q, part in enumerate(parts[1:])]


def attend_back_kernel(me, d_att, probs, packed, *refs, head_dim):
    blocks, (d_packed, d_normed, d_scores, qkv) = refs[:-4], refs[-4:]
    n_dp, rows, part = d_att.shape
    scale = head_dim ** (-0.5)
    assembled(me, blocks, qkv)
    for h in range(part // head_dim):
        a, b = h * head_dim, (h + 1) * head_dim
        q, k, v = packed[:, a:b], packed[:, part + a : part + b], packed[:, 2 * part + a : 2 * part + b]
        kt = k.T
        g = jnp.concatenate([d_att[i, :, a:b] for i in range(n_dp)], axis=0)
        for i in range(0, n_dp, 2):
            lo, hi = i * rows, (i + 2) * rows
            dp = mm(v[:hi], g[lo:hi], 1, 1)
            p = probs[h, :hi, lo:hi].astype(F32)
            delta = jnp.sum(p * dp, axis=0, keepdims=True)
            ds = (p * (dp - delta)).astype(BF)
            d_scores[:hi, lo:hi] = ds
            d_packed[lo:hi, a:b] = (mm(kt[:, :hi], ds).T * scale).astype(BF)
        for i in range(0, n_dp, 2):
            lo, hi = i * rows, (i + 2) * rows
            d_packed[lo:hi, part + a : part + b] = (mm(d_scores[lo:hi, lo:], q[lo:]) * scale).astype(BF)
            d_packed[lo:hi, 2 * part + a : 2 * part + b] = mm(probs[h, lo:hi, lo:], g[lo:]).astype(BF)
    for i in range(n_dp):
        d_normed[i] = mm(d_packed[i * rows : (i + 1) * rows], qkv[:, : 3 * part], 1, 1).astype(BF)


def qkv_grad_kernel(
    me, normed, vectors, d_packed, d_normed, token_normed, d_logits, sums, near, keep, whole, turned, *, experts
):
    n_dp, rows, width = d_normed.shape
    part = width // n_dp
    whole[:, : 3 * part] = mm(normed[...], d_packed[...], 0, 0)
    gain = jnp.zeros((1, width), F32)
    shift = jnp.zeros((1, width), F32)
    for i in range(n_dp):
        d = d_normed[i].astype(F32)
        gain = gain + jnp.sum(d * normed[i * rows : (i + 1) * rows].astype(F32), axis=0, keepdims=True)
        shift = shift + jnp.sum(d, axis=0, keepdims=True)
    gain = (gain - vectors[2:3] * shift) / vectors[0:1]
    columns = jnp.sum(d_packed[...].astype(F32), axis=0, keepdims=True)
    turned[...] = jnp.zeros_like(turned)
    e = experts
    turned[e : e + 1] = gain
    turned[e + 1 : e + 2] = sums[0:1]
    turned[e + 2 : e + 3] = shift
    for d in range(n_dp):
        here = me[0] == d
        turned[e + 3 : e + 4, d * part : (d + 1) * part] = jnp.where(here, columns[:, :part], 0.0)
        turned[e + 4 : e + 5, d * part : (d + 1) * part] = jnp.where(here, columns[:, 2 * part :], 0.0)
    turned[e + 5 : e + 6] = sums[2:3]
    turned[e + 6 : e + 7] = sums[1:2]
    whole[:, 3 * part :] = turned[...].T + mm(token_normed[...], d_logits[...], 0, 0)
    share(me, whole, near, keep)


def weights_end_kernel(me, *refs):
    (qkv, proj, router, gains, biases, wide, came), blocks = refs[-7:], refs[:-7]
    n_dp, own, _ = came.shape
    for j in range(n_dp):
        came[(me[0] + n_dp - j) % n_dp] = blocks[j][...]
    width = proj.shape[1]
    part = width // n_dp
    experts = router.shape[0]
    edge = 3 * part
    total = jnp.zeros((own, 128), F32)
    rows = jnp.zeros((own, width), F32)
    for d in range(n_dp):
        for i in range(3):
            qkv[:, i * width + d * part : i * width + (d + 1) * part] = came[
                d, :, i * part : (i + 1) * part
            ].astype(F32)
        total = total + came[d, :, edge : edge + 128].astype(F32)
        rows = rows + came[d, :, edge + 128 :].astype(F32)
    proj[...] = rows
    wide[...] = jnp.zeros_like(wide)
    wide[:own] = total
    flat = wide[...].T
    router[...] = flat[:experts, :own]
    gains[...] = flat[experts : experts + 2, :own]
    biases[...] = flat[experts + 2 : experts + 7, :own]


def tokens_end_kernel(me, came, tokens, vectors, d_mixed, out):
    total = came[0].astype(F32)
    for d in range(1, came.shape[0]):
        total = total + came[d].astype(F32)
    unit, scale = normalise(tokens[...].astype(F32))
    out[...] = d_mixed[...] + norm_back(total, vectors[0:1], unit, scale)


def shards(
    tokens,
    qkv_weight,
    proj_weight,
    router_weight,
    norm_gains,
    biases,
    up_weight,
    up_bias,
    down_weight,
    down_bias,
    routes,
    slot_order,
    segments,
    parents,
    cotangent,
):
    n_dp, n_ex = lax.axis_size("dp"), lax.axis_size("expert")
    rows, width = tokens.shape[1], tokens.shape[2]
    part = width // n_dp
    head_dim = width // H
    own = qkv_weight.shape[0]
    experts = router_weight.shape[1]
    capacity = (9 * rows + 8 * experts - 1) // (8 * experts)
    pad = -(-capacity // 8) * 8
    pair = -(-capacity // 4) * 8
    length = n_dp * rows
    each = n_ex * capacity
    cols = 3 * part + 128
    x = tokens[0]

    token_blocks = spread(x)
    columns, proj_rows = call(
        weights_kernel,
        [pltpu.HBM((n_dp, own, cols), BF), pltpu.HBM((n_dp, own, width), BF)],
        *far(qkv_weight, proj_weight, router_weight.T, norm_gains, biases),
        scratch=[pltpu.VMEM((128, 128), F32)],
        n_dp=n_dp,
    )
    qkv_blocks = gather_experts(swap(columns, "dp"))
    smem = pl.BlockSpec(memory_space=pltpu.SMEM)
    vmem = pl.BlockSpec(memory_space=pltpu.VMEM)
    grads_out, tableT, route, rank, bias = pl.pallas_call(
        placed(functools.partial(slots_kernel, pad=pad, capacity=capacity, experts=experts)),
        out_shape=[
            pltpu.HBM((n_ex * pad, width), BF),
            pltpu.HBM((n_ex * pad, rows), BF),
            pltpu.HBM((rows, 1), I32),
            pltpu.HBM((rows, 1), I32),
            jax.ShapeDtypeStruct((length, length), BF),
        ],
        in_specs=[smem] + [vmem] * 4,
        out_specs=[vmem] * 5,
        compiler_params=PARAMS,
        name="slots_kernel",
    )(parents, *far(routes.reshape(1, rows), slot_order[0], cotangent[0], segments))

    def dispatch(rows_out):
        came = swap(rows_out.reshape(n_ex, pad, width), "expert").reshape(n_ex * pad, width)
        mine = call(pack_kernel, [pltpu.HBM((each, width), BF)], *far(pack_picks(n_ex, pad, capacity)), came)[0]
        return mine

    grads_in = dispatch(grads_out)
    proj_blocks = gather_experts(swap(proj_rows, "dp"))
    grads_in, bias = lax.optimization_barrier((grads_in, bias))
    grads = spread(grads_in)
    normed1, packed, probs, att_out, vectors, small = call(
        attend_kernel,
        [
            pltpu.HBM((length, width), BF),
            pltpu.HBM((length, 3 * part), BF),
            pltpu.HBM((part // head_dim, length, length), BF),
            pltpu.HBM((n_dp, rows, part), BF),
            ((8, width), F32),
            ((width, 128), BF),
        ],
        bias, *far(*qkv_blocks, *sum(token_blocks, [])),
        scratch=[pltpu.VMEM((width, cols), BF)],
        counts=[len(b) for b in token_blocks], n_ex=n_ex, head_dim=head_dim, experts=experts,
    )
    early = list(range(1, n_dp - 1))
    att_out, *came = lax.optimization_barrier((att_out, *[grads[k][0] for k in early]))
    for k, block in zip(early, came):
        grads[k] = [block]
    attended = swap(att_out, "dp")
    proj = call(assemble_kernel, [pltpu.HBM((n_dp, n_ex, own, width), BF)], *proj_blocks)[0].reshape(width, width)
    mixed, normed2, p, sent = call(
        mix_kernel,
        [pltpu.HBM((rows, width), F32), pltpu.HBM((rows, width), BF), pltpu.HBM((rows, 128), F32), pltpu.HBM((n_ex * pad, width), BF)],
        *far(x), attended, *far(proj), small, vectors, *far(tableT),
        experts=experts,
    )
    mine = dispatch(sent)
    grads = lax.optimization_barrier(grads)
    def expert(slots, k):
        return expert_call(
            small, up_weight[0], down_weight[0], up_bias, down_bias, slots, grads[k], n_dp, experts
        )

    done = {0: expert([mine], 0)}

    def after_own(block):
        block, done[0] = lax.optimization_barrier((block, done[0]))
        return block

    slots = spread(mine, after_own)
    came = [done[0][0]] + [None] * (n_dp - 1)
    last = 0
    for k in [2, 1, 3] if n_dp == 4 else range(1, n_dp):
        if last != 1:
            slots[k], done[last] = lax.optimization_barrier((slots[k], done[last]))
        done[k] = expert(slots[k], k)
        came[k] = across(done[k][0], k)
        last = k
    came[0] = done[0][0]
    all_slots, act, d_pre, d_rows, g_up_bias = ([done[k][i] for k in range(n_dp)] for i in range(1, 6))
    grad_up, grad_down, grad_up_bias, grad_down_bias = expert_grads(
        all_slots, act, d_pre, d_rows, g_up_bias, part
    )
    grad_up, grad_down, *came = lax.optimization_barrier((grad_up, grad_down, *came))
    summed = call(line_sum_kernel, [pltpu.HBM((n_ex * pair, width), BF)], *far(line_picks(n_ex, pair, capacity)), *came)[0]
    back = swap(summed.reshape(n_ex, pair, width), "expert").reshape(n_ex * pair, width)
    outputs, d_mixed, d_low, d_att, d_logits, sums = call(
        combine_kernel,
        [
            pltpu.HBM((rows, width), BF),
            pltpu.HBM((rows, width), F32),
            ((rows, width), BF),
            pltpu.HBM((n_dp, rows, part), BF),
            pltpu.HBM((rows, 128), BF),
            pltpu.HBM((8, width), F32),
        ],
        back, *far(route, rank, mixed, p, cotangent[0]), small, vectors, *far(proj),
        pair=pair, capacity=capacity, experts=experts, part=part,
    )
    d_heads = swap(d_att, "dp")
    half = n_ex // 2
    near, keep = call(
        proj_grad_kernel,
        [pltpu.HBM((half, n_dp, own, width), BF), ((half, n_dp, own, width), BF)],
        *far(attended), d_low,
        scratch=[pltpu.VMEM((width, width), F32)],
    )
    d_heads, *parts = lax.optimization_barrier((d_heads, *core_sum(near, keep)))
    proj_chips = to_chips(parts)
    d_packed, d_normed = call(
        attend_back_kernel,
        [((length, 3 * part), BF), pltpu.HBM((n_dp, rows, width), BF)],
        d_heads, *far(probs, packed, *qkv_blocks),
        scratch=[pltpu.VMEM((length, length), BF), pltpu.VMEM((width, cols), BF)],
        head_dim=head_dim,
    )
    d_packed, *proj_chips = lax.optimization_barrier((d_packed, *proj_chips))
    near, keep = call(
        qkv_grad_kernel,
        [pltpu.HBM((half, n_dp, own, cols), BF), ((half, n_dp, own, cols), BF)],
        *far(normed1), vectors, d_packed, *far(d_normed, normed2, d_logits, sums),
        scratch=[pltpu.VMEM((width, cols), F32), pltpu.VMEM((128, width), F32)],
        experts=experts,
    )
    near, d_normed = lax.optimization_barrier((near, d_normed))
    d_own = swap(d_normed, "dp")
    qkv_chips = to_chips(core_sum(near, keep))
    summed = call(
        chip_sum_kernel, [pltpu.HBM((own, cols + width), BF)] * n_dp, *qkv_chips, *proj_chips,
        scratch=[pltpu.VMEM((n_dp, own, cols + width), BF)], n_dp=n_dp,
    )
    summed = along(summed)
    d_own, summed[1] = lax.optimization_barrier((d_own, summed[1]))
    owned_qkv, owned_proj, owned_router, owned_gains, owned_biases = call(
        weights_end_kernel,
        [
            pltpu.HBM((own, 3 * width), F32),
            pltpu.HBM((own, width), F32),
            pltpu.HBM((experts, own), F32),
            pltpu.HBM((2, own), F32),
            pltpu.HBM((5, own), F32),
        ],
        *summed,
        scratch=[pltpu.VMEM((128, 128), F32), pltpu.VMEM((n_dp, own, cols + width), BF)],
    )
    grad_tokens = call(tokens_end_kernel, [pltpu.HBM((rows, width), F32)], d_own, *far(x), vectors, *far(d_mixed))[0]
    return (
        outputs[None],
        grad_tokens[None],
        owned_qkv,
        owned_proj,
        owned_router.T,
        owned_gains,
        owned_biases,
        grad_up[None],
        grad_up_bias,
        grad_down[None],
        grad_down_bias,
    )


def solution(mesh):
    line = P(("dp", "expert"), None)
    across = P(None, ("dp", "expert"))
    act = P("expert", "dp", None)
    return jax.shard_map(
        shards,
        mesh=mesh,
        in_specs=(
            act,
            line,
            line,
            line,
            across,
            across,
            P("expert", None, "dp"),
            P("expert", "dp"),
            act,
            P("expert", "dp"),
            act,
            act,
            P("expert", None),
            P("expert", None),
            act,
        ),
        out_specs=(
            act,
            act,
            line,
            line,
            line,
            across,
            across,
            P("expert", None, "dp"),
            P("expert", "dp"),
            act,
            P("expert", "dp"),
        ),
        check_vma=False,
    )
```
